32 devices in a mesh: group: 4 (over y, x), dp: 2 (over core), tensor: 4 (over z).
Axes of the slice: x: 2, y: 2, z: 4, core: 2. Of those that a mesh axis runs over, the one named last changes fastest.
Arguments:
- features: bfloat16 [12288, 1024], P(('group', 'dp', 'tensor')), may hold values from -6 to 6
- cotangent: bfloat16 [12288, 1024], P(('group', 'dp', 'tensor')), may hold values from -6 to 6
- frame_counts: int32 [8, 3], P(('group', 'dp')), may hold values from 1 to 768, 1536 in all within a row
- buckets: int32 [8, 3], P(('group', 'dp')), may hold values from 0 to 7
- step_count: int32 [1], replicated, may hold values from 2 to 20
- col_weights: float32 [1024, 5, 1024], P('dp', None, 'tensor'), may hold values from -0.1875 to 0.1875
- mod_weights: float32 [1024, 6, 1024], P('dp', None, 'tensor'), may hold values from -0.375 to 0.375
- row_weights: float32 [3, 1024, 1024], P(None, 'dp', 'tensor'), may hold values from -0.25 to 0.25
- col_first: float32 [4, 1024, 5, 1024], P('group', 'dp', None, 'tensor'), may hold values from -32 to 32
- col_second: float32 [4, 1024, 5, 1024], P('group', 'dp', None, 'tensor'), may hold values from 1.536 to 6.144
- mod_first: float32 [4, 1024, 6, 1024], P('group', 'dp', None, 'tensor'), may hold values from -32 to 32
- mod_second: float32 [4, 1024, 6, 1024], P('group', 'dp', None, 'tensor'), may hold values from 1.536 to 6.144
- row_first: float32 [4, 3, 1024, 1024], P('group', None, 'dp', 'tensor'), may hold values from -32 to 32
- row_second: float32 [4, 3, 1024, 1024], P('group', None, 'dp', 'tensor'), may hold values from 1.536 to 6.144
- col_outer: float32 [1024, 5, 1024], P('dp', None, 'tensor'), may hold values from -1.5 to 1.5
- mod_outer: float32 [1024, 6, 1024], P('dp', None, 'tensor'), may hold values from -1.5 to 1.5
- row_outer: float32 [3, 1024, 1024], P(None, 'dp', 'tensor'), may hold values from -1.5 to 1.5
Outputs:
- output: bfloat16 [12288, 1024], P(('group', 'dp', 'tensor'))
- input_grad: float32 [12288, 1024], P(('group', 'dp', 'tensor'))
- col_first_new: float32 [4, 1024, 5, 1024], P('group', 'dp', None, 'tensor')
- col_second_new: float32 [4, 1024, 5, 1024], P('group', 'dp', None, 'tensor')
- col_average: float32 [1024, 5, 1024], P('dp', None, 'tensor')
- col_outer_new: float32 [1024, 5, 1024], P('dp', None, 'tensor')
- col_new: float32 [1024, 5, 1024], P('dp', None, 'tensor')
- mod_first_new: float32 [4, 1024, 6, 1024], P('group', 'dp', None, 'tensor')
- mod_second_new: float32 [4, 1024, 6, 1024], P('group', 'dp', None, 'tensor')
- mod_average: float32 [1024, 6, 1024], P('dp', None, 'tensor')
- mod_outer_new: float32 [1024, 6, 1024], P('dp', None, 'tensor')
- mod_new: float32 [1024, 6, 1024], P('dp', None, 'tensor')
- row_first_new: float32 [4, 3, 1024, 1024], P('group', None, 'dp', 'tensor')
- row_second_new: float32 [4, 3, 1024, 1024], P('group', None, 'dp', 'tensor')
- row_average: float32 [3, 1024, 1024], P(None, 'dp', 'tensor')
- row_outer_new: float32 [3, 1024, 1024], P(None, 'dp', 'tensor')
- row_new: float32 [3, 1024, 1024], P(None, 'dp', 'tensor')
The draws below stay inside these ranges and needn't reach their ends.
Inputs may be any that keep to these rules, and one draw needn't show every extreme that they name: frame_counts[b] lists the frames of the 3 utterances of pack b; they sum to 1536 and the longest has exactly 768.
All inputs are finite; a program needn't handle non-finite values.
Results may differ from the reference program's by a relative error of at most 0.01695.
The reference program's roundings to bfloat16 on the way count: a program that leaves them out, or rounds other values in their place, can miss the bound.
Values may be sent and summed in bfloat16 or wider, within the bound.
No kernel may reach another device: no remote copies, remote signals or barrier semaphores. Data moves between devices by JAX's collectives and lax.ppermute only.
A program may use at most 256 MiB of HBM per device.

```python
import math
import jax
import jax.numpy as jnp
import numpy as np
from jax import lax

D = 1024
HEADS = 16
HEAD_DIM = 64
FR_DEV = 1536
UTT_DEV = 3
NBUCK = 8
GROUPS = 4
PACKS = 8
LONGEST = 768
TOKENS_G = 3072
TOKENS = 12288
N_GROUP = 4
N_DP = 2


def plant(drawn, rng, smallest, largest):
    index_at = [jax.random.randint(jax.random.fold_in(rng, axis), (), 0, length) for axis, length in enumerate(drawn.shape)]
    main_axis = drawn.shape.index(max(drawn.shape))
    next_to = index_at[:main_axis] + [(index_at[main_axis] + 1) % drawn.shape[main_axis]] + index_at[main_axis + 1:]
    return drawn.at[tuple(index_at)].set(smallest).at[tuple(next_to)].set(largest)


def levels(stream_key, shape, split, low, high):
    factor_of = 1.0
    for dim, parts in split:
        draws = jax.random.uniform(jax.random.fold_in(jax.random.fold_in(stream_key, 6), dim), (parts,), jnp.float32, low / len(split), high / len(split))
        factor_of = factor_of * jnp.repeat(jnp.exp(draws), shape[dim] // parts).reshape((-1,) + (1,) * (len(shape) - 1 - dim))
    return factor_of


def split_up(amount, total, bound, slope):
    portions = [(1 << 20) // math.isqrt(rank ** slope) + 1 for rank in range(2, amount + 1)]
    spare, holding = total - bound - (amount - 1), [1] * (amount - 1)
    while spare > 0:
        candidates = [i for i in range(amount - 1) if holding[i] < bound]
        whole, left = sum([portions[i] for i in candidates]), spare
        for i in candidates:
            extra = min(bound - holding[i], max(1, left * portions[i] // whole), spare)
            holding[i] = holding[i] + extra
            spare = spare - extra
    return np.array([bound] + holding)


def ragged_sizes(stream_key, amount, total, most, lean):
    if amount == 2:
        one = jax.random.randint(stream_key, (), max(1, total - most), min(most, total - 1) + 1)
        return jnp.stack([one, total - one])
    sizes = jnp.asarray(split_up(amount, total, most, lean), jnp.int32)
    pairs = (amount - 1) // 2
    giver, taker = sizes[1:1 + 2 * pairs:2], sizes[2:2 + 2 * pairs:2]
    slack = jnp.minimum(giver - 1, most - taker)
    moved = jax.random.randint(jax.random.fold_in(stream_key, 1), (pairs,), 0, 1 << 20) % (slack + 1)
    sizes = sizes.at[1:1 + 2 * pairs:2].set(giver - moved).at[2:2 + 2 * pairs:2].set(taker + moved)
    return sizes[jax.random.permutation(jax.random.fold_in(stream_key, 2), amount)]


def scatter_about(stream_key, shape, spread, limit, split=(), kind=jnp.bfloat16):
    values = jax.random.normal(stream_key, shape, jnp.float32) * spread
    if len(split) > 0:
        values = levels(stream_key, shape, split, -0.22, 0.18) * values
    return jnp.clip(values, min=-limit, max=limit).astype(kind)


def setup_inputs(seed: int = 0) -> dict:
    streams_of = jax.random.split(jax.random.key(seed), 18)
    features = scatter_about(streams_of[0], (TOKENS, D), 1.0, 6.0, ((0, 32),))
    cotangent = scatter_about(streams_of[1], (TOKENS, D), 1.0, 6.0, ((0, 32),))
    frame_counts = jax.vmap(lambda own: ragged_sizes(own, UTT_DEV, FR_DEV, LONGEST, 1))(jax.random.split(streams_of[2], PACKS)).reshape((PACKS, UTT_DEV)).astype(jnp.int32)
    buckets = plant(jax.random.randint(streams_of[3], (PACKS, UTT_DEV), 0, NBUCK), jax.random.fold_in(streams_of[3], 1), 0, NBUCK - 1).astype(jnp.int32)
    step_count = jax.random.randint(streams_of[4], (1,), 2, 21).astype(jnp.int32)
    col_weights = scatter_about(streams_of[5], (D, 5, D), D ** -0.5, 0.1875, ((0, 2), (2, 4)), jnp.float32)
    mod_weights = scatter_about(streams_of[6], (D, 6, D), (D // 4) ** -0.5, 0.375, ((0, 2), (2, 4)), jnp.float32)
    row_weights = scatter_about(streams_of[7], (3, D, D), (D // 2) ** -0.5, 0.25, ((1, 2), (2, 4)), jnp.float32)
    col_first = scatter_about(streams_of[8], (GROUPS, D, 5, D), (0.1 * TOKENS_G ** 0.5), 32.0, ((0, 4), (1, 2), (3, 4)), jnp.float32)
    col_second = jnp.clip(jnp.exp(math.log(6.144) - 1.3862944 * jax.random.uniform(streams_of[9], (GROUPS, D, 5, D), jnp.float32) ** levels(streams_of[9], (GROUPS, D, 5, D), ((0, 4), (1, 2), (3, 4)), -0.2, 0.2)), 1.536, 6.144)
    mod_first = scatter_about(streams_of[10], (GROUPS, D, 6, D), (0.1 * TOKENS_G ** 0.5), 32.0, ((0, 4), (1, 2), (3, 4)), jnp.float32)
    mod_second = jnp.clip(jnp.exp(math.log(6.144) - 1.3862944 * jax.random.uniform(streams_of[11], (GROUPS, D, 6, D), jnp.float32) ** levels(streams_of[11], (GROUPS, D, 6, D), ((0, 4), (1, 2), (3, 4)), -0.2, 0.2)), 1.536, 6.144)
    row_first = scatter_about(streams_of[12], (GROUPS, 3, D, D), (0.1 * TOKENS_G ** 0.5), 32.0, ((0, 4), (2, 2), (3, 4)), jnp.float32)
    row_second = jnp.clip(jnp.exp(math.log(6.144) - 1.3862944 * jax.random.uniform(streams_of[13], (GROUPS, 3, D, D), jnp.float32) ** levels(streams_of[13], (GROUPS, 3, D, D), ((0, 4), (2, 2), (3, 4)), -0.2, 0.2)), 1.536, 6.144)
    col_outer = scatter_about(streams_of[14], (D, 5, D), 0.1, 1.5, ((0, 2), (2, 4)), jnp.float32)
    mod_outer = scatter_about(streams_of[15], (D, 6, D), 0.1, 1.5, ((0, 2), (2, 4)), jnp.float32)
    row_outer = scatter_about(streams_of[16], (3, D, D), 0.1, 1.5, ((1, 2), (2, 4)), jnp.float32)
    return {"features": features, "cotangent": cotangent, "frame_counts": frame_counts, "buckets": buckets, "step_count": step_count, "col_weights": col_weights, "mod_weights": mod_weights, "row_weights": row_weights, "col_first": col_first, "col_second": col_second, "mod_first": mod_first, "mod_second": mod_second, "row_first": row_first, "row_second": row_second, "col_outer": col_outer, "mod_outer": mod_outer, "row_outer": row_outer}


@jax.custom_vjp
def low(v):
    return lax.optimization_barrier(v.astype(jnp.bfloat16)).astype(jnp.float32)

@jax.custom_vjp
def low_back(v):
    return v

def low_keep(v):
    return (low(v), None)

def low_pass(kept, grad):
    return (grad,)

def back_keep(v):
    return (v, None)

def back_low(kept, grad):
    return (low(grad),)
low.defvjp(low_keep, low_pass)
low_back.defvjp(back_keep, back_low)
highest = lax.Precision.HIGHEST
norm_epsilon = 1e-06
adam_epsilon = 1e-08
beta_first = 0.9
beta_second = 0.999
inner_rate = 0.05
weight_decay = 0.01
outer_rate = 0.7
outer_beta = 0.9

def time_embedding(flow_time, width_all):
    half_width = width_all // 2
    frequency = jnp.exp(jnp.arange(half_width, dtype=jnp.float32) * (-math.log(10000.0) / (half_width - 1)))
    angles = 1000.0 * flow_time[:, None] * frequency[None, :]
    return jnp.concatenate([jnp.sin(angles), jnp.cos(angles)], axis=1)

def pack_geometry(lengths, frames):
    ending = jnp.cumsum(lengths).astype(jnp.int32)
    starting = (ending - lengths).astype(jnp.int32)
    indices = jnp.arange(frames, dtype=jnp.int32)
    member = (indices[:, None] >= starting[None, :]) & (indices[:, None] < ending[None, :])
    onehot = member.astype(jnp.float32)
    offsets = lax.optimization_barrier(jnp.sum(jnp.where(member, starting[None, :], 0), axis=1)).astype(jnp.int32)
    position = (indices - offsets).astype(jnp.float32)
    numbers = jnp.arange(lengths.shape[0], dtype=jnp.int32)
    segment = lax.optimization_barrier(jnp.sum(jnp.where(member, numbers[None, :], 0), axis=1)).astype(jnp.int32)
    same_segment = segment[:, None] == segment[None, :]
    return (onehot, position, same_segment)

def rotary_tables(position, head_width):
    half_width = head_width // 2
    frequency = jnp.exp(jnp.arange(half_width, dtype=jnp.float32) * (-2.0 * math.log(10000.0) / head_width))
    angles = position[:, None] * frequency[None, :]
    return (jnp.cos(angles)[:, None, :], jnp.sin(angles)[:, None, :])

def rotate(values, cosine, sine_part):
    half_width = values.shape[-1] // 2
    leading, trailing = (values[..., :half_width], values[..., half_width:])
    return jnp.concatenate([leading * cosine - trailing * sine_part, trailing * cosine + leading * sine_part], axis=-1)

def normalize(values):
    centered = values - lax.optimization_barrier(jnp.mean(values, axis=-1, keepdims=True))
    inverse_scale = lax.rsqrt(lax.optimization_barrier(jnp.mean(centered * centered, axis=-1, keepdims=True)) + norm_epsilon)
    return centered * inverse_scale

def attention(queries, key_rows, value_rows, same_segment):
    frames = queries.shape[0]
    block_rows = min(512, frames)
    score_scale = 1.0 / math.sqrt(HEAD_DIM)
    query_blocks = queries.reshape(frames // block_rows, block_rows, HEADS, HEAD_DIM)
    mask_blocks = same_segment.reshape(frames // block_rows, block_rows, frames)

    def block_output(block_pair):
        query_block, mask_block = block_pair
        scores = low_back(jnp.einsum('qhd,khd->hqk', query_block, key_rows, precision=highest) * score_scale)
        scores = jnp.where(mask_block[None], scores, -1e+30)
        weights = low(jax.nn.softmax(scores, axis=-1))
        return jnp.einsum('hqk,khd->qhd', weights, value_rows, precision=highest)
    mixed_rows = lax.map(jax.checkpoint(block_output), (query_blocks, mask_blocks))
    return mixed_rows.reshape(frames, HEADS * HEAD_DIM)

def layer_forward(features_in, col_in, mod_in, row_in, condition, onehot, same_segment, cosine, sine_part):
    frames = features_in.shape[0]
    modulation = jnp.einsum('ud,dcj->ucj', low(condition), low(mod_in), precision=highest)
    per_row = jnp.einsum('fu,ucj->fcj', onehot, modulation, precision=highest)
    normed = normalize(features_in)
    att_in = low(normed * (1.0 + per_row[:, 1]) + per_row[:, 0])
    projected = low_back(jnp.einsum('fd,dcj->fcj', att_in, low(col_in[:, 0:3]), precision=highest))
    head_rows = projected.reshape(frames, 3, HEADS, HEAD_DIM)
    queries = low(rotate(head_rows[:, 0], cosine, sine_part))
    key_rows = low(rotate(head_rows[:, 1], cosine, sine_part))
    value_rows = low(head_rows[:, 2])
    mixed_rows = low(low_back(attention(queries, key_rows, value_rows, same_segment)))
    attn_out = low_back(jnp.einsum('fj,dj->fd', mixed_rows, low(row_in[0]), precision=highest))
    residual = features_in + per_row[:, 2] * attn_out
    normed_two = normalize(residual)
    ffn_in = low(normed_two * (1.0 + per_row[:, 4]) + per_row[:, 3])
    upward = low_back(jnp.einsum('fd,dcj->fcj', ffn_in, low(col_in[:, 3:5]), precision=highest))
    hidden = low(jax.nn.gelu(upward, approximate=True))
    ffn_out = low_back(jnp.einsum('fcj,cdj->fd', hidden, low(row_in[1:3]), precision=highest))
    return residual + per_row[:, 5] * ffn_out

def adam_update(grads, first, second, weights, outer, steps_done):
    first_new = beta_first * first + (1.0 - beta_first) * grads
    second_new = beta_second * second + (1.0 - beta_second) * grads * grads
    correct_one = 1.0 - beta_first ** steps_done
    correct_two = 1.0 - beta_second ** steps_done
    difference = inner_rate * (first_new / correct_one / (jnp.sqrt(second_new / correct_two) + adam_epsilon) + weight_decay * weights)
    average = lax.optimization_barrier(jnp.sum(difference, axis=0)) / N_GROUP
    outer_new = outer_beta * outer + average
    weights_new = weights - outer_rate * (average + outer_beta * outer_new)
    return (first_new, second_new, average, outer_new, weights_new)

def reference(features, cotangent, frame_counts, buckets, step_count, col_weights, mod_weights, row_weights, col_first, col_second, mod_first, mod_second, row_first, row_second, col_outer, mod_outer, row_outer):
    features_all = features.astype(jnp.float32).reshape(N_GROUP, N_DP, FR_DEV, D)
    cotangent_all = cotangent.astype(jnp.float32).reshape(N_GROUP, N_DP, FR_DEV, D)
    lengths_all = frame_counts.reshape(N_GROUP, N_DP, UTT_DEV)
    buckets_all = buckets.reshape(N_GROUP, N_DP, UTT_DEV)

    def group_pass(group_items):
        group_index, features_g, cotangent_g, lengths_g, buckets_g = group_items

        def pack_pass(carry, pack_items):
            features_p, cotangent_p, lengths_p, buckets_p = pack_items
            onehot, position, same_segment = pack_geometry(lengths_p, FR_DEV)
            cosine, sine_part = rotary_tables(position, HEAD_DIM)
            flow_time = ((group_index * NBUCK + buckets_p).astype(jnp.float32) + 0.5) / (NBUCK * N_GROUP)
            condition = jax.nn.silu(time_embedding(flow_time, D))

            def forward(features_in, col_in, mod_in, row_in):
                return layer_forward(features_in, col_in, mod_in, row_in, condition, onehot, same_segment, cosine, sine_part)
            result, pullback = jax.vjp(forward, features_p, col_weights, mod_weights, row_weights)
            grad_features, grad_col, grad_mod, grad_row = pullback(cotangent_p)
            carry = (carry[0] + grad_col, carry[1] + grad_mod, carry[2] + grad_row)
            return (carry, (result.astype(jnp.bfloat16), grad_features))
        zeros = (jnp.zeros_like(col_weights), jnp.zeros_like(mod_weights), jnp.zeros_like(row_weights))
        grads, outputs = lax.scan(pack_pass, zeros, (features_g, cotangent_g, lengths_g, buckets_g))
        return (grads, outputs)
    grads, outputs = lax.map(group_pass, (jnp.arange(N_GROUP, dtype=jnp.int32), features_all, cotangent_all, lengths_all, buckets_all))
    col_grad, mod_grad, row_grad = grads
    results, grad_features = outputs
    steps_done = step_count[0].astype(jnp.float32)
    col_a, col_b, col_c, col_d, col_e = adam_update(col_grad, col_first, col_second, col_weights, col_outer, steps_done)
    mod_a, mod_b, mod_c, mod_d, mod_e = adam_update(mod_grad, mod_first, mod_second, mod_weights, mod_outer, steps_done)
    row_a, row_b, row_c, row_d, row_e = adam_update(row_grad, row_first, row_second, row_weights, row_outer, steps_done)
    return (results.reshape(TOKENS, D), grad_features.reshape(TOKENS, D), col_a, col_b, col_c, col_d, col_e, mod_a, mod_b, mod_c, mod_d, mod_e, row_a, row_b, row_c, row_d, row_e)
```

```python
from functools import partial
import math

import jax
import jax.numpy as jnp
from jax import lax
from jax.sharding import PartitionSpec as P

HEAD_DIM = 64
NBUCK = 8


highest = lax.Precision.HIGHEST
norm_epsilon = 1e-06
adam_epsilon = 1e-08
beta_first = 0.9
beta_second = 0.999
inner_rate = 0.05
weight_decay = 0.01
outer_rate = 0.7
outer_beta = 0.9


def time_embedding(flow_time, width_all):
    half_width = width_all // 2
    frequency = jnp.exp(
        jnp.arange(half_width, dtype=jnp.float32) * (-math.log(10000.0) / (half_width - 1))
    )
    angles = 1000.0 * flow_time[:, None] * frequency[None, :]
    return jnp.concatenate([jnp.sin(angles), jnp.cos(angles)], axis=1)


def pack_geometry(lengths, frames):
    ending = jnp.cumsum(lengths)
    starting = ending - lengths
    indices = jnp.arange(frames, dtype=jnp.int32)
    member = (indices[:, None] >= starting[None, :]) & (indices[:, None] < ending[None, :])
    onehot = member.astype(jnp.float32)
    offsets = jnp.sum(jnp.where(member, starting[None, :], 0), axis=1)
    position = (indices - offsets).astype(jnp.float32)
    numbers = jnp.arange(lengths.shape[0], dtype=jnp.int32)
    segment = jnp.sum(jnp.where(member, numbers[None, :], 0), axis=1)
    same_segment = segment[:, None] == segment[None, :]
    return (onehot, position, same_segment)


def rotary_tables(position, head_width):
    half_width = head_width // 2
    frequency = jnp.exp(
        jnp.arange(half_width, dtype=jnp.float32) * (-2.0 * math.log(10000.0) / head_width)
    )
    angles = position[:, None] * frequency[None, :]
    return (jnp.cos(angles)[:, None, :], jnp.sin(angles)[:, None, :])


def rotate(values, cosine, sine_part):
    half_width = values.shape[-1] // 2
    leading, trailing = (values[..., :half_width], values[..., half_width:])
    return jnp.concatenate(
        [leading * cosine - trailing * sine_part, trailing * cosine + leading * sine_part], axis=-1
    )


def rotate_back(grads, cosine, sine_part):
    half_width = grads.shape[-1] // 2
    leading, trailing = (grads[..., :half_width], grads[..., half_width:])
    return jnp.concatenate(
        [leading * cosine + trailing * sine_part, trailing * cosine - leading * sine_part], axis=-1
    )


def normalize(values):
    centered = values - jnp.mean(values, axis=-1, keepdims=True)
    inverse_scale = lax.rsqrt(jnp.mean(centered * centered, axis=-1, keepdims=True) + norm_epsilon)
    return (centered * inverse_scale, inverse_scale)


def normalize_back(grads, normed, inverse_scale):
    return inverse_scale * (
        grads
        - jnp.mean(grads, axis=-1, keepdims=True)
        - normed * jnp.mean(grads * normed, axis=-1, keepdims=True)
    )


def attend(queries, key_rows, value_rows, same_segment):
    frames = queries.shape[0]
    block_rows = min(512, frames)
    score_scale = 1.0 / math.sqrt(queries.shape[-1])

    def block_output(begin_row):
        query_block = lax.dynamic_slice_in_dim(queries, begin_row, block_rows, 0)
        mask_block = lax.dynamic_slice_in_dim(same_segment, begin_row, block_rows, 0)
        scores = (
            jnp.einsum("qhd,khd->hqk", query_block, key_rows, preferred_element_type=jnp.float32)
            * score_scale
        )
        scores = jnp.where(mask_block[None], scores, -1e30)
        largest = jnp.max(scores, axis=-1, keepdims=True)
        exponent = jnp.exp(scores - largest)
        totals = jnp.sum(exponent, axis=-1, keepdims=True)
        weights = (exponent / totals).astype(jnp.bfloat16)
        mixed_block = jnp.einsum(
            "hqk,khd->qhd", weights, value_rows, preferred_element_type=jnp.float32
        )
        return (mixed_block.astype(jnp.bfloat16), (largest + jnp.log(totals))[..., 0])

    begins = jnp.arange(frames // block_rows, dtype=jnp.int32) * block_rows
    mixed_blocks, log_totals = lax.map(block_output, begins)
    return (mixed_blocks.reshape(frames, -1), log_totals)


def attend_back(queries, key_rows, value_rows, same_segment, log_totals, grad_mixed):
    frames, heads_here, head_width = queries.shape
    block_rows = min(512, frames)
    score_scale = 1.0 / math.sqrt(head_width)
    grad_heads = grad_mixed.reshape(frames, heads_here, head_width)

    def block_grads(carry, items):
        key_sum, value_sum = carry
        begin_row, log_block = items
        query_block = lax.dynamic_slice_in_dim(queries, begin_row, block_rows, 0)
        mask_block = lax.dynamic_slice_in_dim(same_segment, begin_row, block_rows, 0)
        grad_block = lax.dynamic_slice_in_dim(grad_heads, begin_row, block_rows, 0)
        scores = (
            jnp.einsum("qhd,khd->hqk", query_block, key_rows, preferred_element_type=jnp.float32)
            * score_scale
        )
        scores = jnp.where(mask_block[None], scores, -1e30)
        probs = jnp.exp(scores - log_block[..., None])
        grad_probs = jnp.einsum(
            "qhd,khd->hqk", grad_block, value_rows, preferred_element_type=jnp.float32
        )
        grad_scores = (
            probs * (grad_probs - jnp.sum(probs * grad_probs, axis=-1, keepdims=True))
        ).astype(jnp.bfloat16)
        grad_query = (
            jnp.einsum("hqk,khd->qhd", grad_scores, key_rows, preferred_element_type=jnp.float32)
            * score_scale
        )
        key_sum = (
            key_sum
            + jnp.einsum(
                "hqk,qhd->khd", grad_scores, query_block, preferred_element_type=jnp.float32
            )
            * score_scale
        )
        value_sum = value_sum + jnp.einsum(
            "hqk,qhd->khd",
            probs.astype(jnp.bfloat16),
            grad_block,
            preferred_element_type=jnp.float32,
        )
        return ((key_sum, value_sum), grad_query)

    zeros = jnp.zeros((frames, heads_here, head_width), jnp.float32)
    begins = jnp.arange(frames // block_rows, dtype=jnp.int32) * block_rows
    sums, grad_queries = lax.scan(block_grads, (zeros, zeros), (begins, log_totals))
    return (grad_queries.reshape(frames, heads_here, head_width), sums[0], sums[1])


def inner_step(grads, first, second, weights, steps_done):
    first_new = beta_first * first + (1.0 - beta_first) * grads
    second_new = beta_second * second + (1.0 - beta_second) * grads * grads
    correct_one = 1.0 - beta_first**steps_done
    correct_two = 1.0 - beta_second**steps_done
    difference = inner_rate * (
        first_new / correct_one / (jnp.sqrt(second_new / correct_two) + adam_epsilon)
        + weight_decay * weights
    )
    return (first_new[None], second_new[None], difference)


def outer_step(average, outer, weights):
    outer_new = outer_beta * outer + average
    return (outer_new, weights - outer_rate * (average + outer_beta * outer_new))


def shifted(values, axis, step):
    size = lax.axis_size(axis)
    return lax.ppermute(values, axis, [(i, (i + step) % size) for i in range(size)])


def ring_gather(own):
    half = own.shape[-2] // 2
    third = shifted(own, "tensor", 1)
    first = shifted(own, "tensor", -1)
    low = shifted(third[..., :half, :], "tensor", 1)
    high = shifted(first[..., half:, :], "tensor", -1)
    return [own, first, jnp.concatenate([low, high], axis=-2), third]


def ring_scatter(blocks):
    half = blocks[0].shape[-2] // 2
    low_bits = jnp.bfloat16
    low = shifted(blocks[2][..., :half, :].astype(low_bits), "tensor", 1)
    high = shifted(blocks[2][..., half:, :].astype(low_bits), "tensor", -1)
    rightward = jnp.concatenate(
        [blocks[1][..., :half, :] + low.astype(jnp.float32), blocks[1][..., half:, :].astype(jnp.float32)], axis=-2
    ).astype(low_bits)
    leftward = jnp.concatenate(
        [blocks[3][..., :half, :].astype(jnp.float32), blocks[3][..., half:, :] + high.astype(jnp.float32)], axis=-2
    ).astype(low_bits)
    return (
        blocks[0].astype(jnp.float32)
        + shifted(rightward, "tensor", 1).astype(jnp.float32)
        + shifted(leftward, "tensor", -1).astype(jnp.float32)
    )


def exchange(blocks):
    got = [blocks[0]]
    for r in range(1, 4):
        got.append(shifted(blocks[4 - r], "tensor", 4 - r))
    return got


def in_order(pieces, axis):
    me = lax.axis_index("tensor")
    width = pieces[0].shape[axis]
    shape = list(pieces[0].shape)
    shape[axis] = 4 * width
    out = jnp.zeros(shape, pieces[0].dtype)
    for r in range(4):
        out = lax.dynamic_update_slice_in_dim(out, pieces[r], (me + r) % 4 * width, axis)
    return out


def dp_gather(own, axis):
    if lax.axis_size("dp") != 2:
        return lax.all_gather(own, "dp", axis=axis, tiled=True)
    other = shifted(own, "dp", 1)
    first = lax.axis_index("dp") == 0
    return jnp.concatenate([jnp.where(first, own, other), jnp.where(first, other, own)], axis=axis)


def dp_share(product, whole):
    parts = lax.axis_size("dp")
    width = whole.shape[1] // parts
    me = lax.axis_index("dp")
    if parts != 2:
        return lax.psum_scatter(
            product(whole), "dp", scatter_dimension=product.split, tiled=True
        )
    away = product(lax.dynamic_slice_in_dim(whole, (1 - me) * width, width, 1)).astype(jnp.bfloat16)
    here = product(lax.dynamic_slice_in_dim(whole, me * width, width, 1))
    return here + shifted(away, "dp", 1).astype(jnp.float32)


class Product:
    def __init__(self, form, other, split):
        self.form, self.other, self.split = form, other, split

    def __call__(self, whole):
        return jnp.einsum(self.form, whole, self.other, preferred_element_type=jnp.float32)


def pick(onehot, rows):
    out = onehot[:, 0:1] * rows[0]
    for u in range(1, rows.shape[0]):
        out = out + onehot[:, u : u + 1] * rows[u]
    return out


def per_device(
    features,
    cotangent,
    frame_counts,
    buckets,
    step_count,
    col_weights,
    mod_weights,
    row_weights,
    col_first,
    col_second,
    mod_first,
    mod_second,
    row_first,
    row_second,
    col_outer,
    mod_outer,
    row_outer,
):
    group_count = lax.axis_size("group")
    packs_here = lax.axis_size("dp")
    own_rows, model_width = features.shape
    frames = own_rows * 4
    me = lax.axis_index("tensor")
    core = lax.axis_index("dp")
    first_row = me * own_rows
    low = jnp.bfloat16
    utterances = buckets.shape[1]
    share = mod_weights.shape[0]

    feature_pieces = ring_gather(features)
    col_low = col_weights.astype(low)
    qkv_low = dp_gather(col_low[:, 0:3], 0)
    wide_low = jnp.concatenate([row_weights.astype(low), jnp.moveaxis(col_low[:, 3:5], 1, 0)], axis=0)

    buckets_all = lax.all_gather(buckets[0], "dp", axis=0, tiled=True) if packs_here != 2 else None
    if buckets_all is None:
        away = shifted(buckets[0], "dp", 1)
        buckets_all = jnp.where(core == 0, jnp.concatenate([buckets[0], away]), jnp.concatenate([away, buckets[0]]))
    flow_time = ((lax.axis_index("group") * NBUCK + buckets_all).astype(jnp.float32) + 0.5) / (
        NBUCK * group_count
    )
    condition_all = jax.nn.silu(time_embedding(flow_time, model_width)).astype(low)
    condition_here = lax.dynamic_slice_in_dim(condition_all, core * share, share, 1)
    mod_terms = jnp.einsum("ud,dcj->ucj", condition_here, mod_weights.astype(low), preferred_element_type=jnp.float32)
    if packs_here != 2:
        mod_part = lax.psum_scatter(mod_terms, "dp", scatter_dimension=0, tiled=True)
    else:
        mod_away = lax.dynamic_slice_in_dim(mod_terms, (1 - core) * utterances, utterances, 0)
        mod_part = lax.dynamic_slice_in_dim(mod_terms, core * utterances, utterances, 0) + shifted(mod_away, "dp", 1)
    modulation = in_order([mod_part] + [shifted(mod_part, "tensor", -r) for r in range(1, 4)], 2)

    onehot_all, position, same_segment = pack_geometry(frame_counts[0], frames)
    onehot_own = lax.dynamic_slice_in_dim(onehot_all, first_row, own_rows, 0)
    cosine, sine_part = rotary_tables(position, HEAD_DIM)
    features_full = in_order(feature_pieces, 0)
    normed_full, _ = normalize(features_full.astype(jnp.float32))
    att_full = (
        normed_full * (1.0 + pick(onehot_all, modulation[:, 1])) + pick(onehot_all, modulation[:, 0])
    ).astype(low)
    projected = jnp.einsum("fd,dcj->fcj", att_full, qkv_low, preferred_element_type=jnp.float32)
    head_rows = projected.reshape(frames, 3, -1, HEAD_DIM)
    queries = rotate(head_rows[:, 0], cosine, sine_part).astype(low)
    key_rows = rotate(head_rows[:, 1], cosine, sine_part).astype(low)
    value_rows = head_rows[:, 2].astype(low)
    mixed_rows, log_totals = attend(queries, key_rows, value_rows, same_segment)

    wide_pieces = ring_gather(wide_low)
    wide_full = dp_gather(jnp.concatenate(wide_pieces, axis=2), 1)
    out_low, down_low, up_low = (wide_full[0], wide_full[1:3], wide_full[3:5])

    def rows_of(values, r):
        return lax.dynamic_slice_in_dim(values, (me + r) % 4 * own_rows, own_rows, 0)

    mixed_own = jnp.concatenate(exchange([rows_of(mixed_rows, r) for r in range(4)]), axis=1)
    per_row = [pick(onehot_own, modulation[:, c]) for c in range(6)]
    features_in = features.astype(jnp.float32)
    grad_output = cotangent.astype(jnp.float32)
    normed, inverse_scale = normalize(features_in)
    grad_ffn = (grad_output * per_row[5]).astype(low)
    attn_out = jnp.einsum("fj,dj->fd", mixed_own, out_low, preferred_element_type=jnp.float32)
    residual = features_in + per_row[2] * attn_out
    normed_two, inverse_two = normalize(residual)
    ffn_in = (normed_two * (1.0 + per_row[4]) + per_row[3]).astype(low)
    upward = jnp.einsum("fd,cdj->fcj", ffn_in, up_low, preferred_element_type=jnp.float32)
    hidden = jax.nn.gelu(upward, approximate=True).astype(low)
    ffn_out = jnp.einsum("fcj,cdj->fd", hidden, down_low, preferred_element_type=jnp.float32)
    output = (residual + per_row[5] * ffn_out).astype(low)
    grad_hidden = jnp.einsum("fd,cdj->fcj", grad_ffn, down_low, preferred_element_type=jnp.float32)
    gelu_pull = jax.vjp(partial(jax.nn.gelu, approximate=True), upward)[1]
    grad_upward = gelu_pull(grad_hidden)[0].astype(low)
    grad_ffn_in = jnp.einsum("fcj,cdj->fd", grad_upward, up_low, preferred_element_type=jnp.float32)
    grad_residual = grad_output + normalize_back(
        grad_ffn_in * (1.0 + per_row[4]), normed_two, inverse_two
    )
    grad_attn = (grad_residual * per_row[2]).astype(low)
    grad_mixed_own = jnp.einsum("fd,dj->fj", grad_attn, out_low, preferred_element_type=jnp.float32).astype(low)
    width = grad_mixed_own.shape[1] // 4
    grad_mixed = in_order(exchange([grad_mixed_own[:, r * width : (r + 1) * width] for r in range(4)]), 0)

    down_share = dp_share(Product("fd,fcj->cdj", hidden, 1), grad_ffn)
    up_share = dp_share(Product("fd,fcj->cdj", grad_upward, 1), ffn_in)
    out_share = dp_share(Product("fd,fj->dj", mixed_own, 0), grad_attn)
    wide_share = jnp.concatenate([out_share[None], down_share, up_share], axis=0)
    wide_grad = ring_scatter([wide_share[:, :, r * width : (r + 1) * width] for r in range(4)])
    row_share = wide_grad[0:3]

    grad_queries, grad_keys, grad_values = attend_back(
        queries, key_rows, value_rows, same_segment, log_totals, grad_mixed
    )
    grad_projected = (
        jnp.stack(
            [
                rotate_back(grad_queries, cosine, sine_part),
                rotate_back(grad_keys, cosine, sine_part),
                grad_values,
            ],
            axis=1,
        )
        .reshape(frames, 3, -1)
        .astype(low)
    )
    grad_att_full = jnp.einsum("fcj,dcj->fd", grad_projected, qkv_low, preferred_element_type=jnp.float32)
    grad_att_in = ring_scatter([rows_of(grad_att_full, r) for r in range(4)])
    qkv_share = dp_share(Product("fd,fcj->dcj", grad_projected, 0), att_full)
    col_share = jnp.concatenate([qkv_share, jnp.moveaxis(wide_grad[3:5], 0, 1)], axis=1)

    grad_features = grad_residual + normalize_back(
        grad_att_in * (1.0 + per_row[1]), normed, inverse_scale
    )
    mod_rows = jnp.stack(
        [
            grad_att_in,
            grad_att_in * normed,
            grad_residual * attn_out,
            grad_ffn_in,
            grad_ffn_in * normed_two,
            grad_output * ffn_out,
        ],
        axis=1,
    )
    mod_sums = jnp.einsum("fu,fcj->ucj", onehot_own, mod_rows, precision=highest)
    mod_mine = [lax.dynamic_slice_in_dim(mod_sums, (me + r) % 4 * width, width, 2) for r in range(4)]
    mod_columns = sum(exchange(mod_mine))
    if packs_here != 2:
        mod_columns_all = lax.all_gather(mod_columns, "dp", axis=0, tiled=True)
    else:
        columns_away = shifted(mod_columns, "dp", 1)
        mod_columns_all = jnp.where(
            core == 0,
            jnp.concatenate([mod_columns, columns_away]),
            jnp.concatenate([columns_away, mod_columns]),
        )
    mod_share = jnp.einsum(
        "ud,ucj->dcj", condition_here.astype(jnp.float32), mod_columns_all, precision=highest
    )

    steps_done = step_count[0].astype(jnp.float32)
    row_first_new, row_second_new, row_diff = inner_step(
        row_share, row_first[0], row_second[0], row_weights, steps_done
    )
    col_first_new, col_second_new, col_diff = inner_step(
        col_share, col_first[0], col_second[0], col_weights, steps_done
    )
    mod_first_new, mod_second_new, mod_diff = inner_step(
        mod_share, mod_first[0], mod_second[0], mod_weights, steps_done
    )
    row_average = lax.psum(row_diff.astype(low), "group").astype(jnp.float32) / group_count
    col_average = lax.psum(col_diff.astype(low), "group").astype(jnp.float32) / group_count
    mod_average = lax.psum(mod_diff.astype(low), "group").astype(jnp.float32) / group_count
    col_outer_new, col_new = outer_step(col_average, col_outer, col_weights)
    mod_outer_new, mod_new = outer_step(mod_average, mod_outer, mod_weights)
    row_outer_new, row_new = outer_step(row_average, row_outer, row_weights)
    return (
        output,
        grad_features,
        col_first_new,
        col_second_new,
        col_average,
        col_outer_new,
        col_new,
        mod_first_new,
        mod_second_new,
        mod_average,
        mod_outer_new,
        mod_new,
        row_first_new,
        row_second_new,
        row_average,
        row_outer_new,
        row_new,
    )


def solution(mesh):
    placed = (
        P(("group", "dp", "tensor"), None),
        P(("group", "dp", "tensor"), None),
        P(("group", "dp"), None),
        P(("group", "dp"), None),
        P(),
        P("dp", None, "tensor"),
        P("dp", None, "tensor"),
        P(None, "dp", "tensor"),
        P("group", "dp", None, "tensor"),
        P("group", "dp", None, "tensor"),
        P("group", "dp", None, "tensor"),
        P("group", "dp", None, "tensor"),
        P("group", None, "dp", "tensor"),
        P("group", None, "dp", "tensor"),
        P("dp", None, "tensor"),
        P("dp", None, "tensor"),
        P(None, "dp", "tensor"),
    )
    return jax.shard_map(
        per_device,
        mesh=mesh,
        in_specs=placed,
        out_specs=(
            P(("group", "dp", "tensor"), None),
            P(("group", "dp", "tensor"), None),
            P("group", "dp", None, "tensor"),
            P("group", "dp", None, "tensor"),
            P("dp", None, "tensor"),
            P("dp", None, "tensor"),
            P("dp", None, "tensor"),
            P("group", "dp", None, "tensor"),
            P("group", "dp", None, "tensor"),
            P("dp", None, "tensor"),
            P("dp", None, "tensor"),
            P("dp", None, "tensor"),
            P("group", None, "dp", "tensor"),
            P("group", None, "dp", "tensor"),
            P(None, "dp", "tensor"),
            P(None, "dp", "tensor"),
            P(None, "dp", "tensor"),
        ),
        check_vma=False,
    )
```

```python
from functools import partial
import math

import jax
import jax.numpy as jnp
from jax import lax
from jax.experimental import pallas as pl
from jax.experimental.pallas import tpu as pltpu
from jax.sharding import PartitionSpec as P

HEAD_DIM = 64
NBUCK = 8
BLOCK = 256
BOUNDS = 3

highest = lax.Precision.HIGHEST
norm_epsilon = 1e-06
adam_epsilon = 1e-08
beta_first = 0.9
beta_second = 0.999
inner_rate = 0.05
weight_decay = 0.01
outer_rate = 0.7
outer_beta = 0.9
low = jnp.bfloat16


def time_embedding(flow_time, width_all):
    half_width = width_all // 2
    frequency = jnp.exp(
        jnp.arange(half_width, dtype=jnp.float32) * (-math.log(10000.0) / (half_width - 1))
    )
    angles = 1000.0 * flow_time[:, None] * frequency[None, :]
    return jnp.concatenate([jnp.sin(angles), jnp.cos(angles)], axis=1)


def utterance_rows(ending, indices):
    number = jnp.zeros(indices.shape, jnp.int32)
    begin = jnp.zeros(indices.shape, jnp.int32)
    for u in range(ending.shape[0] - 1):
        after = indices >= ending[u]
        number = number + after.astype(jnp.int32)
        begin = jnp.where(after, ending[u], begin)
    return number, indices - begin


def rotary_tables(position):
    half_width = HEAD_DIM // 2
    frequency = jnp.exp(
        jnp.arange(half_width, dtype=jnp.float32) * (-2.0 * math.log(10000.0) / HEAD_DIM)
    )
    angles = position.astype(jnp.float32)[:, None] * frequency[None, :]
    cosine, sine = jnp.cos(angles), jnp.sin(angles)
    return jnp.concatenate([cosine] * 4, axis=1), jnp.concatenate([-sine, sine, -sine, sine], axis=1)


def normalize(values):
    centered = values - jnp.mean(values, axis=-1, keepdims=True)
    inverse_scale = lax.rsqrt(jnp.mean(centered * centered, axis=-1, keepdims=True) + norm_epsilon)
    return (centered * inverse_scale, inverse_scale)


def normalize_back(grads, normed, inverse_scale):
    return inverse_scale * (
        grads
        - jnp.mean(grads, axis=-1, keepdims=True)
        - normed * jnp.mean(grads * normed, axis=-1, keepdims=True)
    )


def turn(values, cosine, signed_sine):
    lanes = lax.broadcasted_iota(jnp.int32, values.shape, 1)
    swapped = jnp.where(lanes % 64 < 32, pltpu.roll(values, 96, 1), pltpu.roll(values, 32, 1))
    return values * cosine + swapped * signed_sine


def utterance_of(indices, info_ref, count):
    number = jnp.zeros(indices.shape, jnp.int32)
    for u in range(count - 1):
        number = number + (indices >= info_ref[BOUNDS + u]).astype(jnp.int32)
    return number


def by_utterance(number, table):
    out = table[0:1, :]
    for u in range(1, table.shape[0]):
        out = jnp.where(number >= u, table[u : u + 1, :], out)
    return out


def dot_rows(a, b):
    return lax.dot_general(a, b, (((1,), (1,)), ((), ())), preferred_element_type=jnp.float32)


def dot(a, b):
    return jnp.dot(a, b, preferred_element_type=jnp.float32)


def spread(values):
    centered = values - jnp.mean(values, axis=-1, keepdims=True)
    inverse = lax.rsqrt(jnp.mean(centered * centered, axis=-1, keepdims=True) + norm_epsilon)
    return centered * inverse, inverse


def over_rows(total, chunk, body):
    def step(i, carry):
        body(pl.ds(pl.multiple_of(i * chunk, chunk), chunk), i * chunk)
        return carry

    lax.fori_loop(0, total // chunk, step, 0)


def whole(a):
    shape = a.shape
    return pl.BlockSpec(shape, lambda *_: (0,) * len(shape))


def project_kernel(
    count, info_ref, x_ref, m0_ref, m1_ref, m2_ref, m3_ref, here_ref, away_ref, cos_ref, sin_ref, att_ref, qkv_ref, mod_ref
):
    step = pl.program_id(0)
    me, core = info_ref[0], info_ref[1]
    size = x_ref.shape[0]
    width = m0_ref.shape[2]

    @pl.when(step == 0)
    def _():
        mod_ref[...] = jnp.zeros_like(mod_ref)
        for r, piece in enumerate((m0_ref, m1_ref, m2_ref, m3_ref)):
            at = pl.ds(pl.multiple_of(jnp.bitwise_xor(me, r) * width, 128), width)
            mod_ref[:, 0:count, at] = piece[...]

    chunk = 64

    def norm(at, first):
        normed, _ = spread(x_ref[at, :].astype(jnp.float32))
        number = utterance_of(
            lax.broadcasted_iota(jnp.int32, (chunk, 1), 0) + step * size + first, info_ref, count
        )
        shift, scale = by_utterance(number, mod_ref[0, 0:count, :]), by_utterance(number, mod_ref[1, 0:count, :])
        att_ref[at, :] = (normed * (1.0 + scale) + shift).astype(jnp.bfloat16)

    over_rows(size, chunk, norm)
    depth = here_ref.shape[1]
    near = att_ref[:, pl.ds(pl.multiple_of(core * depth, 128), depth)]
    far = att_ref[:, pl.ds(pl.multiple_of((1 - core) * depth, 128), depth)]
    for c in range(3):
        values = dot(near, here_ref[c]) + dot(far, away_ref[c])
        if c < 2:
            for p in range(values.shape[1] // 128):
                lanes = slice(128 * p, 128 * p + 128)
                turned = turn(values[:, lanes], cos_ref[...], sin_ref[...])
                qkv_ref[c, :, lanes] = (turned * 0.125 if c == 0 else turned).astype(jnp.bfloat16)
        else:
            qkv_ref[c] = values.astype(jnp.bfloat16)


def project(info, features_full, mod_pieces, here, away, cosine, sine):
    frames, model_width = features_full.shape
    size = frames // 4
    cycles, count, width = mod_pieces[0].shape
    columns = here.shape[2]
    rows = lambda i, *_: (i, 0)
    return pl.pallas_call(
        partial(project_kernel, count),
        grid_spec=pltpu.PrefetchScalarGridSpec(
            num_scalar_prefetch=1,
            grid=(4,),
            in_specs=[pl.BlockSpec((size, model_width), rows)]
            + [whole(a) for a in (*mod_pieces, here, away)]
            + [pl.BlockSpec((size, 128), rows)] * 2,
            out_specs=[
                pl.BlockSpec((size, model_width), rows),
                pl.BlockSpec((3, size, columns), lambda i, *_: (0, i, 0)),
                pl.BlockSpec((cycles, 8, model_width), lambda *_: (0, 0, 0)),
            ],
        ),
        out_shape=[
            jax.ShapeDtypeStruct((frames, model_width), jnp.bfloat16),
            jax.ShapeDtypeStruct((3, frames, columns), jnp.bfloat16),
            jax.ShapeDtypeStruct((cycles, 8, model_width), jnp.float32),
        ],
        cost_estimate=pl.CostEstimate(
            flops=6 * frames * model_width * columns, transcendentals=0, bytes_accessed=frames * model_width * 6
        ),
        name="project",
    )(info, features_full, *mod_pieces, here, away, cosine, sine)


def forward_kernel(count, info_ref, range_ref, qkv_ref, out0, out1, out2, out3, log_ref, value_t, scores):
    block = pl.program_id(0)
    _, frames, columns = qkv_ref.shape
    size = out0.shape[0]
    pairs = columns // 128
    heads = 2 * pairs

    @pl.when(block == 0)
    def _():
        def rows(i, carry):
            at = pl.ds(pl.multiple_of(i * BLOCK, BLOCK), BLOCK)
            value_t[:, at] = qkv_ref[2, at, :].T
            return carry

        lax.fori_loop(0, frames // BLOCK, rows, 0)

    here = pl.ds(pl.multiple_of(block * size, 128), size)
    query_t = qkv_ref[0, here, :].T
    head_of = lax.broadcasted_iota(jnp.int32, (128, size), 0) < HEAD_DIM
    zero = jnp.zeros((128, size), jnp.bfloat16)
    query_heads = []
    for p in range(pairs):
        part = query_t[128 * p : 128 * p + 128]
        query_heads += [jnp.where(head_of, part, zero), jnp.where(head_of, zero, part)]
    own = utterance_of(lax.broadcasted_iota(jnp.int32, (1, size), 1) + block * size, info_ref, count)
    begin, end = range_ref[0, block], range_ref[1, block]

    def score(i, tops):
        at = pl.ds(pl.multiple_of(i * BLOCK, BLOCK), BLOCK)
        theirs = utterance_of(lax.broadcasted_iota(jnp.int32, (BLOCK, 1), 0) + i * BLOCK, info_ref, count)
        same = theirs == own
        out = []
        for h in range(heads):
            keys = qkv_ref[1, at, 128 * (h // 2) : 128 * (h // 2) + 128]
            s = jnp.dot(keys, query_heads[h], preferred_element_type=jnp.float32)
            s = jnp.where(same, s, -1e30)
            scores[h, at, :] = s
            out.append(jnp.maximum(tops[h], jnp.max(s, axis=0, keepdims=True)))
        return tuple(out)

    lowest = jnp.full((1, size), -1e30, jnp.float32)
    tops = lax.fori_loop(begin, end, score, (lowest,) * heads)

    def weigh(i, carry):
        at = pl.ds(pl.multiple_of(i * BLOCK, BLOCK), BLOCK)
        out = []
        for h in range(heads):
            total, mixed = carry[h]
            p = jnp.exp(scores[h, at, :] - tops[h])
            total = total + jnp.sum(p, axis=0, keepdims=True)
            mixed = mixed + jnp.dot(
                value_t[h * HEAD_DIM : (h + 1) * HEAD_DIM, at], p.astype(jnp.bfloat16), preferred_element_type=jnp.float32
            )
            out.append((total, mixed))
        return tuple(out)

    start = (jnp.zeros((1, size), jnp.float32), jnp.zeros((HEAD_DIM, size), jnp.float32))
    sums = lax.fori_loop(begin, end, weigh, (start,) * heads)
    mixed = jnp.concatenate([sums[h][1] / sums[h][0] for h in range(heads)], axis=0).T.astype(jnp.bfloat16)
    relative = jnp.bitwise_xor(block, info_ref[0])
    for r, out in enumerate((out0, out1, out2, out3)):

        @pl.when(relative == r)
        def _():
            out[...] = mixed

    for h in range(heads):
        log_ref[h : h + 1, here] = tops[h] + jnp.log(sums[h][0])


def backward_kernel(
    count, info_ref, range_ref, qkv_ref, grad0, grad1, grad2, grad3, log_ref, cos_ref, sin_ref, here_ref, away_ref,
    out_ref, part0, part1, part2, part3, key_t, key_sum, value_sum, probs,
    grads, grad_ref
):
    block = pl.program_id(0)
    _, frames, columns = qkv_ref.shape
    size = grad0.shape[0]
    pairs = columns // 128
    heads = 2 * pairs

    @pl.when(block == 0)
    def _():
        key_sum[...] = jnp.zeros_like(key_sum)
        value_sum[...] = jnp.zeros_like(value_sum)

        def rows(i, carry):
            at = pl.ds(pl.multiple_of(i * BLOCK, BLOCK), BLOCK)
            key_t[:, at] = qkv_ref[1, at, :].T
            return carry

        lax.fori_loop(0, frames // BLOCK, rows, 0)

    here = pl.ds(pl.multiple_of(block * size, 128), size)
    relative = jnp.bitwise_xor(block, info_ref[0])
    for r, piece in enumerate((grad0, grad1, grad2, grad3)):

        @pl.when(relative == r)
        def _():
            grad_ref[...] = piece[...]

    upper_t = lax.broadcasted_iota(jnp.int32, (128, size), 0) < HEAD_DIM
    upper = lax.broadcasted_iota(jnp.int32, (size, 128), 1) < HEAD_DIM
    zero_t, zero = jnp.zeros((128, size), jnp.bfloat16), jnp.zeros((size, 128), jnp.bfloat16)
    query_ts, grad_ts, queries, grad_heads = [], [], [], []
    for p in range(pairs):
        query = qkv_ref[0, here, 128 * p : 128 * p + 128]
        grad = grad_ref[:, 128 * p : 128 * p + 128]
        query_t, grad_t = query.T, grad.T
        query_ts += [jnp.where(upper_t, query_t, zero_t), jnp.where(upper_t, zero_t, query_t)]
        grad_ts += [jnp.where(upper_t, grad_t, zero_t), jnp.where(upper_t, zero_t, grad_t)]
        queries += [jnp.where(upper, query, zero), jnp.where(upper, zero, query)]
        grad_heads += [jnp.where(upper, grad, zero), jnp.where(upper, zero, grad)]
    own = utterance_of(lax.broadcasted_iota(jnp.int32, (1, size), 1) + block * size, info_ref, count)
    begin, end = range_ref[0, block], range_ref[1, block]
    logs = [log_ref[h : h + 1, here] for h in range(heads)]

    def first(i, deltas):
        at = pl.ds(pl.multiple_of(i * BLOCK, BLOCK), BLOCK)
        theirs = utterance_of(lax.broadcasted_iota(jnp.int32, (BLOCK, 1), 0) + i * BLOCK, info_ref, count)
        same = theirs == own
        out = []
        for h in range(heads):
            lanes = slice(128 * (h // 2), 128 * (h // 2) + 128)
            s = jnp.dot(qkv_ref[1, at, lanes], query_ts[h], preferred_element_type=jnp.float32)
            p = jnp.exp(jnp.where(same, s, -1e30) - logs[h])
            g = jnp.dot(qkv_ref[2, at, lanes], grad_ts[h], preferred_element_type=jnp.float32)
            probs[h, at, :] = p
            grads[h, at, :] = g
            out.append(deltas[h] + jnp.sum(p * g, axis=0, keepdims=True))
        return tuple(out)

    none = jnp.zeros((1, size), jnp.float32)
    deltas = lax.fori_loop(begin, end, first, (none,) * heads)

    def second(i, sums):
        at = pl.ds(pl.multiple_of(i * BLOCK, BLOCK), BLOCK)
        out = []
        for p in range(pairs):
            lanes = slice(128 * p, 128 * p + 128)
            key_add, value_add = key_sum[at, lanes], value_sum[at, lanes]
            for h in (2 * p, 2 * p + 1):
                weight = probs[h, at, :]
                ds = (weight * (grads[h, at, :] - deltas[h])).astype(jnp.bfloat16)
                out.append(
                    sums[h]
                    + jnp.dot(key_t[h * HEAD_DIM : (h + 1) * HEAD_DIM, at], ds, preferred_element_type=jnp.float32)
                )
                key_add = key_add + jnp.dot(ds, queries[h], preferred_element_type=jnp.float32)
                value_add = value_add + jnp.dot(
                    weight.astype(jnp.bfloat16), grad_heads[h], preferred_element_type=jnp.float32
                )
            key_sum[at, lanes] = key_add
            value_sum[at, lanes] = value_add
        return tuple(out)

    zero_sum = jnp.zeros((HEAD_DIM, size), jnp.float32)
    sums = lax.fori_loop(begin, end, second, (zero_sum,) * heads)
    grad_query = jnp.concatenate(sums, axis=0).T * 0.125
    for p in range(pairs):
        lanes = slice(128 * p, 128 * p + 128)
        out_ref[0, here, lanes] = turn(grad_query[:, lanes], cos_ref[here, :], -sin_ref[here, :]).astype(jnp.bfloat16)

    @pl.when(block == pl.num_programs(0) - 1)
    def _():
        def rows(i, carry):
            at = pl.ds(pl.multiple_of(i * BLOCK, BLOCK), BLOCK)
            for p in range(pairs):
                lanes = slice(128 * p, 128 * p + 128)
                out_ref[1, at, lanes] = turn(key_sum[at, lanes], cos_ref[at, :], -sin_ref[at, :]).astype(jnp.bfloat16)
            out_ref[2, at, :] = value_sum[at, :].astype(jnp.bfloat16)
            return carry

        lax.fori_loop(0, frames // BLOCK, rows, 0)
        depth = here_ref.shape[1]
        for r, part in enumerate((part0, part1, part2, part3)):
            at = pl.ds(pl.multiple_of(jnp.bitwise_xor(info_ref[0], r) * size, 128), size)
            for side, weight in ((info_ref[1], here_ref), (1 - info_ref[1], away_ref)):
                total = dot_rows(out_ref[0, at, :], weight[0])
                for c in (1, 2):
                    total = total + dot_rows(out_ref[c, at, :], weight[c])
                part[:, pl.ds(pl.multiple_of(side * depth, 128), depth)] = total.astype(part.dtype)


def key_ranges(ending, frames, size):
    starting = jnp.concatenate([jnp.zeros((1,), jnp.int32), ending[:-1]])
    begins = jnp.arange(frames // size, dtype=jnp.int32) * size
    first_key = jnp.min(jnp.where(ending[None, :] > begins[:, None], starting[None, :], frames), axis=1)
    last_key = jnp.max(jnp.where(starting[None, :] < begins[:, None] + size, ending[None, :], 0), axis=1)
    return jnp.stack([first_key // BLOCK, (last_key + BLOCK - 1) // BLOCK]).astype(jnp.int32)


def attend(info, ranges, qkv, count):
    _, frames, columns = qkv.shape
    heads = columns // HEAD_DIM
    size = frames // 4
    flat = lambda b, *_: (0, 0)
    return pl.pallas_call(
        partial(forward_kernel, count),
        grid_spec=pltpu.PrefetchScalarGridSpec(
            num_scalar_prefetch=2,
            grid=(4,),
            in_specs=[pl.BlockSpec((3, frames, columns), lambda b, *_: (0, 0, 0))],
            out_specs=[pl.BlockSpec((size, columns), flat)] * 4 + [pl.BlockSpec((heads, frames), flat)],
            scratch_shapes=[
                pltpu.VMEM((columns, frames), jnp.bfloat16),
                pltpu.VMEM((heads, frames, size), jnp.float32),
            ],
        ),
        out_shape=[jax.ShapeDtypeStruct((size, columns), jnp.bfloat16)] * 4
        + [jax.ShapeDtypeStruct((heads, frames), jnp.float32)],
        cost_estimate=pl.CostEstimate(
            flops=8 * frames * frames * columns, transcendentals=heads * frames * frames, bytes_accessed=frames * columns * 8
        ),
        name="attend",
    )(info, ranges, qkv)


def attend_back(info, ranges, qkv, grad_pieces, logs, cosine, sine, here, away, count):
    _, frames, columns = qkv.shape
    heads = columns // HEAD_DIM
    size = frames // 4
    cube = lambda b, *_: (0, 0, 0)
    flat = lambda b, *_: (0, 0)
    return pl.pallas_call(
        partial(backward_kernel, count),
        grid_spec=pltpu.PrefetchScalarGridSpec(
            num_scalar_prefetch=2,
            grid=(4,),
            in_specs=[pl.BlockSpec((3, frames, columns), cube)]
            + [pl.BlockSpec((size, columns), flat)] * 4
            + [pl.BlockSpec((heads, frames), flat), pl.BlockSpec((frames, 128), flat), pl.BlockSpec((frames, 128), flat)]
            + [whole(here), whole(away)],
            out_specs=[pl.BlockSpec((3, frames, columns), cube)] + [pl.BlockSpec((size, 2 * here.shape[1]), flat)] * 4,
            scratch_shapes=[
                pltpu.VMEM((columns, frames), jnp.bfloat16),
                pltpu.VMEM((frames, columns), jnp.float32),
                pltpu.VMEM((frames, columns), jnp.float32),
                pltpu.VMEM((heads, frames, size), jnp.float32),
                pltpu.VMEM((heads, frames, size), jnp.float32),
                pltpu.VMEM((size, columns), jnp.bfloat16),
            ],
        ),
        out_shape=[jax.ShapeDtypeStruct((3, frames, columns), jnp.bfloat16)]
        + [jax.ShapeDtypeStruct((size, 2 * here.shape[1]), jnp.bfloat16 if r else jnp.float32) for r in range(4)],
        cost_estimate=pl.CostEstimate(
            flops=16 * frames * frames * columns, transcendentals=heads * frames * frames, bytes_accessed=frames * columns * 20
        ),
        name="attend_back",
    )(info, ranges, qkv, *grad_pieces, logs, cosine, sine, here, away)


def middle_kernel(
    count, info_ref, x_ref, cot_ref, mixed0, mixed1, mixed2, mixed3, mod_ref, *refs
):
    pieces = refs[:10]
    out_ref, res_ref, g0, g1, g2, g3, sums_ref, ffn_in_ref, hidden_ref, grad_up_ref, grad_attn_ref, grad_ffn_ref = refs[10:22]
    wide, mixed, residual, attn, up, ffn, inverse, sems = refs[22:]
    me, core, group = info_ref[0], info_ref[1], info_ref[2]
    size = x_ref.shape[0]
    width = mixed0.shape[1]
    quarter = pieces[0].shape[2]
    depth = 4 * quarter

    copies = ([], [])
    for side in range(2):
        half = core if side == 0 else 1 - core
        for k, r in [(k, r) for k in range(4) for r in range(4)]:
            if k < 3:
                piece = pieces[5 * side + k].at[r]
            else:
                piece = pieces[5 * side + 3 + r // 2].at[r % 2]
            at = pl.ds(pl.multiple_of(half * depth + jnp.bitwise_xor(group, k) * quarter, 16), quarter)
            lanes = slice(r * width, (r + 1) * width)
            for part, cs in enumerate((slice(0, 1), slice(1, 5))):
                copy = pltpu.make_async_copy(
                    piece.at[cs], wide.at[cs, at, lanes], sems.at[part * 32 + side * 16 + k * 4 + r]
                )
                copies[part].append(copy)
    for copy in copies[0] + copies[1]:
        copy.start()
    for r, piece in enumerate((mixed0, mixed1, mixed2, mixed3)):
        mixed[:, r * width : (r + 1) * width] = piece[...]
    chunk = 64

    def table(c, number):
        return by_utterance(number, mod_ref[c, 0:count, :])

    def numbers(first):
        return utterance_of(lax.broadcasted_iota(jnp.int32, (chunk, 1), 0) + me * size + first, info_ref, count)

    for copy in copies[0]:
        copy.wait()
    attn[...] = dot_rows(mixed[...], wide[0])

    def enter(at, first):
        number = numbers(first)
        value = x_ref[at, :].astype(jnp.float32) + table(2, number) * attn[at, :]
        residual[at, :] = value
        normed, scale = spread(value)
        inverse[at, :] = jnp.broadcast_to(scale, (chunk, 128))
        ffn[at, :] = normed
        ffn_in_ref[at, :] = (normed * (1.0 + table(4, number)) + table(3, number)).astype(jnp.bfloat16)
        grad_ffn_ref[at, :] = (cot_ref[at, :].astype(jnp.float32) * table(5, number)).astype(jnp.bfloat16)

    over_rows(size, chunk, enter)
    for copy in copies[1]:
        copy.wait()
    for c in range(2):
        up[c] = dot(ffn_in_ref[...], wide[3 + c])

    root = math.sqrt(2.0 / math.pi)

    def act(at, first):
        for c in range(2):
            value = up[c, at, :]
            square = value * value
            bend = jnp.tanh(root * (value + 0.044715 * (value * square)))
            hidden_ref[c, at, :] = (0.5 * value * (1.0 + bend)).astype(jnp.bfloat16)
            up[c, at, :] = 0.5 * (1.0 + bend) + 0.5 * value * (1.0 - bend * bend) * (root * (1.0 + 0.134145 * square))

    over_rows(size, chunk, act)
    grad_hidden = [dot(grad_ffn_ref[...], wide[1 + c]) for c in range(2)]
    for c in range(2):
        grad_up_ref[c] = (up[c] * grad_hidden[c]).astype(jnp.bfloat16)
    up[0] = dot_rows(hidden_ref[0], wide[1]) + dot_rows(hidden_ref[1], wide[2])
    up[1] = dot_rows(grad_up_ref[0], wide[3]) + dot_rows(grad_up_ref[1], wide[4])
    sums_ref[...] = jnp.zeros_like(sums_ref)

    def leave(at, first):
        number = numbers(first)
        cot = cot_ref[at, :].astype(jnp.float32)
        ffn_out, grad_in, normed = up[0, at, :], up[1, at, :], ffn[at, :]
        out_ref[at, :] = (residual[at, :] + table(5, number) * ffn_out).astype(jnp.bfloat16)
        h = grad_in * (1.0 + table(4, number))
        grad = cot + inverse[at, 0:1] * (
            h - jnp.mean(h, axis=-1, keepdims=True) - normed * jnp.mean(h * normed, axis=-1, keepdims=True)
        )
        res_ref[at, :] = grad
        grad_attn_ref[at, :] = (grad * table(2, number)).astype(jnp.bfloat16)
        for c, rows in enumerate((grad * attn[at, :], grad_in, grad_in * normed, cot * ffn_out)):
            for u in range(count):
                sums_ref[c, u : u + 1, :] += jnp.sum(jnp.where(number == u, rows, 0.0), axis=0, keepdims=True)

    over_rows(size, chunk, leave)
    grad_mixed = dot(grad_attn_ref[...], wide[0]).astype(jnp.bfloat16)
    for r, piece in enumerate((g0, g1, g2, g3)):
        piece[...] = grad_mixed[:, r * width : (r + 1) * width]


def middle(info, features, cotangent, mixed_pieces, modulation, wide_here, wide_away, count):
    size, model_width = features.shape
    width = mixed_pieces[0].shape[1]
    pieces = (*wide_here, *wide_away)
    shapes = [
        ((size, model_width), jnp.bfloat16),
        ((size, model_width), jnp.float32),
        *[((size, width), jnp.bfloat16)] * 4,
        ((4, 8, model_width), jnp.float32),
        ((size, model_width), jnp.bfloat16),
        ((2, size, 4 * width), jnp.bfloat16),
        ((2, size, 4 * width), jnp.bfloat16),
        ((size, model_width), jnp.bfloat16),
        ((size, model_width), jnp.bfloat16),
    ]
    outs = [jax.ShapeDtypeStruct(shape, kind) for shape, kind in shapes]
    return pl.pallas_call(
        partial(middle_kernel, count),
        grid_spec=pltpu.PrefetchScalarGridSpec(
            num_scalar_prefetch=1,
            grid=(1,),
            in_specs=[whole(a) for a in (features, cotangent, *mixed_pieces, modulation)]
            + [pl.BlockSpec(memory_space=pl.ANY)] * 10,
            out_specs=[whole(a) for a in outs],
            scratch_shapes=[
                pltpu.VMEM((5, model_width, 4 * width), jnp.bfloat16),
                pltpu.VMEM((size, 4 * width), jnp.bfloat16),
                pltpu.VMEM((size, model_width), jnp.float32),
                pltpu.VMEM((size, model_width), jnp.float32),
                pltpu.VMEM((2, size, 4 * width), jnp.float32),
                pltpu.VMEM((size, model_width), jnp.float32),
                pltpu.VMEM((size, 128), jnp.float32),
                pltpu.SemaphoreType.DMA((64,)),
            ],
        ),
        out_shape=outs,
        cost_estimate=pl.CostEstimate(
            flops=20 * size * model_width * 4 * width, transcendentals=size * 8 * width, bytes_accessed=10 * model_width * 4 * width
        ),
        name="middle",
    )(info, features, cotangent, *mixed_pieces, modulation, *pieces)


def wide_grad_kernel(side, summed, info_ref, mixed_ref, hidden_ref, grad_up_ref, *refs):
    grad_refs, other_ref, out_ref, turned = refs[:3], refs[3] if summed else None, refs[-2], refs[-1]
    depth = out_ref.shape[2]
    half = info_ref[1] if side == 0 else 1 - info_ref[1]

    @pl.when(pl.program_id(0) == 0)
    def _():
        at = pl.ds(pl.multiple_of(half * depth, 128), depth)
        for i in range(3):
            turned[i] = grad_refs[i][:, at].T

    def block(c):
        if c == 0:
            return dot(turned[0], mixed_ref[0])
        if c < 3:
            return dot(turned[1], hidden_ref[c - 1])
        return dot(turned[2], grad_up_ref[c - 3])

    for c in range(5):
        value = block(c)
        if summed:
            value = value + other_ref[0, c].astype(jnp.float32)
        out_ref[0, c] = value.astype(jnp.bfloat16)


def wide_grads(info, side, mixed, hidden, grad_up, grad_attn, grad_ffn, ffn_in, other=None):
    _, size, width = mixed.shape
    depth = grad_attn.shape[1] // 2
    lanes = lambda r, info: (0, 0, r)
    target = pl.BlockSpec((1, 5, depth, width), lambda r, info: (jnp.bitwise_xor(info[0], r), 0, 0, 0))
    return pl.pallas_call(
        partial(wide_grad_kernel, side, other is not None),
        grid_spec=pltpu.PrefetchScalarGridSpec(
            num_scalar_prefetch=1,
            grid=(4,),
            in_specs=[
                pl.BlockSpec((1, size, width), lambda r, info: (r, 0, 0)),
                pl.BlockSpec((2, size, width), lanes),
                pl.BlockSpec((2, size, width), lanes),
                whole(grad_attn),
                whole(grad_ffn),
                whole(ffn_in),
            ]
            + ([target] if other is not None else []),
            out_specs=target,
            scratch_shapes=[pltpu.VMEM((3, depth, size), jnp.bfloat16)],
        ),
        out_shape=jax.ShapeDtypeStruct((4, 5, depth, width), jnp.bfloat16),
        cost_estimate=pl.CostEstimate(
            flops=40 * size * depth * width, transcendentals=0, bytes_accessed=60 * depth * width
        ),
        name="wide_grads",
    )(info, mixed, hidden, grad_up, grad_attn, grad_ffn, ffn_in, *([other] if other is not None else []))


def qkv_grad_kernel(side, summed, info_ref, grad_ref, att_ref, *refs):
    other_ref, out_ref, turned = refs[0] if summed else None, refs[-2], refs[-1]
    depth = out_ref.shape[1]
    half = info_ref[1] if side == 0 else 1 - info_ref[1]

    @pl.when(pl.program_id(0) == 0)
    def _():
        turned[...] = att_ref[:, pl.ds(pl.multiple_of(half * depth, 128), depth)].T

    value = dot(turned[...], grad_ref[0])
    if summed:
        value = value + other_ref[0].astype(jnp.float32)
    out_ref[0] = value.astype(out_ref.dtype)


def qkv_grads(info, side, gradients, att_full, other=None, kind=jnp.bfloat16):
    _, frames, columns = gradients.shape
    depth = att_full.shape[1] // 2
    target = pl.BlockSpec((1, depth, columns), lambda c, *_: (c, 0, 0))
    return pl.pallas_call(
        partial(qkv_grad_kernel, side, other is not None),
        grid_spec=pltpu.PrefetchScalarGridSpec(
            num_scalar_prefetch=1,
            grid=(3,),
            in_specs=[pl.BlockSpec((1, frames, columns), lambda c, *_: (c, 0, 0)), whole(att_full)]
            + ([target] if other is not None else []),
            out_specs=target,
            scratch_shapes=[pltpu.VMEM((depth, frames), jnp.bfloat16)],
        ),
        out_shape=jax.ShapeDtypeStruct((3, depth, columns), kind),
        cost_estimate=pl.CostEstimate(
            flops=6 * frames * depth * columns, transcendentals=0, bytes_accessed=frames * depth * 6
        ),
        name="qkv_grads",
    )(info, gradients, att_full, *([other] if other is not None else []))


def inner_step(grads, first, second, weights, steps_done):
    first_new = beta_first * first + (1.0 - beta_first) * grads
    second_new = beta_second * second + (1.0 - beta_second) * grads * grads
    correct_one = 1.0 - beta_first**steps_done
    correct_two = 1.0 - beta_second**steps_done
    difference = inner_rate * (
        first_new / correct_one / (jnp.sqrt(second_new / correct_two) + adam_epsilon)
        + weight_decay * weights
    )
    return (first_new[None], second_new[None], difference)


def outer_step(average, outer, weights):
    outer_new = outer_beta * outer + average
    return (outer_new, weights - outer_rate * (average + outer_beta * outer_new))


def swapped(values, axis, bits):
    size = lax.axis_size(axis)
    return lax.ppermute(values, axis, [(i, i ^ bits) for i in range(size)])


def exchange(blocks, axis="tensor"):
    return [blocks[0]] + [swapped(blocks[r], axis, r) for r in range(1, 4)]


def after(values, *others):
    return lax.optimization_barrier((values, *others))[0]


def dp_rows(own):
    if lax.axis_size("dp") != 2:
        return lax.all_gather(own, "dp", axis=0, tiled=True)
    other = swapped(own, "dp", 1)
    first = lax.axis_index("dp") == 0
    return jnp.concatenate([jnp.where(first, own, other), jnp.where(first, other, own)], axis=0)


def dp_pair(own):
    if lax.axis_size("dp") == 2:
        return own, swapped(own, "dp", 1)
    return tuple(jnp.split(lax.all_gather(own, "dp", axis=1, tiled=True), 2, axis=1))


def gather_wide(half):
    group = lax.axis_index("group")
    quarter = half.shape[1] // 4
    own = lax.dynamic_slice_in_dim(half, group * quarter, quarter, 1)
    stack = jnp.stack(exchange([own] * 4))
    one, two = swapped(stack, "group", 1), swapped(stack, "group", 2)
    return [stack, one, two, swapped(one[:2], "group", 2), swapped(two[2:], "group", 1)]


def wide_halves(own):
    if lax.axis_size("dp") == 2:
        here = gather_wide(own)
        return here, [swapped(piece, "dp", 1) for piece in here]
    halves = dp_pair(own)
    return gather_wide(halves[0]), gather_wide(halves[1])


def group_sum(values):
    group = lax.axis_index("group")
    quarter = values.shape[1] // 4
    parts = exchange([lax.dynamic_slice_in_dim(values, (group ^ r) * quarter, quarter, 1) for r in range(4)], "group")
    total = sum(part.astype(jnp.float32) for part in parts).astype(low)
    out = jnp.zeros_like(values)
    for r, part in enumerate(exchange([total] * 4, "group")):
        out = lax.dynamic_update_slice_in_dim(out, part, (group ^ r) * quarter, 1)
    return out


def per_device(
    features,
    cotangent,
    frame_counts,
    buckets,
    step_count,
    col_weights,
    mod_weights,
    row_weights,
    col_first,
    col_second,
    mod_first,
    mod_second,
    row_first,
    row_second,
    col_outer,
    mod_outer,
    row_outer,
):
    group_count = lax.axis_size("group")
    packs_here = lax.axis_size("dp")
    own_rows, model_width = features.shape
    frames = own_rows * 4
    me = lax.axis_index("tensor")
    core = lax.axis_index("dp")
    group = lax.axis_index("group")
    count = buckets.shape[1]
    share = mod_weights.shape[0]
    width = col_weights.shape[2]

    def columns_first(values):
        return jnp.swapaxes(values, -3, -2)

    features_full = lax.all_gather(features, "tensor", axis=0, tiled=True)

    buckets_all = dp_rows(buckets[0])
    flow_time = ((group * NBUCK + buckets_all).astype(jnp.float32) + 0.5) / (NBUCK * group_count)
    condition_all = jax.nn.silu(time_embedding(flow_time, model_width)).astype(low)
    condition_here = lax.dynamic_slice_in_dim(condition_all, core * share, share, 1)
    mod_terms = jnp.einsum("ud,dcj->cuj", condition_here, mod_weights.astype(low), preferred_element_type=jnp.float32)
    if packs_here != 2:
        mod_part = lax.psum_scatter(mod_terms, "dp", scatter_dimension=1, tiled=True)
    else:
        mod_away = lax.dynamic_slice_in_dim(mod_terms, (1 - core) * count, count, 1)
        mod_part = lax.dynamic_slice_in_dim(mod_terms, core * count, count, 1) + swapped(mod_away, "dp", 1)
    mod_pieces = exchange([mod_part] * 4)

    ending = jnp.cumsum(frame_counts[0]).astype(jnp.int32)
    half_core = core if packs_here == 2 else jnp.zeros_like(core)
    info = jnp.concatenate([jnp.stack([me, half_core, group]).astype(jnp.int32), ending])
    _, position = utterance_rows(ending, jnp.arange(frames, dtype=jnp.int32))
    cosine, sine = rotary_tables(position)
    ranges = key_ranges(ending, frames, own_rows)
    col_major = columns_first(col_weights).astype(low)
    qkv_here, qkv_away = dp_pair(col_major[0:3])
    wide_low = after(jnp.concatenate([row_weights.astype(low), col_major[3:5]], axis=0), *mod_pieces)
    wide_here, wide_away = wide_halves(wide_low)

    att_full, qkv, modulation = project(info, features_full, mod_pieces, qkv_here, qkv_away, cosine, sine)
    *mixed_pieces, log_totals = attend(info, ranges, qkv, count)
    mixed_pieces = exchange(mixed_pieces)

    (output, grad_residual, g0, g1, g2, g3, late_sums, ffn_in, hidden, grad_up, grad_attn, grad_ffn) = middle(
        info, features, cotangent, mixed_pieces, modulation, wide_here, wide_away, count
    )
    grad_pieces = exchange([g0, g1, g2, g3])
    wide_args = (jnp.stack(mixed_pieces), hidden, grad_up, grad_attn, grad_ffn, ffn_in)
    if packs_here == 2:
        wide_blocks = wide_grads(info, 0, *wide_args, other=swapped(wide_grads(info, 1, *wide_args), "dp", 1))
    else:
        both = jnp.concatenate([wide_grads(info, side, *wide_args) for side in range(2)], axis=2).astype(jnp.float32)
        wide_blocks = lax.psum_scatter(both, "dp", scatter_dimension=2, tiled=True).astype(low)
    wide_grad = lax.psum_scatter(wide_blocks, "tensor", scatter_dimension=0, tiled=False).astype(jnp.float32)

    def mod_gradient(sums):
        mine = [lax.dynamic_slice_in_dim(sums, (me ^ r) * width, width, 2) for r in range(4)]
        columns = dp_rows(jnp.swapaxes(sum(exchange(mine)), 0, 1))
        if packs_here != 2:
            return jnp.einsum("ud,ucj->cdj", condition_here.astype(jnp.float32), columns, precision=highest)
        total = 0.0
        for u in range(columns.shape[0]):
            total = total + condition_here[u].astype(jnp.float32)[None, :, None] * columns[u][:, None, :]
        return total

    late_mod = mod_gradient(late_sums[:, :count])
    gradients, *att_parts = attend_back(
        info, ranges, qkv, grad_pieces, log_totals, cosine, sine, qkv_here, qkv_away, count
    )
    att_parts = exchange(att_parts)
    grad_att_in = sum(part.astype(jnp.float32) for part in att_parts)
    if packs_here == 2:
        qkv_away_grad = swapped(qkv_grads(info, 1, gradients, att_full), "dp", 1)
        qkv_share = qkv_grads(info, 0, gradients, att_full, other=qkv_away_grad, kind=jnp.float32)
    else:
        both = [qkv_grads(info, side, gradients, att_full, kind=jnp.float32) for side in range(2)]
        qkv_share = lax.psum_scatter(jnp.concatenate(both, axis=1), "dp", scatter_dimension=1, tiled=True)

    number_own, _ = utterance_rows(ending, me * own_rows + jnp.arange(own_rows, dtype=jnp.int32))
    number_own = number_own[:, None]
    normed, inverse_scale = normalize(features.astype(jnp.float32))
    grad_features = grad_residual + normalize_back(
        grad_att_in * (1.0 + by_utterance(number_own, modulation[1, :count])), normed, inverse_scale
    )
    early_rows = (grad_att_in, grad_att_in * normed)
    early_sums = jnp.stack(
        [
            jnp.stack([jnp.sum(jnp.where(number_own == u, rows, 0.0), axis=0) for u in range(count)])
            for rows in early_rows
        ]
    )
    early_mod = mod_gradient(early_sums)

    steps_done = step_count[0].astype(jnp.float32)
    row_first_new, row_second_new, row_diff = inner_step(
        wide_grad[0:3], row_first[0], row_second[0], row_weights, steps_done
    )
    col_first_new, col_second_new, col_diff = inner_step(
        columns_first(jnp.concatenate([qkv_share, wide_grad[3:5]], axis=0)), col_first[0], col_second[0], col_weights, steps_done
    )
    mod_first_new, mod_second_new, mod_diff = inner_step(
        columns_first(jnp.concatenate([early_mod, late_mod], axis=0)), mod_first[0], mod_second[0], mod_weights, steps_done
    )

    diffs = jnp.concatenate(
        [row_diff.astype(low), columns_first(col_diff).astype(low), columns_first(mod_diff).astype(low)], axis=0
    )
    averages = group_sum(diffs).astype(jnp.float32) / group_count
    row_average, col_average, mod_average = averages[0:3], columns_first(averages[3:8]), columns_first(averages[8:14])
    col_outer_new, col_new = outer_step(col_average, col_outer, col_weights)
    mod_outer_new, mod_new = outer_step(mod_average, mod_outer, mod_weights)
    row_outer_new, row_new = outer_step(row_average, row_outer, row_weights)
    return (
        output,
        grad_features,
        col_first_new,
        col_second_new,
        col_average,
        col_outer_new,
        col_new,
        mod_first_new,
        mod_second_new,
        mod_average,
        mod_outer_new,
        mod_new,
        row_first_new,
        row_second_new,
        row_average,
        row_outer_new,
        row_new,
    )


def solution(mesh):
    placed = (
        P(("group", "dp", "tensor"), None),
        P(("group", "dp", "tensor"), None),
        P(("group", "dp"), None),
        P(("group", "dp"), None),
        P(),
        P("dp", None, "tensor"),
        P("dp", None, "tensor"),
        P(None, "dp", "tensor"),
        P("group", "dp", None, "tensor"),
        P("group", "dp", None, "tensor"),
        P("group", "dp", None, "tensor"),
        P("group", "dp", None, "tensor"),
        P("group", None, "dp", "tensor"),
        P("group", None, "dp", "tensor"),
        P("dp", None, "tensor"),
        P("dp", None, "tensor"),
        P(None, "dp", "tensor"),
    )
    return jax.shard_map(
        per_device,
        mesh=mesh,
        in_specs=placed,
        out_specs=(
            P(("group", "dp", "tensor"), None),
            P(("group", "dp", "tensor"), None),
            P("group", "dp", None, "tensor"),
            P("group", "dp", None, "tensor"),
            P("dp", None, "tensor"),
            P("dp", None, "tensor"),
            P("dp", None, "tensor"),
            P("group", "dp", None, "tensor"),
            P("group", "dp", None, "tensor"),
            P("dp", None, "tensor"),
            P("dp", None, "tensor"),
            P("dp", None, "tensor"),
            P("group", None, "dp", "tensor"),
            P("group", None, "dp", "tensor"),
            P(None, "dp", "tensor"),
            P(None, "dp", "tensor"),
            P(None, "dp", "tensor"),
        ),
        check_vma=False,
    )
```

```python
from functools import partial
import math

import jax
import jax.numpy as jnp
from jax import lax
from jax.experimental import pallas as pl
from jax.experimental.pallas import tpu as pltpu
from jax.sharding import PartitionSpec as P

HEAD_DIM = 64
NBUCK = 8
BLOCK = 256
BOUNDS = 3

highest = lax.Precision.HIGHEST
norm_epsilon = 1e-06
adam_epsilon = 1e-08
beta_first = 0.9
beta_second = 0.999
inner_rate = 0.05
weight_decay = 0.01
outer_rate = 0.7
outer_beta = 0.9
low = jnp.bfloat16


def time_embedding(flow_time, width_all):
    half_width = width_all // 2
    frequency = jnp.exp(
        jnp.arange(half_width, dtype=jnp.float32) * (-math.log(10000.0) / (half_width - 1))
    )
    angles = 1000.0 * flow_time[:, None] * frequency[None, :]
    return jnp.concatenate([jnp.sin(angles), jnp.cos(angles)], axis=1)


def utterance_rows(ending, indices):
    number = jnp.zeros(indices.shape, jnp.int32)
    begin = jnp.zeros(indices.shape, jnp.int32)
    for u in range(ending.shape[0] - 1):
        after = indices >= ending[u]
        number = number + after.astype(jnp.int32)
        begin = jnp.where(after, ending[u], begin)
    return number, indices - begin


def rotary_tables(position):
    half_width = HEAD_DIM // 2
    frequency = jnp.exp(
        jnp.arange(half_width, dtype=jnp.float32) * (-2.0 * math.log(10000.0) / HEAD_DIM)
    )
    angles = position.astype(jnp.float32)[:, None] * frequency[None, :]
    cosine, sine = jnp.cos(angles), jnp.sin(angles)
    return jnp.concatenate([cosine] * 4, axis=1), jnp.concatenate([-sine, sine, -sine, sine], axis=1)


def normalize(values):
    centered = values - jnp.mean(values, axis=-1, keepdims=True)
    inverse_scale = lax.rsqrt(jnp.mean(centered * centered, axis=-1, keepdims=True) + norm_epsilon)
    return (centered * inverse_scale, inverse_scale)


def normalize_back(grads, normed, inverse_scale):
    return inverse_scale * (
        grads
        - jnp.mean(grads, axis=-1, keepdims=True)
        - normed * jnp.mean(grads * normed, axis=-1, keepdims=True)
    )


def turn(values, cosine, signed_sine):
    lanes = lax.broadcasted_iota(jnp.int32, values.shape, 1)
    swapped = jnp.where(lanes % 64 < 32, pltpu.roll(values, 96, 1), pltpu.roll(values, 32, 1))
    return values * cosine + swapped * signed_sine


def utterance_of(indices, info_ref, count):
    number = jnp.zeros(indices.shape, jnp.int32)
    for u in range(count - 1):
        number = number + (indices >= info_ref[BOUNDS + u]).astype(jnp.int32)
    return number


def by_utterance(number, table):
    out = table[0:1, :]
    for u in range(1, table.shape[0]):
        out = jnp.where(number >= u, table[u : u + 1, :], out)
    return out


def dot_rows(a, b):
    return lax.dot_general(a, b, (((1,), (1,)), ((), ())), preferred_element_type=jnp.float32)


def dot(a, b):
    return jnp.dot(a, b, preferred_element_type=jnp.float32)


def spread(values):
    centered = values - jnp.mean(values, axis=-1, keepdims=True)
    inverse = lax.rsqrt(jnp.mean(centered * centered, axis=-1, keepdims=True) + norm_epsilon)
    return centered * inverse, inverse


def over_rows(total, chunk, body):
    def step(i, carry):
        body(pl.ds(pl.multiple_of(i * chunk, chunk), chunk), i * chunk)
        return carry

    lax.fori_loop(0, total // chunk, step, 0)


def whole(a):
    shape = a.shape
    return pl.BlockSpec(shape, lambda *_: (0,) * len(shape))


def project_kernel(
    count, info_ref, x_ref, m0_ref, m1_ref, m2_ref, m3_ref, here_ref, away_ref, cos_ref, sin_ref, att_ref, qkv_ref, mod_ref
):
    step = pl.program_id(0)
    me, core = info_ref[0], info_ref[1]
    size = x_ref.shape[0]
    width = m0_ref.shape[2]

    @pl.when(step == 0)
    def _():
        mod_ref[...] = jnp.zeros_like(mod_ref)
        for r, piece in enumerate((m0_ref, m1_ref, m2_ref, m3_ref)):
            at = pl.ds(pl.multiple_of(jnp.bitwise_xor(me, r) * width, 128), width)
            mod_ref[:, 0:count, at] = piece[...]

    chunk = 64

    def norm(at, first):
        normed, _ = spread(x_ref[at, :].astype(jnp.float32))
        number = utterance_of(
            lax.broadcasted_iota(jnp.int32, (chunk, 1), 0) + step * size + first, info_ref, count
        )
        shift, scale = by_utterance(number, mod_ref[0, 0:count, :]), by_utterance(number, mod_ref[1, 0:count, :])
        att_ref[at, :] = (normed * (1.0 + scale) + shift).astype(jnp.bfloat16)

    over_rows(size, chunk, norm)
    depth = here_ref.shape[1]
    near = att_ref[:, pl.ds(pl.multiple_of(core * depth, 128), depth)]
    far = att_ref[:, pl.ds(pl.multiple_of((1 - core) * depth, 128), depth)]
    for c in range(3):
        values = dot(near, here_ref[c]) + dot(far, away_ref[c])
        if c < 2:
            for p in range(values.shape[1] // 128):
                lanes = slice(128 * p, 128 * p + 128)
                turned = turn(values[:, lanes], cos_ref[...], sin_ref[...])
                qkv_ref[c, :, lanes] = (turned * 0.125 if c == 0 else turned).astype(jnp.bfloat16)
        else:
            qkv_ref[c] = values.astype(jnp.bfloat16)


def project(info, features_full, mod_pieces, here, away, cosine, sine):
    frames, model_width = features_full.shape
    size = frames // 4
    cycles, count, width = mod_pieces[0].shape
    columns = here.shape[2]
    rows = lambda i, *_: (i, 0)
    return pl.pallas_call(
        partial(project_kernel, count),
        grid_spec=pltpu.PrefetchScalarGridSpec(
            num_scalar_prefetch=1,
            grid=(4,),
            in_specs=[pl.BlockSpec((size, model_width), rows)]
            + [whole(a) for a in (*mod_pieces, here, away)]
            + [pl.BlockSpec((size, 128), rows)] * 2,
            out_specs=[
                pl.BlockSpec((size, model_width), rows),
                pl.BlockSpec((3, size, columns), lambda i, *_: (0, i, 0)),
                pl.BlockSpec((cycles, 8, model_width), lambda *_: (0, 0, 0)),
            ],
        ),
        out_shape=[
            jax.ShapeDtypeStruct((frames, model_width), jnp.bfloat16),
            jax.ShapeDtypeStruct((3, frames, columns), jnp.bfloat16),
            jax.ShapeDtypeStruct((cycles, 8, model_width), jnp.float32),
        ],
        cost_estimate=pl.CostEstimate(
            flops=6 * frames * model_width * columns, transcendentals=0, bytes_accessed=frames * model_width * 6
        ),
        name="project",
    )(info, features_full, *mod_pieces, here, away, cosine, sine)


def forward_kernel(count, info_ref, range_ref, qkv_ref, out0, out1, out2, out3, log_ref, value_t, scores):
    block = pl.program_id(0)
    _, frames, columns = qkv_ref.shape
    size = out0.shape[0]
    pairs = columns // 128
    heads = 2 * pairs

    @pl.when(block == 0)
    def _():
        def rows(i, carry):
            at = pl.ds(pl.multiple_of(i * BLOCK, BLOCK), BLOCK)
            value_t[:, at] = qkv_ref[2, at, :].T
            return carry

        lax.fori_loop(0, frames // BLOCK, rows, 0)

    here = pl.ds(pl.multiple_of(block * size, 128), size)
    query_t = qkv_ref[0, here, :].T
    head_of = lax.broadcasted_iota(jnp.int32, (128, size), 0) < HEAD_DIM
    zero = jnp.zeros((128, size), jnp.bfloat16)
    query_heads = []
    for p in range(pairs):
        part = query_t[128 * p : 128 * p + 128]
        query_heads += [jnp.where(head_of, part, zero), jnp.where(head_of, zero, part)]
    own = utterance_of(lax.broadcasted_iota(jnp.int32, (1, size), 1) + block * size, info_ref, count)
    begin, end = range_ref[0, block], range_ref[1, block]

    def score(i, tops):
        at = pl.ds(pl.multiple_of(i * BLOCK, BLOCK), BLOCK)
        theirs = utterance_of(lax.broadcasted_iota(jnp.int32, (BLOCK, 1), 0) + i * BLOCK, info_ref, count)
        same = theirs == own
        out = []
        for h in range(heads):
            keys = qkv_ref[1, at, 128 * (h // 2) : 128 * (h // 2) + 128]
            s = jnp.dot(keys, query_heads[h], preferred_element_type=jnp.float32)
            s = jnp.where(same, s, -1e30)
            scores[h, at, :] = s
            out.append(jnp.maximum(tops[h], jnp.max(s, axis=0, keepdims=True)))
        return tuple(out)

    lowest = jnp.full((1, size), -1e30, jnp.float32)
    tops = lax.fori_loop(begin, end, score, (lowest,) * heads)

    def weigh(i, carry):
        at = pl.ds(pl.multiple_of(i * BLOCK, BLOCK), BLOCK)
        out = []
        for h in range(heads):
            total, mixed = carry[h]
            p = jnp.exp(scores[h, at, :] - tops[h])
            total = total + jnp.sum(p, axis=0, keepdims=True)
            mixed = mixed + jnp.dot(
                value_t[h * HEAD_DIM : (h + 1) * HEAD_DIM, at], p.astype(jnp.bfloat16), preferred_element_type=jnp.float32
            )
            out.append((total, mixed))
        return tuple(out)

    start = (jnp.zeros((1, size), jnp.float32), jnp.zeros((HEAD_DIM, size), jnp.float32))
    sums = lax.fori_loop(begin, end, weigh, (start,) * heads)
    mixed = jnp.concatenate([sums[h][1] / sums[h][0] for h in range(heads)], axis=0).T.astype(jnp.bfloat16)
    relative = jnp.bitwise_xor(block, info_ref[0])
    for r, out in enumerate((out0, out1, out2, out3)):

        @pl.when(relative == r)
        def _():
            out[...] = mixed

    for h in range(heads):
        log_ref[h : h + 1, here] = tops[h] + jnp.log(sums[h][0])


def backward_kernel(
    count, info_ref, range_ref, qkv_ref, grad0, grad1, grad2, grad3, log_ref, cos_ref, sin_ref, here_ref, away_ref,
    x_ref, out_ref, part0, part1, part2, part3, sums_ref, key_t, key_sum, value_sum, probs,
    grads, grad_ref, total_ref
):
    block = pl.program_id(0)
    _, frames, columns = qkv_ref.shape
    size = grad0.shape[0]
    pairs = columns // 128
    heads = 2 * pairs

    @pl.when(block == 0)
    def _():
        key_sum[...] = jnp.zeros_like(key_sum)
        value_sum[...] = jnp.zeros_like(value_sum)

        def rows(i, carry):
            at = pl.ds(pl.multiple_of(i * BLOCK, BLOCK), BLOCK)
            key_t[:, at] = qkv_ref[1, at, :].T
            return carry

        lax.fori_loop(0, frames // BLOCK, rows, 0)

    here = pl.ds(pl.multiple_of(block * size, 128), size)
    relative = jnp.bitwise_xor(block, info_ref[0])
    for r, piece in enumerate((grad0, grad1, grad2, grad3)):

        @pl.when(relative == r)
        def _():
            grad_ref[...] = piece[...]

    upper_t = lax.broadcasted_iota(jnp.int32, (128, size), 0) < HEAD_DIM
    upper = lax.broadcasted_iota(jnp.int32, (size, 128), 1) < HEAD_DIM
    zero_t, zero = jnp.zeros((128, size), jnp.bfloat16), jnp.zeros((size, 128), jnp.bfloat16)
    query_ts, grad_ts, queries, grad_heads = [], [], [], []
    for p in range(pairs):
        query = qkv_ref[0, here, 128 * p : 128 * p + 128]
        grad = grad_ref[:, 128 * p : 128 * p + 128]
        query_t, grad_t = query.T, grad.T
        query_ts += [jnp.where(upper_t, query_t, zero_t), jnp.where(upper_t, zero_t, query_t)]
        grad_ts += [jnp.where(upper_t, grad_t, zero_t), jnp.where(upper_t, zero_t, grad_t)]
        queries += [jnp.where(upper, query, zero), jnp.where(upper, zero, query)]
        grad_heads += [jnp.where(upper, grad, zero), jnp.where(upper, zero, grad)]
    own = utterance_of(lax.broadcasted_iota(jnp.int32, (1, size), 1) + block * size, info_ref, count)
    begin, end = range_ref[0, block], range_ref[1, block]
    logs = [log_ref[h : h + 1, here] for h in range(heads)]

    def first(i, deltas):
        at = pl.ds(pl.multiple_of(i * BLOCK, BLOCK), BLOCK)
        theirs = utterance_of(lax.broadcasted_iota(jnp.int32, (BLOCK, 1), 0) + i * BLOCK, info_ref, count)
        same = theirs == own
        out = []
        for h in range(heads):
            lanes = slice(128 * (h // 2), 128 * (h // 2) + 128)
            s = jnp.dot(qkv_ref[1, at, lanes], query_ts[h], preferred_element_type=jnp.float32)
            p = jnp.exp(jnp.where(same, s, -1e30) - logs[h])
            g = jnp.dot(qkv_ref[2, at, lanes], grad_ts[h], preferred_element_type=jnp.float32)
            probs[h, at, :] = p
            grads[h, at, :] = g
            out.append(deltas[h] + jnp.sum(p * g, axis=0, keepdims=True))
        return tuple(out)

    none = jnp.zeros((1, size), jnp.float32)
    deltas = lax.fori_loop(begin, end, first, (none,) * heads)

    def second(i, sums):
        at = pl.ds(pl.multiple_of(i * BLOCK, BLOCK), BLOCK)
        out = []
        for p in range(pairs):
            lanes = slice(128 * p, 128 * p + 128)
            key_add, value_add = key_sum[at, lanes], value_sum[at, lanes]
            for h in (2 * p, 2 * p + 1):
                weight = probs[h, at, :]
                ds = (weight * (grads[h, at, :] - deltas[h])).astype(jnp.bfloat16)
                out.append(
                    sums[h]
                    + jnp.dot(key_t[h * HEAD_DIM : (h + 1) * HEAD_DIM, at], ds, preferred_element_type=jnp.float32)
                )
                key_add = key_add + jnp.dot(ds, queries[h], preferred_element_type=jnp.float32)
                value_add = value_add + jnp.dot(
                    weight.astype(jnp.bfloat16), grad_heads[h], preferred_element_type=jnp.float32
                )
            key_sum[at, lanes] = key_add
            value_sum[at, lanes] = value_add
        return tuple(out)

    zero_sum = jnp.zeros((HEAD_DIM, size), jnp.float32)
    sums = lax.fori_loop(begin, end, second, (zero_sum,) * heads)
    grad_query = jnp.concatenate(sums, axis=0).T * 0.125
    for p in range(pairs):
        lanes = slice(128 * p, 128 * p + 128)
        out_ref[0, here, lanes] = turn(grad_query[:, lanes], cos_ref[here, :], -sin_ref[here, :]).astype(jnp.bfloat16)

    @pl.when(block == pl.num_programs(0) - 1)
    def _():
        def rows(i, carry):
            at = pl.ds(pl.multiple_of(i * BLOCK, BLOCK), BLOCK)
            for p in range(pairs):
                lanes = slice(128 * p, 128 * p + 128)
                out_ref[1, at, lanes] = turn(key_sum[at, lanes], cos_ref[at, :], -sin_ref[at, :]).astype(jnp.bfloat16)
            out_ref[2, at, :] = value_sum[at, :].astype(jnp.bfloat16)
            return carry

        lax.fori_loop(0, frames // BLOCK, rows, 0)
        depth = here_ref.shape[1]
        chunk = 64
        sums_ref[...] = jnp.zeros_like(sums_ref)
        for r, part in enumerate((part0, part1, part2, part3)):
            base = jnp.bitwise_xor(info_ref[0], r) * size
            at = pl.ds(pl.multiple_of(base, 128), size)
            for side, weight in ((info_ref[1], here_ref), (1 - info_ref[1], away_ref)):
                total = dot_rows(out_ref[0, at, :], weight[0])
                for c in (1, 2):
                    total = total + dot_rows(out_ref[c, at, :], weight[c])
                total_ref[:, pl.ds(pl.multiple_of(side * depth, 128), depth)] = total

            def add(own, first):
                start = base + first
                grad_in = total_ref[own, :]
                part[own, :] = grad_in.astype(part.dtype)
                normed, _ = spread(x_ref[pl.ds(pl.multiple_of(start, chunk), chunk), :].astype(jnp.float32))
                index = lax.broadcasted_iota(jnp.int32, (chunk, 1), 0) + start
                for u in range(count):
                    begin = info_ref[BOUNDS + u - 1] if u else 0
                    end = info_ref[BOUNDS + u]

                    @pl.when((begin < start + chunk) & (end > start))
                    def _():
                        chosen = jnp.where((index >= begin) & (index < end), grad_in, 0.0)
                        sums_ref[0, u : u + 1, :] += jnp.sum(chosen, axis=0, keepdims=True)
                        sums_ref[1, u : u + 1, :] += jnp.sum(chosen * normed, axis=0, keepdims=True)

            over_rows(size, chunk, add)


def key_ranges(ending, frames, size):
    starting = jnp.concatenate([jnp.zeros((1,), jnp.int32), ending[:-1]])
    begins = jnp.arange(frames // size, dtype=jnp.int32) * size
    first_key = jnp.min(jnp.where(ending[None, :] > begins[:, None], starting[None, :], frames), axis=1)
    last_key = jnp.max(jnp.where(starting[None, :] < begins[:, None] + size, ending[None, :], 0), axis=1)
    return jnp.stack([first_key // BLOCK, (last_key + BLOCK - 1) // BLOCK]).astype(jnp.int32)


def attend(info, ranges, qkv, count):
    _, frames, columns = qkv.shape
    heads = columns // HEAD_DIM
    size = frames // 4
    flat = lambda b, *_: (0, 0)
    return pl.pallas_call(
        partial(forward_kernel, count),
        grid_spec=pltpu.PrefetchScalarGridSpec(
            num_scalar_prefetch=2,
            grid=(4,),
            in_specs=[pl.BlockSpec((3, frames, columns), lambda b, *_: (0, 0, 0))],
            out_specs=[pl.BlockSpec((size, columns), flat)] * 4 + [pl.BlockSpec((heads, frames), flat)],
            scratch_shapes=[
                pltpu.VMEM((columns, frames), jnp.bfloat16),
                pltpu.VMEM((heads, frames, size), jnp.float32),
            ],
        ),
        out_shape=[jax.ShapeDtypeStruct((size, columns), jnp.bfloat16)] * 4
        + [jax.ShapeDtypeStruct((heads, frames), jnp.float32)],
        cost_estimate=pl.CostEstimate(
            flops=8 * frames * frames * columns, transcendentals=heads * frames * frames, bytes_accessed=frames * columns * 8
        ),
        name="attend",
    )(info, ranges, qkv)


def attend_back(info, ranges, qkv, grad_pieces, logs, cosine, sine, here, away, features_full, count):
    _, frames, columns = qkv.shape
    model_width = features_full.shape[1]
    heads = columns // HEAD_DIM
    size = frames // 4
    cube = lambda b, *_: (0, 0, 0)
    flat = lambda b, *_: (0, 0)
    return pl.pallas_call(
        partial(backward_kernel, count),
        grid_spec=pltpu.PrefetchScalarGridSpec(
            num_scalar_prefetch=2,
            grid=(4,),
            in_specs=[pl.BlockSpec((3, frames, columns), cube)]
            + [pl.BlockSpec((size, columns), flat)] * 4
            + [pl.BlockSpec((heads, frames), flat), pl.BlockSpec((frames, 128), flat), pl.BlockSpec((frames, 128), flat)]
            + [whole(here), whole(away), whole(features_full)],
            out_specs=[pl.BlockSpec((3, frames, columns), cube)]
            + [pl.BlockSpec((size, model_width), flat)] * 4
            + [pl.BlockSpec((2, 8, model_width), cube)],
            scratch_shapes=[
                pltpu.VMEM((columns, frames), jnp.bfloat16),
                pltpu.VMEM((frames, columns), jnp.float32),
                pltpu.VMEM((frames, columns), jnp.float32),
                pltpu.VMEM((heads, frames, size), jnp.float32),
                pltpu.VMEM((heads, frames, size), jnp.float32),
                pltpu.VMEM((size, columns), jnp.bfloat16),
                pltpu.VMEM((size, model_width), jnp.float32),
            ],
        ),
        out_shape=[jax.ShapeDtypeStruct((3, frames, columns), jnp.bfloat16)]
        + [jax.ShapeDtypeStruct((size, model_width), jnp.bfloat16 if r else jnp.float32) for r in range(4)]
        + [jax.ShapeDtypeStruct((2, 8, model_width), jnp.float32)],
        cost_estimate=pl.CostEstimate(
            flops=16 * frames * frames * columns, transcendentals=heads * frames * frames, bytes_accessed=frames * columns * 20
        ),
        name="attend_back",
    )(info, ranges, qkv, *grad_pieces, logs, cosine, sine, here, away, features_full)


def middle_kernel(
    count, info_ref, x_ref, cot_ref, mixed0, mixed1, mixed2, mixed3, mod_ref, *refs
):
    pieces = refs[:10]
    out_ref, res_ref, g0, g1, g2, g3, sums_ref, ffn_in_ref, hidden_ref, grad_up_ref, grad_attn_ref, grad_ffn_ref = refs[10:22]
    mixed, wide, residual, attn, up, ffn, inverse, sems = refs[22:]
    me, core, group = info_ref[0], info_ref[1], info_ref[2]
    size = x_ref.shape[0]
    width = mixed0.shape[1]
    quarter = pieces[0].shape[2]
    depth = 4 * quarter

    copies = ([], [])
    for side in range(2):
        half = core if side == 0 else 1 - core
        for k, r in [(k, r) for k in range(4) for r in range(4)]:
            if k < 3:
                piece = pieces[5 * side + k].at[r]
            else:
                piece = pieces[5 * side + 3 + r // 2].at[r % 2]
            at = pl.ds(pl.multiple_of(half * depth + jnp.bitwise_xor(group, k) * quarter, 16), quarter)
            lanes = pl.ds(pl.multiple_of(jnp.bitwise_xor(me, r) * width, 128), width)
            for part, cs in enumerate((slice(0, 1), slice(1, 5))):
                copy = pltpu.make_async_copy(
                    piece.at[cs], wide.at[cs, at, lanes], sems.at[part * 32 + side * 16 + k * 4 + r]
                )
                copies[part].append(copy)
    for copy in copies[0] + copies[1]:
        copy.start()
    for r, piece in enumerate((mixed0, mixed1, mixed2, mixed3)):
        mixed[:, r * width : (r + 1) * width] = piece[...]
    chunk = 64

    def table(c, number):
        return by_utterance(number, mod_ref[c, 0:count, :])

    def numbers(first):
        return utterance_of(lax.broadcasted_iota(jnp.int32, (chunk, 1), 0) + me * size + first, info_ref, count)

    for copy in copies[0]:
        copy.wait()
    attn[...] = dot_rows(mixed[...], wide[0])

    def enter(at, first):
        number = numbers(first)
        value = x_ref[at, :].astype(jnp.float32) + table(2, number) * attn[at, :]
        residual[at, :] = value
        normed, scale = spread(value)
        inverse[at, :] = jnp.broadcast_to(scale, (chunk, 128))
        ffn[at, :] = normed
        ffn_in_ref[at, :] = (normed * (1.0 + table(4, number)) + table(3, number)).astype(jnp.bfloat16)
        grad_ffn_ref[at, :] = (cot_ref[at, :].astype(jnp.float32) * table(5, number)).astype(jnp.bfloat16)

    over_rows(size, chunk, enter)
    for copy in copies[1]:
        copy.wait()
    for c in range(2):
        up[c] = dot(ffn_in_ref[...], wide[3 + c])

    root = math.sqrt(2.0 / math.pi)

    def act(at, first):
        for c in range(2):
            value = up[c, at, :]
            square = value * value
            bend = jnp.tanh(root * (value + 0.044715 * (value * square)))
            hidden_ref[c, at, :] = (0.5 * value * (1.0 + bend)).astype(jnp.bfloat16)
            up[c, at, :] = 0.5 * (1.0 + bend) + 0.5 * value * (1.0 - bend * bend) * (root * (1.0 + 0.134145 * square))

    over_rows(size, chunk, act)
    grad_hidden = [dot(grad_ffn_ref[...], wide[1 + c]) for c in range(2)]
    for c in range(2):
        grad_up_ref[c] = (up[c] * grad_hidden[c]).astype(jnp.bfloat16)
    up[0] = dot_rows(hidden_ref[0], wide[1]) + dot_rows(hidden_ref[1], wide[2])
    up[1] = dot_rows(grad_up_ref[0], wide[3]) + dot_rows(grad_up_ref[1], wide[4])
    sums_ref[...] = jnp.zeros_like(sums_ref)

    def leave(at, first):
        number = numbers(first)
        cot = cot_ref[at, :].astype(jnp.float32)
        ffn_out, grad_in, normed = up[0, at, :], up[1, at, :], ffn[at, :]
        out_ref[at, :] = (residual[at, :] + table(5, number) * ffn_out).astype(jnp.bfloat16)
        h = grad_in * (1.0 + table(4, number))
        grad = cot + inverse[at, 0:1] * (
            h - jnp.mean(h, axis=-1, keepdims=True) - normed * jnp.mean(h * normed, axis=-1, keepdims=True)
        )
        res_ref[at, :] = grad
        grad_attn_ref[at, :] = (grad * table(2, number)).astype(jnp.bfloat16)
        for c, rows in enumerate((grad * attn[at, :], grad_in, grad_in * normed, cot * ffn_out)):
            for u in range(count):
                sums_ref[c, u : u + 1, :] += jnp.sum(jnp.where(number == u, rows, 0.0), axis=0, keepdims=True)

    over_rows(size, chunk, leave)
    grad_mixed = dot(grad_attn_ref[...], wide[0]).astype(jnp.bfloat16)
    for r, piece in enumerate((g0, g1, g2, g3)):
        piece[...] = grad_mixed[:, r * width : (r + 1) * width]


def middle(info, features, cotangent, mixed_pieces, modulation, wide_here, wide_away, count):
    size, model_width = features.shape
    width = mixed_pieces[0].shape[1]
    pieces = (*wide_here, *wide_away)
    shapes = [
        ((size, model_width), jnp.bfloat16),
        ((size, model_width), jnp.float32),
        *[((size, width), jnp.bfloat16)] * 4,
        ((4, 8, model_width), jnp.float32),
        ((size, model_width), jnp.bfloat16),
        ((2, size, 4 * width), jnp.bfloat16),
        ((2, size, 4 * width), jnp.bfloat16),
        ((size, model_width), jnp.bfloat16),
        ((size, model_width), jnp.bfloat16),
        ((size, 4 * width), jnp.bfloat16),
    ]
    outs = [jax.ShapeDtypeStruct(shape, kind) for shape, kind in shapes]
    return pl.pallas_call(
        partial(middle_kernel, count),
        grid_spec=pltpu.PrefetchScalarGridSpec(
            num_scalar_prefetch=1,
            grid=(1,),
            in_specs=[whole(a) for a in (features, cotangent, *mixed_pieces, modulation)]
            + [pl.BlockSpec(memory_space=pl.ANY)] * 10,
            out_specs=[whole(a) for a in outs],
            scratch_shapes=[
                pltpu.VMEM((5, model_width, 4 * width), jnp.bfloat16),
                pltpu.VMEM((size, model_width), jnp.float32),
                pltpu.VMEM((size, model_width), jnp.float32),
                pltpu.VMEM((2, size, 4 * width), jnp.float32),
                pltpu.VMEM((size, model_width), jnp.float32),
                pltpu.VMEM((size, 128), jnp.float32),
                pltpu.SemaphoreType.DMA((64,)),
            ],
        ),
        out_shape=outs,
        cost_estimate=pl.CostEstimate(
            flops=20 * size * model_width * 4 * width, transcendentals=size * 8 * width, bytes_accessed=10 * model_width * 4 * width
        ),
        name="middle",
    )(info, features, cotangent, *mixed_pieces, modulation, *pieces)


def wide_grad_kernel(side, summed, info_ref, mixed_ref, hidden_ref, grad_up_ref, *refs):
    grad_refs, other_ref, out_ref, turned = refs[:3], refs[3] if summed else None, refs[-2], refs[-1]
    depth = out_ref.shape[2]
    half = info_ref[1] if side == 0 else 1 - info_ref[1]

    @pl.when(pl.program_id(0) == 0)
    def _():
        at = pl.ds(pl.multiple_of(half * depth, 128), depth)
        for i in range(3):
            turned[i] = grad_refs[i][:, at].T

    def block(c):
        if c == 0:
            return dot(turned[0], mixed_ref[...])
        if c < 3:
            return dot(turned[1], hidden_ref[c - 1])
        return dot(turned[2], grad_up_ref[c - 3])

    for c in range(5):
        value = block(c)
        if summed:
            value = value + other_ref[0, c].astype(jnp.float32)
        out_ref[0, c] = value.astype(jnp.bfloat16)


def wide_grads(info, side, mixed, hidden, grad_up, grad_attn, grad_ffn, ffn_in, other=None):
    size, width = mixed.shape[0], mixed.shape[1] // 4
    depth = grad_attn.shape[1] // 2
    lanes = lambda r, info: (0, 0, r)
    target = pl.BlockSpec((1, 5, depth, width), lambda r, info: (jnp.bitwise_xor(info[0], r), 0, 0, 0))
    return pl.pallas_call(
        partial(wide_grad_kernel, side, other is not None),
        grid_spec=pltpu.PrefetchScalarGridSpec(
            num_scalar_prefetch=1,
            grid=(4,),
            in_specs=[
                pl.BlockSpec((size, width), lambda r, info: (0, r)),
                pl.BlockSpec((2, size, width), lanes),
                pl.BlockSpec((2, size, width), lanes),
                whole(grad_attn),
                whole(grad_ffn),
                whole(ffn_in),
            ]
            + ([target] if other is not None else []),
            out_specs=target,
            scratch_shapes=[pltpu.VMEM((3, depth, size), jnp.bfloat16)],
        ),
        out_shape=jax.ShapeDtypeStruct((4, 5, depth, width), jnp.bfloat16),
        cost_estimate=pl.CostEstimate(
            flops=40 * size * depth * width, transcendentals=0, bytes_accessed=60 * depth * width
        ),
        name="wide_grads",
    )(info, mixed, hidden, grad_up, grad_attn, grad_ffn, ffn_in, *([other] if other is not None else []))


def qkv_grad_kernel(side, summed, info_ref, grad_ref, att_ref, *refs):
    other_ref, out_ref, turned = refs[0] if summed else None, refs[-2], refs[-1]
    depth = out_ref.shape[1]
    half = info_ref[1] if side == 0 else 1 - info_ref[1]

    @pl.when(pl.program_id(0) == 0)
    def _():
        turned[...] = att_ref[:, pl.ds(pl.multiple_of(half * depth, 128), depth)].T

    value = dot(turned[...], grad_ref[0])
    if summed:
        value = value + other_ref[0].astype(jnp.float32)
    out_ref[0] = value.astype(out_ref.dtype)


def qkv_grads(info, side, gradients, att_full, other=None, kind=jnp.bfloat16):
    _, frames, columns = gradients.shape
    depth = att_full.shape[1] // 2
    target = pl.BlockSpec((1, depth, columns), lambda c, *_: (c, 0, 0))
    return pl.pallas_call(
        partial(qkv_grad_kernel, side, other is not None),
        grid_spec=pltpu.PrefetchScalarGridSpec(
            num_scalar_prefetch=1,
            grid=(3,),
            in_specs=[pl.BlockSpec((1, frames, columns), lambda c, *_: (c, 0, 0)), whole(att_full)]
            + ([target] if other is not None else []),
            out_specs=target,
            scratch_shapes=[pltpu.VMEM((depth, frames), jnp.bfloat16)],
        ),
        out_shape=jax.ShapeDtypeStruct((3, depth, columns), kind),
        cost_estimate=pl.CostEstimate(
            flops=6 * frames * depth * columns, transcendentals=0, bytes_accessed=frames * depth * 6
        ),
        name="qkv_grads",
    )(info, gradients, att_full, *([other] if other is not None else []))


def inner_step(grads, first, second, weights, steps_done):
    first_new = beta_first * first + (1.0 - beta_first) * grads
    second_new = beta_second * second + (1.0 - beta_second) * grads * grads
    correct_one = 1.0 - beta_first**steps_done
    correct_two = 1.0 - beta_second**steps_done
    difference = inner_rate * (
        first_new / correct_one / (jnp.sqrt(second_new / correct_two) + adam_epsilon)
        + weight_decay * weights
    )
    return (first_new[None], second_new[None], difference)


def outer_step(average, outer, weights):
    outer_new = outer_beta * outer + average
    return (outer_new, weights - outer_rate * (average + outer_beta * outer_new))


def swapped(values, axis, bits):
    size = lax.axis_size(axis)
    return lax.ppermute(values, axis, [(i, i ^ bits) for i in range(size)])


def exchange(blocks, axis="tensor"):
    return [blocks[0]] + [swapped(blocks[r], axis, r) for r in range(1, 4)]


def after(values, *others):
    return lax.optimization_barrier((values, *others))[0]


def dp_rows(own):
    if lax.axis_size("dp") != 2:
        return lax.all_gather(own, "dp", axis=0, tiled=True)
    other = swapped(own, "dp", 1)
    first = lax.axis_index("dp") == 0
    return jnp.concatenate([jnp.where(first, own, other), jnp.where(first, other, own)], axis=0)


def dp_pair(own):
    if lax.axis_size("dp") == 2:
        return own, swapped(own, "dp", 1)
    return tuple(jnp.split(lax.all_gather(own, "dp", axis=1, tiled=True), 2, axis=1))


def quarter_of(half):
    quarter = half.shape[1] // 4
    return lax.dynamic_slice_in_dim(half, lax.axis_index("group") * quarter, quarter, 1)


def spread_wide(stack):
    one, two = swapped(stack, "group", 1), swapped(stack, "group", 2)
    return [stack, one, two, swapped(one[:2], "group", 2), swapped(two[2:], "group", 1)]


def group_parts(values):
    group = lax.axis_index("group")
    quarter = values.shape[1] // 4
    parts = exchange([lax.dynamic_slice_in_dim(values, (group ^ r) * quarter, quarter, 1) for r in range(4)], "group")
    return sum(part.astype(jnp.float32) for part in parts).astype(low)


def group_whole(total):
    group = lax.axis_index("group")
    quarter = total.shape[1]
    out = jnp.zeros((total.shape[0], 4 * quarter, total.shape[2]), total.dtype)
    for r, part in enumerate(exchange([total] * 4, "group")):
        out = lax.dynamic_update_slice_in_dim(out, part, (group ^ r) * quarter, 1)
    return out


def per_device(
    features,
    cotangent,
    frame_counts,
    buckets,
    step_count,
    col_weights,
    mod_weights,
    row_weights,
    col_first,
    col_second,
    mod_first,
    mod_second,
    row_first,
    row_second,
    col_outer,
    mod_outer,
    row_outer,
):
    group_count = lax.axis_size("group")
    packs_here = lax.axis_size("dp")
    own_rows, model_width = features.shape
    frames = own_rows * 4
    me = lax.axis_index("tensor")
    core = lax.axis_index("dp")
    group = lax.axis_index("group")
    count = buckets.shape[1]
    share = mod_weights.shape[0]
    width = col_weights.shape[2]

    def columns_first(values):
        return jnp.swapaxes(values, -3, -2)

    col_major = columns_first(col_weights).astype(low)
    wide_low = jnp.concatenate([row_weights.astype(low), col_major[3:5]], axis=0)
    halves = [wide_low] if packs_here == 2 else list(dp_pair(wide_low))
    stacks = [lax.all_gather(quarter_of(half), "tensor", axis=0) for half in halves]
    features_full = lax.all_gather(after(features, *stacks), "tensor", axis=0, tiled=True)

    buckets_all = dp_rows(buckets[0])
    flow_time = ((group * NBUCK + buckets_all).astype(jnp.float32) + 0.5) / (NBUCK * group_count)
    condition_all = jax.nn.silu(time_embedding(flow_time, model_width)).astype(low)
    condition_here = lax.dynamic_slice_in_dim(condition_all, core * share, share, 1)
    mod_terms = jnp.einsum("ud,dcj->cuj", condition_here, mod_weights.astype(low), preferred_element_type=jnp.float32)
    if packs_here != 2:
        mod_part = lax.psum_scatter(mod_terms, "dp", scatter_dimension=1, tiled=True)
    else:
        mod_away = lax.dynamic_slice_in_dim(mod_terms, (1 - core) * count, count, 1)
        mod_part = lax.dynamic_slice_in_dim(mod_terms, core * count, count, 1) + swapped(mod_away, "dp", 1)
    mod_pieces = exchange([mod_part] * 4)

    ending = jnp.cumsum(frame_counts[0]).astype(jnp.int32)
    half_core = core if packs_here == 2 else jnp.zeros_like(core)
    info = jnp.concatenate([jnp.stack([me, half_core, group]).astype(jnp.int32), ending])
    _, position = utterance_rows(ending, jnp.arange(frames, dtype=jnp.int32))
    cosine, sine = rotary_tables(position)
    ranges = key_ranges(ending, frames, own_rows)
    qkv_here, qkv_away = dp_pair(col_major[0:3])
    wide_sets = [spread_wide(stack) for stack in stacks]
    if packs_here == 2:
        wide_sets.append([swapped(piece, "dp", 1) for piece in wide_sets[0]])

    att_full, qkv, modulation = project(info, features_full, mod_pieces, qkv_here, qkv_away, cosine, sine)
    *mixed_pieces, log_totals = attend(info, ranges, qkv, count)
    mixed_pieces = exchange(mixed_pieces)

    (output, grad_residual, g0, g1, g2, g3, late_sums, ffn_in, hidden, grad_up, grad_attn, grad_ffn, mixed) = middle(
        info, features, cotangent, mixed_pieces, modulation, *wide_sets, count
    )
    grad_pieces = exchange([g0, g1, g2, g3])
    wide_args = (mixed, hidden, grad_up, grad_attn, grad_ffn, ffn_in)
    if packs_here == 2:
        wide_away_grad = after(swapped(wide_grads(info, 1, *wide_args), "dp", 1), *grad_pieces)
        wide_blocks = wide_grads(info, 0, *wide_args, other=wide_away_grad)
    else:
        both = jnp.concatenate([wide_grads(info, side, *wide_args) for side in range(2)], axis=2).astype(jnp.float32)
        wide_blocks = lax.psum_scatter(both, "dp", scatter_dimension=2, tiled=True).astype(low)
    wide_grad = lax.psum_scatter(wide_blocks, "tensor", scatter_dimension=0, tiled=False)

    gradients, *att_parts, early_sums = attend_back(
        info, ranges, qkv, grad_pieces, log_totals, cosine, sine, qkv_here, qkv_away, features_full, count
    )
    sums = jnp.concatenate([early_sums[:, :count], late_sums[:, :count]], axis=0)
    mine = [lax.dynamic_slice_in_dim(sums, (me ^ r) * width, width, 2) for r in range(4)]
    columns = sum(exchange(mine))
    own_part, *away_parts = att_parts
    away_parts = lax.optimization_barrier((*away_parts, columns))[:3]
    att_parts = exchange([own_part, *away_parts])
    columns = dp_rows(jnp.swapaxes(columns, 0, 1))
    if packs_here != 2:
        mod_grad = jnp.einsum("ud,ucj->cdj", condition_here.astype(jnp.float32), columns, precision=highest)
    else:
        mod_grad = 0.0
        for u in range(columns.shape[0]):
            mod_grad = mod_grad + condition_here[u].astype(jnp.float32)[None, :, None] * columns[u][:, None, :]
    if packs_here == 2:
        qkv_away_grad = swapped(qkv_grads(info, 1, gradients, att_full), "dp", 1)
        qkv_share = qkv_grads(info, 0, gradients, att_full, other=qkv_away_grad, kind=jnp.float32)
    else:
        both = [qkv_grads(info, side, gradients, att_full, kind=jnp.float32) for side in range(2)]
        qkv_share = lax.psum_scatter(jnp.concatenate(both, axis=1), "dp", scatter_dimension=1, tiled=True)

    steps_done = step_count[0].astype(jnp.float32)
    mod_first_new, mod_second_new, mod_diff = inner_step(
        columns_first(mod_grad), mod_first[0], mod_second[0], mod_weights, steps_done
    )
    _, _, qkv_diff = inner_step(
        qkv_share,
        columns_first(col_first[0])[0:3],
        columns_first(col_second[0])[0:3],
        columns_first(col_weights)[0:3],
        steps_done,
    )
    early_total = group_parts(jnp.concatenate([qkv_diff.astype(low), columns_first(mod_diff).astype(low)], axis=0))
    wide_grad = after(wide_grad, early_total).astype(jnp.float32)
    early_averages = group_whole(early_total).astype(jnp.float32) / group_count
    row_first_new, row_second_new, row_diff = inner_step(
        wide_grad[0:3], row_first[0], row_second[0], row_weights, steps_done
    )
    col_first_new, col_second_new, col_diff = inner_step(
        columns_first(jnp.concatenate([qkv_share, wide_grad[3:5]], axis=0)), col_first[0], col_second[0], col_weights, steps_done
    )
    late_total = group_parts(jnp.concatenate([row_diff.astype(low), columns_first(col_diff)[3:5].astype(low)], axis=0))
    late_averages = group_whole(late_total).astype(jnp.float32) / group_count

    att_parts = lax.optimization_barrier((*att_parts, late_total))[:4]
    grad_att_in = sum(part.astype(jnp.float32) for part in att_parts)
    number_own, _ = utterance_rows(ending, me * own_rows + jnp.arange(own_rows, dtype=jnp.int32))
    normed, inverse_scale = normalize(features.astype(jnp.float32))
    grad_features = grad_residual + normalize_back(
        grad_att_in * (1.0 + by_utterance(number_own[:, None], modulation[1, :count])), normed, inverse_scale
    )

    row_average, mod_average = late_averages[0:3], columns_first(early_averages[3:9])
    col_average = columns_first(jnp.concatenate([early_averages[0:3], late_averages[3:5]], axis=0))
    col_outer_new, col_new = outer_step(col_average, col_outer, col_weights)
    mod_outer_new, mod_new = outer_step(mod_average, mod_outer, mod_weights)
    row_outer_new, row_new = outer_step(row_average, row_outer, row_weights)
    return (
        output,
        grad_features,
        col_first_new,
        col_second_new,
        col_average,
        col_outer_new,
        col_new,
        mod_first_new,
        mod_second_new,
        mod_average,
        mod_outer_new,
        mod_new,
        row_first_new,
        row_second_new,
        row_average,
        row_outer_new,
        row_new,
    )


def solution(mesh):
    placed = (
        P(("group", "dp", "tensor"), None),
        P(("group", "dp", "tensor"), None),
        P(("group", "dp"), None),
        P(("group", "dp"), None),
        P(),
        P("dp", None, "tensor"),
        P("dp", None, "tensor"),
        P(None, "dp", "tensor"),
        P("group", "dp", None, "tensor"),
        P("group", "dp", None, "tensor"),
        P("group", "dp", None, "tensor"),
        P("group", "dp", None, "tensor"),
        P("group", None, "dp", "tensor"),
        P("group", None, "dp", "tensor"),
        P("dp", None, "tensor"),
        P("dp", None, "tensor"),
        P(None, "dp", "tensor"),
    )
    return jax.shard_map(
        per_device,
        mesh=mesh,
        in_specs=placed,
        out_specs=(
            P(("group", "dp", "tensor"), None),
            P(("group", "dp", "tensor"), None),
            P("group", "dp", None, "tensor"),
            P("group", "dp", None, "tensor"),
            P("dp", None, "tensor"),
            P("dp", None, "tensor"),
            P("dp", None, "tensor"),
            P("group", "dp", None, "tensor"),
            P("group", "dp", None, "tensor"),
            P("dp", None, "tensor"),
            P("dp", None, "tensor"),
            P("dp", None, "tensor"),
            P("group", None, "dp", "tensor"),
            P("group", None, "dp", "tensor"),
            P(None, "dp", "tensor"),
            P(None, "dp", "tensor"),
            P(None, "dp", "tensor"),
        ),
        check_vma=False,
    )
```

```python
from functools import partial
import math

import jax
import jax.numpy as jnp
from jax import lax
from jax.experimental import pallas as pl
from jax.experimental.pallas import tpu as pltpu
from jax.sharding import PartitionSpec as P

HEAD_DIM = 64
NBUCK = 8
BLOCK = 256
BOUNDS = 3

highest = lax.Precision.HIGHEST
norm_epsilon = 1e-06
adam_epsilon = 1e-08
beta_first = 0.9
beta_second = 0.999
inner_rate = 0.05
weight_decay = 0.01
outer_rate = 0.7
outer_beta = 0.9
low = jnp.bfloat16


def time_embedding(flow_time, width_all):
    half_width = width_all // 2
    frequency = jnp.exp(
        jnp.arange(half_width, dtype=jnp.float32) * (-math.log(10000.0) / (half_width - 1))
    )
    angles = 1000.0 * flow_time[:, None] * frequency[None, :]
    return jnp.concatenate([jnp.sin(angles), jnp.cos(angles)], axis=1)


def utterance_rows(ending, indices):
    number = jnp.zeros(indices.shape, jnp.int32)
    begin = jnp.zeros(indices.shape, jnp.int32)
    for u in range(ending.shape[0] - 1):
        after = indices >= ending[u]
        number = number + after.astype(jnp.int32)
        begin = jnp.where(after, ending[u], begin)
    return number, indices - begin


def rotary_tables(position):
    half_width = HEAD_DIM // 2
    frequency = jnp.exp(
        jnp.arange(half_width, dtype=jnp.float32) * (-2.0 * math.log(10000.0) / HEAD_DIM)
    )
    angles = position.astype(jnp.float32)[:, None] * frequency[None, :]
    cosine, sine = jnp.cos(angles), jnp.sin(angles)
    return jnp.concatenate([cosine] * 4, axis=1), jnp.concatenate([-sine, sine, -sine, sine], axis=1)


def normalize(values):
    centered = values - jnp.mean(values, axis=-1, keepdims=True)
    inverse_scale = lax.rsqrt(jnp.mean(centered * centered, axis=-1, keepdims=True) + norm_epsilon)
    return (centered * inverse_scale, inverse_scale)


def normalize_back(grads, normed, inverse_scale):
    return inverse_scale * (
        grads
        - jnp.mean(grads, axis=-1, keepdims=True)
        - normed * jnp.mean(grads * normed, axis=-1, keepdims=True)
    )


def turn(values, cosine, signed_sine):
    lanes = lax.broadcasted_iota(jnp.int32, values.shape, 1)
    swapped = jnp.where(lanes % 64 < 32, pltpu.roll(values, 96, 1), pltpu.roll(values, 32, 1))
    return values * cosine + swapped * signed_sine


def utterance_of(indices, info_ref, count):
    number = jnp.zeros(indices.shape, jnp.int32)
    for u in range(count - 1):
        number = number + (indices >= info_ref[BOUNDS + u]).astype(jnp.int32)
    return number


def by_utterance(number, table):
    out = table[0:1, :]
    for u in range(1, table.shape[0]):
        out = jnp.where(number >= u, table[u : u + 1, :], out)
    return out


def dot_rows(a, b):
    return lax.dot_general(a, b, (((1,), (1,)), ((), ())), preferred_element_type=jnp.float32)


def dot(a, b):
    return jnp.dot(a, b, preferred_element_type=jnp.float32)


def spread(values):
    centered = values - jnp.mean(values, axis=-1, keepdims=True)
    inverse = lax.rsqrt(jnp.mean(centered * centered, axis=-1, keepdims=True) + norm_epsilon)
    return centered * inverse, inverse


def over_rows(total, chunk, body):
    def step(i, carry):
        body(pl.ds(pl.multiple_of(i * chunk, chunk), chunk), i * chunk)
        return carry

    lax.fori_loop(0, total // chunk, step, 0)


def whole(a):
    shape = a.shape
    return pl.BlockSpec(shape, lambda *_: (0,) * len(shape))


def project_kernel(
    count, info_ref, x_ref, m0_ref, m1_ref, m2_ref, m3_ref, here_ref, away_ref, cos_ref, sin_ref, att_ref, qkv_ref, mod_ref
):
    step = pl.program_id(0)
    me, core = info_ref[0], info_ref[1]
    size = x_ref.shape[0]
    width = m0_ref.shape[2]

    @pl.when(step == 0)
    def _():
        mod_ref[...] = jnp.zeros_like(mod_ref)
        for r, piece in enumerate((m0_ref, m1_ref, m2_ref, m3_ref)):
            at = pl.ds(pl.multiple_of(jnp.bitwise_xor(me, r) * width, 128), width)
            mod_ref[:, 0:count, at] = piece[...]

    chunk = 64

    def norm(at, first):
        normed, _ = spread(x_ref[at, :].astype(jnp.float32))
        number = utterance_of(
            lax.broadcasted_iota(jnp.int32, (chunk, 1), 0) + step * size + first, info_ref, count
        )
        shift, scale = by_utterance(number, mod_ref[0, 0:count, :]), by_utterance(number, mod_ref[1, 0:count, :])
        att_ref[at, :] = (normed * (1.0 + scale) + shift).astype(jnp.bfloat16)

    over_rows(size, chunk, norm)
    depth = here_ref.shape[1]
    near = att_ref[:, pl.ds(pl.multiple_of(core * depth, 128), depth)]
    far = att_ref[:, pl.ds(pl.multiple_of((1 - core) * depth, 128), depth)]
    for c in range(3):
        values = dot(near, here_ref[c]) + dot(far, away_ref[c])
        if c < 2:
            for p in range(values.shape[1] // 128):
                lanes = slice(128 * p, 128 * p + 128)
                turned = turn(values[:, lanes], cos_ref[...], sin_ref[...])
                qkv_ref[c, :, lanes] = (turned * 0.125 if c == 0 else turned).astype(jnp.bfloat16)
        else:
            qkv_ref[c] = values.astype(jnp.bfloat16)


def project(info, features_full, mod_pieces, here, away, cosine, sine):
    frames, model_width = features_full.shape
    size = frames // 4
    cycles, count, width = mod_pieces[0].shape
    columns = here.shape[2]
    rows = lambda i, *_: (i, 0)
    return pl.pallas_call(
        partial(project_kernel, count),
        grid_spec=pltpu.PrefetchScalarGridSpec(
            num_scalar_prefetch=1,
            grid=(4,),
            in_specs=[pl.BlockSpec((size, model_width), rows)]
            + [whole(a) for a in (*mod_pieces, here, away)]
            + [pl.BlockSpec((size, 128), rows)] * 2,
            out_specs=[
                pl.BlockSpec((size, model_width), rows),
                pl.BlockSpec((3, size, columns), lambda i, *_: (0, i, 0)),
                pl.BlockSpec((cycles, 8, model_width), lambda *_: (0, 0, 0)),
            ],
        ),
        out_shape=[
            jax.ShapeDtypeStruct((frames, model_width), jnp.bfloat16),
            jax.ShapeDtypeStruct((3, frames, columns), jnp.bfloat16),
            jax.ShapeDtypeStruct((cycles, 8, model_width), jnp.float32),
        ],
        cost_estimate=pl.CostEstimate(
            flops=6 * frames * model_width * columns, transcendentals=0, bytes_accessed=frames * model_width * 6
        ),
        name="project",
    )(info, features_full, *mod_pieces, here, away, cosine, sine)


def forward_kernel(count, info_ref, range_ref, qkv_ref, out0, out1, out2, out3, log_ref, value_t, scores):
    block = pl.program_id(0)
    _, frames, columns = qkv_ref.shape
    size = out0.shape[0]
    pairs = columns // 128
    heads = 2 * pairs

    @pl.when(block == 0)
    def _():
        def rows(i, carry):
            at = pl.ds(pl.multiple_of(i * BLOCK, BLOCK), BLOCK)
            value_t[:, at] = qkv_ref[2, at, :].T
            return carry

        lax.fori_loop(0, frames // BLOCK, rows, 0)

    here = pl.ds(pl.multiple_of(block * size, 128), size)
    query_t = qkv_ref[0, here, :].T
    head_of = lax.broadcasted_iota(jnp.int32, (128, size), 0) < HEAD_DIM
    zero = jnp.zeros((128, size), jnp.bfloat16)
    query_heads = []
    for p in range(pairs):
        part = query_t[128 * p : 128 * p + 128]
        query_heads += [jnp.where(head_of, part, zero), jnp.where(head_of, zero, part)]
    own = utterance_of(lax.broadcasted_iota(jnp.int32, (1, size), 1) + block * size, info_ref, count)
    begin, end = range_ref[0, block], range_ref[1, block]

    def score(i, tops):
        at = pl.ds(pl.multiple_of(i * BLOCK, BLOCK), BLOCK)
        theirs = utterance_of(lax.broadcasted_iota(jnp.int32, (BLOCK, 1), 0) + i * BLOCK, info_ref, count)
        same = theirs == own
        out = []
        for h in range(heads):
            keys = qkv_ref[1, at, 128 * (h // 2) : 128 * (h // 2) + 128]
            s = jnp.dot(keys, query_heads[h], preferred_element_type=jnp.float32)
            s = jnp.where(same, s, -1e30)
            scores[h, at, :] = s
            out.append(jnp.maximum(tops[h], jnp.max(s, axis=0, keepdims=True)))
        return tuple(out)

    lowest = jnp.full((1, size), -1e30, jnp.float32)
    tops = lax.fori_loop(begin, end, score, (lowest,) * heads)

    def weigh(i, carry):
        at = pl.ds(pl.multiple_of(i * BLOCK, BLOCK), BLOCK)
        out = []
        for h in range(heads):
            total, mixed = carry[h]
            p = jnp.exp(scores[h, at, :] - tops[h])
            total = total + jnp.sum(p, axis=0, keepdims=True)
            mixed = mixed + jnp.dot(
                value_t[h * HEAD_DIM : (h + 1) * HEAD_DIM, at], p.astype(jnp.bfloat16), preferred_element_type=jnp.float32
            )
            out.append((total, mixed))
        return tuple(out)

    start = (jnp.zeros((1, size), jnp.float32), jnp.zeros((HEAD_DIM, size), jnp.float32))
    sums = lax.fori_loop(begin, end, weigh, (start,) * heads)
    mixed = jnp.concatenate([sums[h][1] / sums[h][0] for h in range(heads)], axis=0).T.astype(jnp.bfloat16)
    relative = jnp.bitwise_xor(block, info_ref[0])
    for r, out in enumerate((out0, out1, out2, out3)):

        @pl.when(relative == r)
        def _():
            out[...] = mixed

    for h in range(heads):
        log_ref[h : h + 1, here] = tops[h] + jnp.log(sums[h][0])


def backward_kernel(
    count, info_ref, range_ref, qkv_ref, grad0, grad1, grad2, grad3, log_ref, cos_ref, sin_ref, here_ref, away_ref,
    x_ref, out_ref, part_ref, sums_ref, key_t, key_sum, value_sum, probs,
    grads, grad_ref, total_ref
):
    block = pl.program_id(0)
    _, frames, columns = qkv_ref.shape
    size = grad0.shape[0]
    pairs = columns // 128
    heads = 2 * pairs

    @pl.when(block == 0)
    def _():
        key_sum[...] = jnp.zeros_like(key_sum)
        value_sum[...] = jnp.zeros_like(value_sum)

        def rows(i, carry):
            at = pl.ds(pl.multiple_of(i * BLOCK, BLOCK), BLOCK)
            key_t[:, at] = qkv_ref[1, at, :].T
            return carry

        lax.fori_loop(0, frames // BLOCK, rows, 0)

    here = pl.ds(pl.multiple_of(block * size, 128), size)
    relative = jnp.bitwise_xor(block, info_ref[0])
    for r, piece in enumerate((grad0, grad1, grad2, grad3)):

        @pl.when(relative == r)
        def _():
            grad_ref[...] = piece[...]

    upper_t = lax.broadcasted_iota(jnp.int32, (128, size), 0) < HEAD_DIM
    upper = lax.broadcasted_iota(jnp.int32, (size, 128), 1) < HEAD_DIM
    zero_t, zero = jnp.zeros((128, size), jnp.bfloat16), jnp.zeros((size, 128), jnp.bfloat16)
    query_ts, grad_ts, queries, grad_heads = [], [], [], []
    for p in range(pairs):
        query = qkv_ref[0, here, 128 * p : 128 * p + 128]
        grad = grad_ref[:, 128 * p : 128 * p + 128]
        query_t, grad_t = query.T, grad.T
        query_ts += [jnp.where(upper_t, query_t, zero_t), jnp.where(upper_t, zero_t, query_t)]
        grad_ts += [jnp.where(upper_t, grad_t, zero_t), jnp.where(upper_t, zero_t, grad_t)]
        queries += [jnp.where(upper, query, zero), jnp.where(upper, zero, query)]
        grad_heads += [jnp.where(upper, grad, zero), jnp.where(upper, zero, grad)]
    own = utterance_of(lax.broadcasted_iota(jnp.int32, (1, size), 1) + block * size, info_ref, count)
    begin, end = range_ref[0, block], range_ref[1, block]
    logs = [log_ref[h : h + 1, here] for h in range(heads)]

    def first(i, deltas):
        at = pl.ds(pl.multiple_of(i * BLOCK, BLOCK), BLOCK)
        theirs = utterance_of(lax.broadcasted_iota(jnp.int32, (BLOCK, 1), 0) + i * BLOCK, info_ref, count)
        same = theirs == own
        out = []
        for h in range(heads):
            lanes = slice(128 * (h // 2), 128 * (h // 2) + 128)
            s = jnp.dot(qkv_ref[1, at, lanes], query_ts[h], preferred_element_type=jnp.float32)
            p = jnp.exp(jnp.where(same, s, -1e30) - logs[h])
            g = jnp.dot(qkv_ref[2, at, lanes], grad_ts[h], preferred_element_type=jnp.float32)
            probs[h, at, :] = p
            grads[h, at, :] = g
            out.append(deltas[h] + jnp.sum(p * g, axis=0, keepdims=True))
        return tuple(out)

    none = jnp.zeros((1, size), jnp.float32)
    deltas = lax.fori_loop(begin, end, first, (none,) * heads)

    def second(i, sums):
        at = pl.ds(pl.multiple_of(i * BLOCK, BLOCK), BLOCK)
        out = []
        for p in range(pairs):
            lanes = slice(128 * p, 128 * p + 128)
            key_add, value_add = key_sum[at, lanes], value_sum[at, lanes]
            for h in (2 * p, 2 * p + 1):
                weight = probs[h, at, :]
                ds = (weight * (grads[h, at, :] - deltas[h])).astype(jnp.bfloat16)
                out.append(
                    sums[h]
                    + jnp.dot(key_t[h * HEAD_DIM : (h + 1) * HEAD_DIM, at], ds, preferred_element_type=jnp.float32)
                )
                key_add = key_add + jnp.dot(ds, queries[h], preferred_element_type=jnp.float32)
                value_add = value_add + jnp.dot(
                    weight.astype(jnp.bfloat16), grad_heads[h], preferred_element_type=jnp.float32
                )
            key_sum[at, lanes] = key_add
            value_sum[at, lanes] = value_add
        return tuple(out)

    zero_sum = jnp.zeros((HEAD_DIM, size), jnp.float32)
    sums = lax.fori_loop(begin, end, second, (zero_sum,) * heads)
    grad_query = jnp.concatenate(sums, axis=0).T * 0.125
    for p in range(pairs):
        lanes = slice(128 * p, 128 * p + 128)
        out_ref[0, here, lanes] = turn(grad_query[:, lanes], cos_ref[here, :], -sin_ref[here, :]).astype(jnp.bfloat16)

    @pl.when(block == pl.num_programs(0) - 1)
    def _():
        def rows(i, carry):
            at = pl.ds(pl.multiple_of(i * BLOCK, BLOCK), BLOCK)
            for p in range(pairs):
                lanes = slice(128 * p, 128 * p + 128)
                out_ref[1, at, lanes] = turn(key_sum[at, lanes], cos_ref[at, :], -sin_ref[at, :]).astype(jnp.bfloat16)
            out_ref[2, at, :] = value_sum[at, :].astype(jnp.bfloat16)
            return carry

        lax.fori_loop(0, frames // BLOCK, rows, 0)
        depth = here_ref.shape[1]
        chunk = 64
        sums_ref[...] = jnp.zeros_like(sums_ref)

        def share(i, carry):
            base = i * size
            at = pl.ds(pl.multiple_of(base, 128), size)
            for side, weight in ((info_ref[1], here_ref), (1 - info_ref[1], away_ref)):
                total = dot_rows(out_ref[0, at, :], weight[0])
                for c in (1, 2):
                    total = total + dot_rows(out_ref[c, at, :], weight[c])
                total_ref[:, pl.ds(pl.multiple_of(side * depth, 128), depth)] = total

            def add(own, first):
                start = base + first
                rows = pl.ds(pl.multiple_of(start, chunk), chunk)
                grad_in = total_ref[own, :]
                part_ref[rows, :] = grad_in.astype(part_ref.dtype)
                normed, _ = spread(x_ref[rows, :].astype(jnp.float32))
                index = lax.broadcasted_iota(jnp.int32, (chunk, 1), 0) + start
                for u in range(count):
                    begin = info_ref[BOUNDS + u - 1] if u else 0
                    end = info_ref[BOUNDS + u]

                    @pl.when((begin < start + chunk) & (end > start))
                    def _():
                        chosen = jnp.where((index >= begin) & (index < end), grad_in, 0.0)
                        sums_ref[0, u : u + 1, :] += jnp.sum(chosen, axis=0, keepdims=True)
                        sums_ref[1, u : u + 1, :] += jnp.sum(chosen * normed, axis=0, keepdims=True)

            over_rows(size, chunk, add)
            return carry

        lax.fori_loop(0, frames // size, share, 0)


def key_ranges(ending, frames, size):
    starting = jnp.concatenate([jnp.zeros((1,), jnp.int32), ending[:-1]])
    begins = jnp.arange(frames // size, dtype=jnp.int32) * size
    first_key = jnp.min(jnp.where(ending[None, :] > begins[:, None], starting[None, :], frames), axis=1)
    last_key = jnp.max(jnp.where(starting[None, :] < begins[:, None] + size, ending[None, :], 0), axis=1)
    return jnp.stack([first_key // BLOCK, (last_key + BLOCK - 1) // BLOCK]).astype(jnp.int32)


def attend(info, ranges, qkv, count):
    _, frames, columns = qkv.shape
    heads = columns // HEAD_DIM
    size = frames // 4
    flat = lambda b, *_: (0, 0)
    return pl.pallas_call(
        partial(forward_kernel, count),
        grid_spec=pltpu.PrefetchScalarGridSpec(
            num_scalar_prefetch=2,
            grid=(4,),
            in_specs=[pl.BlockSpec((3, frames, columns), lambda b, *_: (0, 0, 0))],
            out_specs=[pl.BlockSpec((size, columns), flat)] * 4 + [pl.BlockSpec((heads, frames), flat)],
            scratch_shapes=[
                pltpu.VMEM((columns, frames), jnp.bfloat16),
                pltpu.VMEM((heads, frames, size), jnp.float32),
            ],
        ),
        out_shape=[jax.ShapeDtypeStruct((size, columns), jnp.bfloat16)] * 4
        + [jax.ShapeDtypeStruct((heads, frames), jnp.float32)],
        cost_estimate=pl.CostEstimate(
            flops=8 * frames * frames * columns, transcendentals=heads * frames * frames, bytes_accessed=frames * columns * 8
        ),
        name="attend",
    )(info, ranges, qkv)


def attend_back(info, ranges, qkv, grad_pieces, logs, cosine, sine, here, away, features_full, count):
    _, frames, columns = qkv.shape
    model_width = features_full.shape[1]
    heads = columns // HEAD_DIM
    size = frames // 4
    cube = lambda b, *_: (0, 0, 0)
    flat = lambda b, *_: (0, 0)
    return pl.pallas_call(
        partial(backward_kernel, count),
        grid_spec=pltpu.PrefetchScalarGridSpec(
            num_scalar_prefetch=2,
            grid=(4,),
            in_specs=[pl.BlockSpec((3, frames, columns), cube)]
            + [pl.BlockSpec((size, columns), flat)] * 4
            + [pl.BlockSpec((heads, frames), flat), pl.BlockSpec((frames, 128), flat), pl.BlockSpec((frames, 128), flat)]
            + [whole(here), whole(away), whole(features_full)],
            out_specs=[pl.BlockSpec((3, frames, columns), cube)]
            + [pl.BlockSpec((frames, model_width), flat)]
            + [pl.BlockSpec((2, 8, model_width), cube)],
            scratch_shapes=[
                pltpu.VMEM((columns, frames), jnp.bfloat16),
                pltpu.VMEM((frames, columns), jnp.float32),
                pltpu.VMEM((frames, columns), jnp.float32),
                pltpu.VMEM((heads, frames, size), jnp.float32),
                pltpu.VMEM((heads, frames, size), jnp.float32),
                pltpu.VMEM((size, columns), jnp.bfloat16),
                pltpu.VMEM((size, model_width), jnp.float32),
            ],
        ),
        out_shape=[jax.ShapeDtypeStruct((3, frames, columns), jnp.bfloat16)]
        + [jax.ShapeDtypeStruct((frames, model_width), jnp.bfloat16)]
        + [jax.ShapeDtypeStruct((2, 8, model_width), jnp.float32)],
        cost_estimate=pl.CostEstimate(
            flops=16 * frames * frames * columns, transcendentals=heads * frames * frames, bytes_accessed=frames * columns * 20
        ),
        name="attend_back",
    )(info, ranges, qkv, *grad_pieces, logs, cosine, sine, here, away, features_full)


def middle_kernel(
    count, info_ref, x_ref, cot_ref, mixed0, mixed1, mixed2, mixed3, mod_ref, *refs
):
    pieces = refs[:10]
    out_ref, res_ref, g0, g1, g2, g3, sums_ref, ffn_in_ref, hidden_ref, grad_up_ref, grad_attn_ref, grad_ffn_ref = refs[10:22]
    mixed, wide, residual, attn, up, ffn, inverse, sems = refs[22:]
    me, core, group = info_ref[0], info_ref[1], info_ref[2]
    size = x_ref.shape[0]
    width = mixed0.shape[1]
    quarter = pieces[0].shape[2]
    depth = 4 * quarter

    copies = ([], [])
    for side in range(2):
        half = core if side == 0 else 1 - core
        for k, r in [(k, r) for k in range(4) for r in range(4)]:
            if k < 3:
                piece = pieces[5 * side + k].at[r]
            else:
                piece = pieces[5 * side + 3 + r // 2].at[r % 2]
            at = pl.ds(pl.multiple_of(half * depth + jnp.bitwise_xor(group, k) * quarter, 16), quarter)
            lanes = pl.ds(pl.multiple_of(jnp.bitwise_xor(me, r) * width, 128), width)
            for part, cs in enumerate((slice(0, 1), slice(1, 5))):
                copy = pltpu.make_async_copy(
                    piece.at[cs], wide.at[cs, at, lanes], sems.at[part * 32 + side * 16 + k * 4 + r]
                )
                copies[part].append(copy)
    for copy in copies[0] + copies[1]:
        copy.start()
    for r, piece in enumerate((mixed0, mixed1, mixed2, mixed3)):
        mixed[:, r * width : (r + 1) * width] = piece[...]
    chunk = 64

    def table(c, number):
        return by_utterance(number, mod_ref[c, 0:count, :])

    def numbers(first):
        return utterance_of(lax.broadcasted_iota(jnp.int32, (chunk, 1), 0) + me * size + first, info_ref, count)

    for copy in copies[0]:
        copy.wait()
    attn[...] = dot_rows(mixed[...], wide[0])

    def enter(at, first):
        number = numbers(first)
        value = x_ref[at, :].astype(jnp.float32) + table(2, number) * attn[at, :]
        residual[at, :] = value
        normed, scale = spread(value)
        inverse[at, :] = jnp.broadcast_to(scale, (chunk, 128))
        ffn[at, :] = normed
        ffn_in_ref[at, :] = (normed * (1.0 + table(4, number)) + table(3, number)).astype(jnp.bfloat16)
        grad_ffn_ref[at, :] = (cot_ref[at, :].astype(jnp.float32) * table(5, number)).astype(jnp.bfloat16)

    over_rows(size, chunk, enter)
    for copy in copies[1]:
        copy.wait()
    for c in range(2):
        up[c] = dot(ffn_in_ref[...], wide[3 + c])

    root = math.sqrt(2.0 / math.pi)

    def act(at, first):
        for c in range(2):
            value = up[c, at, :]
            square = value * value
            bend = jnp.tanh(root * (value + 0.044715 * (value * square)))
            hidden_ref[c, at, :] = (0.5 * value * (1.0 + bend)).astype(jnp.bfloat16)
            up[c, at, :] = 0.5 * (1.0 + bend) + 0.5 * value * (1.0 - bend * bend) * (root * (1.0 + 0.134145 * square))

    over_rows(size, chunk, act)
    grad_hidden = [dot(grad_ffn_ref[...], wide[1 + c]) for c in range(2)]
    for c in range(2):
        grad_up_ref[c] = (up[c] * grad_hidden[c]).astype(jnp.bfloat16)
    up[0] = dot_rows(hidden_ref[0], wide[1]) + dot_rows(hidden_ref[1], wide[2])
    up[1] = dot_rows(grad_up_ref[0], wide[3]) + dot_rows(grad_up_ref[1], wide[4])
    sums_ref[...] = jnp.zeros_like(sums_ref)

    def leave(at, first):
        number = numbers(first)
        cot = cot_ref[at, :].astype(jnp.float32)
        ffn_out, grad_in, normed = up[0, at, :], up[1, at, :], ffn[at, :]
        out_ref[at, :] = (residual[at, :] + table(5, number) * ffn_out).astype(jnp.bfloat16)
        h = grad_in * (1.0 + table(4, number))
        grad = cot + inverse[at, 0:1] * (
            h - jnp.mean(h, axis=-1, keepdims=True) - normed * jnp.mean(h * normed, axis=-1, keepdims=True)
        )
        res_ref[at, :] = grad
        grad_attn_ref[at, :] = (grad * table(2, number)).astype(jnp.bfloat16)
        for c, rows in enumerate((grad * attn[at, :], grad_in, grad_in * normed, cot * ffn_out)):
            for u in range(count):
                sums_ref[c, u : u + 1, :] += jnp.sum(jnp.where(number == u, rows, 0.0), axis=0, keepdims=True)

    over_rows(size, chunk, leave)
    grad_mixed = dot(grad_attn_ref[...], wide[0]).astype(jnp.bfloat16)
    for r, piece in enumerate((g0, g1, g2, g3)):
        piece[...] = grad_mixed[:, r * width : (r + 1) * width]


def middle(info, features, cotangent, mixed_pieces, modulation, wide_here, wide_away, count):
    size, model_width = features.shape
    width = mixed_pieces[0].shape[1]
    pieces = (*wide_here, *wide_away)
    shapes = [
        ((size, model_width), jnp.bfloat16),
        ((size, model_width), jnp.float32),
        *[((size, width), jnp.bfloat16)] * 4,
        ((4, 8, model_width), jnp.float32),
        ((size, model_width), jnp.bfloat16),
        ((2, size, 4 * width), jnp.bfloat16),
        ((2, size, 4 * width), jnp.bfloat16),
        ((size, model_width), jnp.bfloat16),
        ((size, model_width), jnp.bfloat16),
        ((size, 4 * width), jnp.bfloat16),
    ]
    outs = [jax.ShapeDtypeStruct(shape, kind) for shape, kind in shapes]
    return pl.pallas_call(
        partial(middle_kernel, count),
        grid_spec=pltpu.PrefetchScalarGridSpec(
            num_scalar_prefetch=1,
            grid=(1,),
            in_specs=[whole(a) for a in (features, cotangent, *mixed_pieces, modulation)]
            + [pl.BlockSpec(memory_space=pl.ANY)] * 10,
            out_specs=[whole(a) for a in outs],
            scratch_shapes=[
                pltpu.VMEM((5, model_width, 4 * width), jnp.bfloat16),
                pltpu.VMEM((size, model_width), jnp.float32),
                pltpu.VMEM((size, model_width), jnp.float32),
                pltpu.VMEM((2, size, 4 * width), jnp.float32),
                pltpu.VMEM((size, model_width), jnp.float32),
                pltpu.VMEM((size, 128), jnp.float32),
                pltpu.SemaphoreType.DMA((64,)),
            ],
        ),
        out_shape=outs,
        cost_estimate=pl.CostEstimate(
            flops=20 * size * model_width * 4 * width, transcendentals=size * 8 * width, bytes_accessed=10 * model_width * 4 * width
        ),
        name="middle",
    )(info, features, cotangent, *mixed_pieces, modulation, *pieces)


def wide_grad_kernel(side, summed, info_ref, mixed_ref, hidden_ref, grad_up_ref, *refs):
    grad_refs, other_ref, out_ref, turned = refs[:3], refs[3] if summed else None, refs[-2], refs[-1]
    depth = out_ref.shape[2]
    half = info_ref[1] if side == 0 else 1 - info_ref[1]

    @pl.when(pl.program_id(0) == 0)
    def _():
        at = pl.ds(pl.multiple_of(half * depth, 128), depth)
        for i in range(3):
            turned[i] = grad_refs[i][:, at].T

    def block(c):
        if c == 0:
            return dot(turned[0], mixed_ref[...])
        if c < 3:
            return dot(turned[1], hidden_ref[c - 1])
        return dot(turned[2], grad_up_ref[c - 3])

    for c in range(5):
        value = block(c)
        if summed:
            value = value + other_ref[0, c].astype(jnp.float32)
        out_ref[0, c] = value.astype(jnp.bfloat16)


def wide_grads(info, side, mixed, hidden, grad_up, grad_attn, grad_ffn, ffn_in, other=None):
    size, width = mixed.shape[0], mixed.shape[1] // 4
    depth = grad_attn.shape[1] // 2
    lanes = lambda r, info: (0, 0, r)
    target = pl.BlockSpec((1, 5, depth, width), lambda r, info: (jnp.bitwise_xor(info[0], r), 0, 0, 0))
    return pl.pallas_call(
        partial(wide_grad_kernel, side, other is not None),
        grid_spec=pltpu.PrefetchScalarGridSpec(
            num_scalar_prefetch=1,
            grid=(4,),
            in_specs=[
                pl.BlockSpec((size, width), lambda r, info: (0, r)),
                pl.BlockSpec((2, size, width), lanes),
                pl.BlockSpec((2, size, width), lanes),
                whole(grad_attn),
                whole(grad_ffn),
                whole(ffn_in),
            ]
            + ([target] if other is not None else []),
            out_specs=target,
            scratch_shapes=[pltpu.VMEM((3, depth, size), jnp.bfloat16)],
        ),
        out_shape=jax.ShapeDtypeStruct((4, 5, depth, width), jnp.bfloat16),
        cost_estimate=pl.CostEstimate(
            flops=40 * size * depth * width, transcendentals=0, bytes_accessed=60 * depth * width
        ),
        name="wide_grads",
    )(info, mixed, hidden, grad_up, grad_attn, grad_ffn, ffn_in, *([other] if other is not None else []))


def qkv_grad_kernel(side, summed, info_ref, grad_ref, att_ref, *refs):
    other_ref, out_ref, turned = refs[0] if summed else None, refs[-2], refs[-1]
    depth = out_ref.shape[1]
    half = info_ref[1] if side == 0 else 1 - info_ref[1]

    @pl.when(pl.program_id(0) == 0)
    def _():
        turned[...] = att_ref[:, pl.ds(pl.multiple_of(half * depth, 128), depth)].T

    value = dot(turned[...], grad_ref[0])
    if summed:
        value = value + other_ref[0].astype(jnp.float32)
    out_ref[0] = value.astype(out_ref.dtype)


def qkv_grads(info, side, gradients, att_full, other=None, kind=jnp.bfloat16):
    _, frames, columns = gradients.shape
    depth = att_full.shape[1] // 2
    target = pl.BlockSpec((1, depth, columns), lambda c, *_: (c, 0, 0))
    return pl.pallas_call(
        partial(qkv_grad_kernel, side, other is not None),
        grid_spec=pltpu.PrefetchScalarGridSpec(
            num_scalar_prefetch=1,
            grid=(3,),
            in_specs=[pl.BlockSpec((1, frames, columns), lambda c, *_: (c, 0, 0)), whole(att_full)]
            + ([target] if other is not None else []),
            out_specs=target,
            scratch_shapes=[pltpu.VMEM((depth, frames), jnp.bfloat16)],
        ),
        out_shape=jax.ShapeDtypeStruct((3, depth, columns), kind),
        cost_estimate=pl.CostEstimate(
            flops=6 * frames * depth * columns, transcendentals=0, bytes_accessed=frames * depth * 6
        ),
        name="qkv_grads",
    )(info, gradients, att_full, *([other] if other is not None else []))


def inner_step(grads, first, second, weights, steps_done):
    first_new = beta_first * first + (1.0 - beta_first) * grads
    second_new = beta_second * second + (1.0 - beta_second) * grads * grads
    correct_one = 1.0 - beta_first**steps_done
    correct_two = 1.0 - beta_second**steps_done
    difference = inner_rate * (
        first_new / correct_one / (jnp.sqrt(second_new / correct_two) + adam_epsilon)
        + weight_decay * weights
    )
    return (first_new[None], second_new[None], difference)


def outer_step(average, outer, weights):
    outer_new = outer_beta * outer + average
    return (outer_new, weights - outer_rate * (average + outer_beta * outer_new))


def swapped(values, axis, bits):
    size = lax.axis_size(axis)
    return lax.ppermute(values, axis, [(i, i ^ bits) for i in range(size)])


def exchange(blocks, axis="tensor"):
    return [blocks[0]] + [swapped(blocks[r], axis, r) for r in range(1, 4)]


def after(values, *others):
    return lax.optimization_barrier((values, *others))[0]


def dp_rows(own):
    if lax.axis_size("dp") != 2:
        return lax.all_gather(own, "dp", axis=0, tiled=True)
    other = swapped(own, "dp", 1)
    first = lax.axis_index("dp") == 0
    return jnp.concatenate([jnp.where(first, own, other), jnp.where(first, other, own)], axis=0)


def dp_pair(own):
    if lax.axis_size("dp") == 2:
        return own, swapped(own, "dp", 1)
    return tuple(jnp.split(lax.all_gather(own, "dp", axis=1, tiled=True), 2, axis=1))


def quarter_of(half):
    quarter = half.shape[1] // 4
    return lax.dynamic_slice_in_dim(half, lax.axis_index("group") * quarter, quarter, 1)


def spread_wide(stack):
    one, two = swapped(stack, "group", 1), swapped(stack, "group", 2)
    return [stack, one, two, swapped(one[:2], "group", 2), swapped(two[2:], "group", 1)]


def group_parts(values):
    group = lax.axis_index("group")
    quarter = values.shape[1] // 4
    return exchange([lax.dynamic_slice_in_dim(values, (group ^ r) * quarter, quarter, 1) for r in range(4)], "group")


def add_parts(parts):
    return sum(part.astype(jnp.float32) for part in parts).astype(low)


def group_pieces(total):
    return exchange([total] * 4, "group")


def group_average(pieces):
    group = lax.axis_index("group")
    for bit in (1, 2):
        differs = (group & bit) == bit
        pieces = [jnp.where(differs, pieces[q ^ bit], pieces[q]) for q in range(4)]
    return jnp.concatenate(pieces, axis=1).astype(jnp.float32) / lax.axis_size("group")


def per_device(
    features,
    cotangent,
    frame_counts,
    buckets,
    step_count,
    col_weights,
    mod_weights,
    row_weights,
    col_first,
    col_second,
    mod_first,
    mod_second,
    row_first,
    row_second,
    col_outer,
    mod_outer,
    row_outer,
):
    group_count = lax.axis_size("group")
    packs_here = lax.axis_size("dp")
    own_rows, model_width = features.shape
    frames = own_rows * 4
    me = lax.axis_index("tensor")
    core = lax.axis_index("dp")
    group = lax.axis_index("group")
    count = buckets.shape[1]
    share = mod_weights.shape[0]
    width = col_weights.shape[2]

    def columns_first(values):
        return jnp.swapaxes(values, -3, -2)

    col_major = columns_first(col_weights).astype(low)
    wide_low = jnp.concatenate([row_weights.astype(low), col_major[3:5]], axis=0)
    halves = [wide_low] if packs_here == 2 else list(dp_pair(wide_low))
    stacks = [lax.all_gather(quarter_of(half), "tensor", axis=0) for half in halves]
    features_full = lax.all_gather(after(features, *stacks), "tensor", axis=0, tiled=True)

    buckets_all = dp_rows(buckets[0])
    flow_time = ((group * NBUCK + buckets_all).astype(jnp.float32) + 0.5) / (NBUCK * group_count)
    condition_all = jax.nn.silu(time_embedding(flow_time, model_width)).astype(low)
    condition_here = lax.dynamic_slice_in_dim(condition_all, core * share, share, 1)
    mod_terms = jnp.einsum("ud,dcj->cuj", condition_here, mod_weights.astype(low), preferred_element_type=jnp.float32)
    if packs_here != 2:
        mod_part = lax.psum_scatter(mod_terms, "dp", scatter_dimension=1, tiled=True)
    else:
        mod_away = lax.dynamic_slice_in_dim(mod_terms, (1 - core) * count, count, 1)
        mod_part = lax.dynamic_slice_in_dim(mod_terms, core * count, count, 1) + swapped(mod_away, "dp", 1)
    mod_pieces = exchange([mod_part] * 4)

    ending = jnp.cumsum(frame_counts[0]).astype(jnp.int32)
    half_core = core if packs_here == 2 else jnp.zeros_like(core)
    info = jnp.concatenate([jnp.stack([me, half_core, group]).astype(jnp.int32), ending])
    _, position = utterance_rows(ending, jnp.arange(frames, dtype=jnp.int32))
    cosine, sine = rotary_tables(position)
    ranges = key_ranges(ending, frames, own_rows)
    qkv_here, qkv_away = dp_pair(col_major[0:3])
    wide_sets = [spread_wide(stack) for stack in stacks]
    if packs_here == 2:
        wide_sets.append([swapped(piece, "dp", 1) for piece in wide_sets[0]])

    att_full, qkv, modulation = project(info, features_full, mod_pieces, qkv_here, qkv_away, cosine, sine)
    *mixed_pieces, log_totals = attend(info, ranges, qkv, count)
    mixed_pieces = exchange(mixed_pieces)

    (output, grad_residual, g0, g1, g2, g3, late_sums, ffn_in, hidden, grad_up, grad_attn, grad_ffn, mixed) = middle(
        info, features, cotangent, mixed_pieces, modulation, *wide_sets, count
    )
    def to_owners(sums):
        return sum(exchange([lax.dynamic_slice_in_dim(sums, (me ^ r) * width, width, 2) for r in range(4)]))

    def mod_gradient(sums):
        columns = dp_rows(jnp.swapaxes(sums, 0, 1))
        if packs_here != 2:
            return jnp.einsum("ud,ucj->cdj", condition_here.astype(jnp.float32), columns, precision=highest)
        total = 0.0
        for u in range(columns.shape[0]):
            total = total + condition_here[u].astype(jnp.float32)[None, :, None] * columns[u][:, None, :]
        return total

    def some_diff(grads, first, second, weights, some):
        state = [columns_first(a)[some] for a in (first[0], second[0], weights)]
        return inner_step(grads, *state, steps_done)[2].astype(low)

    steps_done = step_count[0].astype(jnp.float32)
    grad_pieces = exchange([g0, g1, g2, g3])
    late_sums = to_owners(late_sums[:, :count])
    wide_args = (mixed, hidden, grad_up, grad_attn, grad_ffn, ffn_in)
    if packs_here == 2:
        wide_away_grad = after(swapped(wide_grads(info, 1, *wide_args), "dp", 1), *grad_pieces, late_sums)
        wide_blocks = wide_grads(info, 0, *wide_args, other=wide_away_grad)
    else:
        both = jnp.concatenate([wide_grads(info, side, *wide_args) for side in range(2)], axis=2).astype(jnp.float32)
        wide_blocks = lax.psum_scatter(both, "dp", scatter_dimension=2, tiled=True).astype(low)
    wide_grad = lax.psum_scatter(wide_blocks, "tensor", scatter_dimension=0, tiled=False)

    late_mod = mod_gradient(after(late_sums, wide_blocks))
    first_parts = group_parts(some_diff(late_mod, mod_first, mod_second, mod_weights, slice(2, 6)))
    attended = attend_back(
        info, ranges, qkv, grad_pieces, log_totals, cosine, sine, qkv_here, qkv_away, features_full, count
    )
    gradients, att_part, early_sums, *first_parts = lax.optimization_barrier((*attended, *first_parts))
    grad_att_in = lax.psum_scatter(after(att_part, wide_blocks), "tensor", scatter_dimension=0, tiled=True)
    first_pieces = group_pieces(add_parts(first_parts))
    early_mod = mod_gradient(to_owners(early_sums[:, :count]))
    if packs_here == 2:
        qkv_away_grad = swapped(qkv_grads(info, 1, gradients, att_full), "dp", 1)
        qkv_away_grad, *first_pieces = lax.optimization_barrier((qkv_away_grad, *first_pieces))
        qkv_share = qkv_grads(info, 0, gradients, att_full, other=qkv_away_grad, kind=jnp.float32)
    else:
        both = [qkv_grads(info, side, gradients, att_full, kind=jnp.float32) for side in range(2)]
        qkv_share = lax.psum_scatter(jnp.concatenate(both, axis=1), "dp", scatter_dimension=1, tiled=True)
    second_parts = group_parts(
        jnp.concatenate(
            [
                some_diff(qkv_share, col_first, col_second, col_weights, slice(0, 3)),
                some_diff(early_mod, mod_first, mod_second, mod_weights, slice(0, 2)),
            ],
            axis=0,
        )
    )

    row_first_new, row_second_new, row_diff = inner_step(
        wide_grad[0:3].astype(jnp.float32), row_first[0], row_second[0], row_weights, steps_done
    )
    col_first_new, col_second_new, col_diff = inner_step(
        columns_first(jnp.concatenate([qkv_share, wide_grad[3:5].astype(jnp.float32)], axis=0)), col_first[0], col_second[0], col_weights, steps_done
    )
    wide_diff = jnp.concatenate([row_diff.astype(low), columns_first(col_diff)[3:5].astype(low)], axis=0)
    wide_diff, *second_parts = lax.optimization_barrier((wide_diff, *second_parts))
    third_parts = group_parts(wide_diff)
    second_sum = add_parts(second_parts)
    second_pieces = group_pieces(second_sum)
    both = lax.optimization_barrier((*second_pieces, *third_parts))
    second_pieces, third_parts = both[:4], both[4:]
    third_sum = add_parts(third_parts)
    third_pieces = group_pieces(third_sum)
    mod_first_new, mod_second_new, _ = inner_step(
        columns_first(after(jnp.concatenate([early_mod, late_mod], axis=0), second_sum)),
        mod_first[0],
        mod_second[0],
        mod_weights,
        steps_done,
    )

    first_average, second_average = group_average(first_pieces), group_average(second_pieces)
    mod_average = columns_first(jnp.concatenate([second_average[3:5], first_average], axis=0))
    mod_outer_new, mod_new = outer_step(mod_average, mod_outer, mod_weights)
    third_pieces = lax.optimization_barrier((*third_pieces, mod_average, mod_outer_new, mod_new))[:4]
    third_average = group_average(third_pieces)
    row_average = third_average[0:3]
    col_average = columns_first(jnp.concatenate([second_average[0:3], third_average[3:5]], axis=0))
    col_outer_new, col_new = outer_step(col_average, col_outer, col_weights)
    row_outer_new, row_new = outer_step(row_average, row_outer, row_weights)

    grad_att_in = after(grad_att_in, col_new, row_new).astype(jnp.float32)
    number_own, _ = utterance_rows(ending, me * own_rows + jnp.arange(own_rows, dtype=jnp.int32))
    normed, inverse_scale = normalize(features.astype(jnp.float32))
    grad_features = grad_residual + normalize_back(
        grad_att_in * (1.0 + by_utterance(number_own[:, None], modulation[1, :count])), normed, inverse_scale
    )
    return (
        output,
        grad_features,
        col_first_new,
        col_second_new,
        col_average,
        col_outer_new,
        col_new,
        mod_first_new,
        mod_second_new,
        mod_average,
        mod_outer_new,
        mod_new,
        row_first_new,
        row_second_new,
        row_average,
        row_outer_new,
        row_new,
    )


def solution(mesh):
    placed = (
        P(("group", "dp", "tensor"), None),
        P(("group", "dp", "tensor"), None),
        P(("group", "dp"), None),
        P(("group", "dp"), None),
        P(),
        P("dp", None, "tensor"),
        P("dp", None, "tensor"),
        P(None, "dp", "tensor"),
        P("group", "dp", None, "tensor"),
        P("group", "dp", None, "tensor"),
        P("group", "dp", None, "tensor"),
        P("group", "dp", None, "tensor"),
        P("group", None, "dp", "tensor"),
        P("group", None, "dp", "tensor"),
        P("dp", None, "tensor"),
        P("dp", None, "tensor"),
        P(None, "dp", "tensor"),
    )
    return jax.shard_map(
        per_device,
        mesh=mesh,
        in_specs=placed,
        out_specs=(
            P(("group", "dp", "tensor"), None),
            P(("group", "dp", "tensor"), None),
            P("group", "dp", None, "tensor"),
            P("group", "dp", None, "tensor"),
            P("dp", None, "tensor"),
            P("dp", None, "tensor"),
            P("dp", None, "tensor"),
            P("group", "dp", None, "tensor"),
            P("group", "dp", None, "tensor"),
            P("dp", None, "tensor"),
            P("dp", None, "tensor"),
            P("dp", None, "tensor"),
            P("group", None, "dp", "tensor"),
            P("group", None, "dp", "tensor"),
            P(None, "dp", "tensor"),
            P(None, "dp", "tensor"),
            P(None, "dp", "tensor"),
        ),
        check_vma=False,
    )
```

```python
from functools import partial
import math

import jax
import jax.numpy as jnp
from jax import lax
from jax.experimental import pallas as pl
from jax.experimental.pallas import tpu as pltpu
from jax.sharding import PartitionSpec as P

HEAD_DIM = 64
NBUCK = 8
BLOCK = 256
BOUNDS = 3

highest = lax.Precision.HIGHEST
norm_epsilon = 1e-06
adam_epsilon = 1e-08
beta_first = 0.9
beta_second = 0.999
inner_rate = 0.05
weight_decay = 0.01
outer_rate = 0.7
outer_beta = 0.9
low = jnp.bfloat16


def time_embedding(flow_time, width_all):
    half_width = width_all // 2
    frequency = jnp.exp(
        jnp.arange(half_width, dtype=jnp.float32) * (-math.log(10000.0) / (half_width - 1))
    )
    angles = 1000.0 * flow_time[:, None] * frequency[None, :]
    return jnp.concatenate([jnp.sin(angles), jnp.cos(angles)], axis=1)


def utterance_rows(ending, indices):
    number = jnp.zeros(indices.shape, jnp.int32)
    begin = jnp.zeros(indices.shape, jnp.int32)
    for u in range(ending.shape[0] - 1):
        after = indices >= ending[u]
        number = number + after.astype(jnp.int32)
        begin = jnp.where(after, ending[u], begin)
    return number, indices - begin


def rotary_tables(position):
    half_width = HEAD_DIM // 2
    frequency = jnp.exp(
        jnp.arange(half_width, dtype=jnp.float32) * (-2.0 * math.log(10000.0) / HEAD_DIM)
    )
    angles = position.astype(jnp.float32)[:, None] * frequency[None, :]
    cosine, sine = jnp.cos(angles), jnp.sin(angles)
    return jnp.concatenate([cosine] * 4, axis=1), jnp.concatenate([-sine, sine, -sine, sine], axis=1)


def normalize_back(grads, normed, inverse_scale):
    return inverse_scale * (
        grads
        - jnp.mean(grads, axis=-1, keepdims=True)
        - normed * jnp.mean(grads * normed, axis=-1, keepdims=True)
    )


def turn(values, cosine, signed_sine):
    lanes = lax.broadcasted_iota(jnp.int32, values.shape, 1)
    swapped = jnp.where(lanes % 64 < 32, pltpu.roll(values, 96, 1), pltpu.roll(values, 32, 1))
    return values * cosine + swapped * signed_sine


def utterance_of(indices, info_ref, count):
    number = jnp.zeros(indices.shape, jnp.int32)
    for u in range(count - 1):
        number = number + (indices >= info_ref[BOUNDS + u]).astype(jnp.int32)
    return number


def by_utterance(number, table):
    out = table[0:1, :]
    for u in range(1, table.shape[0]):
        out = jnp.where(number >= u, table[u : u + 1, :], out)
    return out


def dot_rows(a, b):
    return lax.dot_general(a, b, (((1,), (1,)), ((), ())), preferred_element_type=jnp.float32)


def dot(a, b):
    return jnp.dot(a, b, preferred_element_type=jnp.float32)


def spread(values):
    centered = values - jnp.mean(values, axis=-1, keepdims=True)
    inverse = lax.rsqrt(jnp.mean(centered * centered, axis=-1, keepdims=True) + norm_epsilon)
    return centered * inverse, inverse


def over_rows(total, chunk, body):
    def step(i, carry):
        body(pl.ds(pl.multiple_of(i * chunk, chunk), chunk), i * chunk)
        return carry

    lax.fori_loop(0, total // chunk, step, 0)


def whole(a):
    shape = a.shape
    return pl.BlockSpec(shape, lambda *_: (0,) * len(shape))


def project_kernel(
    count, info_ref, x_ref, m0_ref, m1_ref, m2_ref, m3_ref, here_ref, away_ref, cos_ref, sin_ref, att_ref, qkv_ref, mod_ref,
    mean_ref, inverse_ref
):
    step = pl.program_id(0)
    me, core = info_ref[0], info_ref[1]
    size = x_ref.shape[0]
    width = m0_ref.shape[2]

    @pl.when(step == 0)
    def _():
        mod_ref[...] = jnp.zeros_like(mod_ref)
        for r, piece in enumerate((m0_ref, m1_ref, m2_ref, m3_ref)):
            at = pl.ds(pl.multiple_of(jnp.bitwise_xor(me, r) * width, 128), width)
            mod_ref[:, 0:count, at] = piece[...]

    chunk = 64

    def norm(at, first):
        values = x_ref[at, :].astype(jnp.float32)
        mean = jnp.mean(values, axis=-1, keepdims=True)
        centered = values - mean
        inverse = lax.rsqrt(jnp.mean(centered * centered, axis=-1, keepdims=True) + norm_epsilon)
        normed = centered * inverse
        mean_ref[at, :] = jnp.broadcast_to(mean, (chunk, 128))
        inverse_ref[at, :] = jnp.broadcast_to(inverse, (chunk, 128))
        number = utterance_of(
            lax.broadcasted_iota(jnp.int32, (chunk, 1), 0) + step * size + first, info_ref, count
        )
        shift, scale = by_utterance(number, mod_ref[0, 0:count, :]), by_utterance(number, mod_ref[1, 0:count, :])
        att_ref[at, :] = (normed * (1.0 + scale) + shift).astype(jnp.bfloat16)

    over_rows(size, chunk, norm)
    depth = here_ref.shape[1]
    near = att_ref[:, pl.ds(pl.multiple_of(core * depth, 128), depth)]
    far = att_ref[:, pl.ds(pl.multiple_of((1 - core) * depth, 128), depth)]
    for c in range(3):
        values = dot(near, here_ref[c]) + dot(far, away_ref[c])
        if c < 2:
            for p in range(values.shape[1] // 128):
                lanes = slice(128 * p, 128 * p + 128)
                turned = turn(values[:, lanes], cos_ref[...], sin_ref[...])
                qkv_ref[c, :, lanes] = (turned * 0.125 if c == 0 else turned).astype(jnp.bfloat16)
        else:
            qkv_ref[c] = values.astype(jnp.bfloat16)


def project(info, features_full, mod_pieces, here, away, cosine, sine):
    frames, model_width = features_full.shape
    size = frames // 4
    cycles, count, width = mod_pieces[0].shape
    columns = here.shape[2]
    rows = lambda i, *_: (i, 0)
    return pl.pallas_call(
        partial(project_kernel, count),
        grid_spec=pltpu.PrefetchScalarGridSpec(
            num_scalar_prefetch=1,
            grid=(4,),
            in_specs=[pl.BlockSpec((size, model_width), rows)]
            + [whole(a) for a in (*mod_pieces, here, away)]
            + [pl.BlockSpec((size, 128), rows)] * 2,
            out_specs=[
                pl.BlockSpec((size, model_width), rows),
                pl.BlockSpec((3, size, columns), lambda i, *_: (0, i, 0)),
                pl.BlockSpec((cycles, 8, model_width), lambda *_: (0, 0, 0)),
            ]
            + [pl.BlockSpec((size, 128), rows)] * 2,
        ),
        out_shape=[
            jax.ShapeDtypeStruct((frames, model_width), jnp.bfloat16),
            jax.ShapeDtypeStruct((3, frames, columns), jnp.bfloat16),
            jax.ShapeDtypeStruct((cycles, 8, model_width), jnp.float32),
        ]
        + [jax.ShapeDtypeStruct((frames, 128), jnp.float32)] * 2,
        cost_estimate=pl.CostEstimate(
            flops=6 * frames * model_width * columns, transcendentals=0, bytes_accessed=frames * model_width * 6
        ),
        name="project",
    )(info, features_full, *mod_pieces, here, away, cosine, sine)


def forward_kernel(count, info_ref, range_ref, qkv_ref, out0, out1, out2, out3, log_ref, value_t, scores):
    block = pl.program_id(0)
    _, frames, columns = qkv_ref.shape
    size = out0.shape[0]
    pairs = columns // 128
    heads = 2 * pairs

    @pl.when(block == 0)
    def _():
        def rows(i, carry):
            at = pl.ds(pl.multiple_of(i * BLOCK, BLOCK), BLOCK)
            value_t[:, at] = qkv_ref[2, at, :].T
            return carry

        lax.fori_loop(0, frames // BLOCK, rows, 0)

    here = pl.ds(pl.multiple_of(block * size, 128), size)
    query_t = qkv_ref[0, here, :].T
    head_of = lax.broadcasted_iota(jnp.int32, (128, size), 0) < HEAD_DIM
    zero = jnp.zeros((128, size), jnp.bfloat16)
    query_heads = []
    for p in range(pairs):
        part = query_t[128 * p : 128 * p + 128]
        query_heads += [jnp.where(head_of, part, zero), jnp.where(head_of, zero, part)]
    own = utterance_of(lax.broadcasted_iota(jnp.int32, (1, size), 1) + block * size, info_ref, count)
    begin, end = range_ref[0, block], range_ref[1, block]

    def score(i, tops):
        at = pl.ds(pl.multiple_of(i * BLOCK, BLOCK), BLOCK)
        theirs = utterance_of(lax.broadcasted_iota(jnp.int32, (BLOCK, 1), 0) + i * BLOCK, info_ref, count)
        same = theirs == own
        out = []
        for h in range(heads):
            keys = qkv_ref[1, at, 128 * (h // 2) : 128 * (h // 2) + 128]
            s = jnp.dot(keys, query_heads[h], preferred_element_type=jnp.float32)
            s = jnp.where(same, s, -1e30)
            scores[h, at, :] = s
            out.append(jnp.maximum(tops[h], jnp.max(s, axis=0, keepdims=True)))
        return tuple(out)

    lowest = jnp.full((1, size), -1e30, jnp.float32)
    tops = lax.fori_loop(begin, end, score, (lowest,) * heads)

    def weigh(i, carry):
        at = pl.ds(pl.multiple_of(i * BLOCK, BLOCK), BLOCK)
        out = []
        for h in range(heads):
            total, mixed = carry[h]
            p = jnp.exp(scores[h, at, :] - tops[h])
            total = total + jnp.sum(p, axis=0, keepdims=True)
            mixed = mixed + jnp.dot(
                value_t[h * HEAD_DIM : (h + 1) * HEAD_DIM, at], p.astype(jnp.bfloat16), preferred_element_type=jnp.float32
            )
            out.append((total, mixed))
        return tuple(out)

    start = (jnp.zeros((1, size), jnp.float32), jnp.zeros((HEAD_DIM, size), jnp.float32))
    sums = lax.fori_loop(begin, end, weigh, (start,) * heads)
    mixed = jnp.concatenate([sums[h][1] / sums[h][0] for h in range(heads)], axis=0).T.astype(jnp.bfloat16)
    relative = jnp.bitwise_xor(block, info_ref[0])
    for r, out in enumerate((out0, out1, out2, out3)):

        @pl.when(relative == r)
        def _():
            out[...] = mixed

    for h in range(heads):
        log_ref[h : h + 1, here] = tops[h] + jnp.log(sums[h][0])


def backward_kernel(
    count, info_ref, range_ref, qkv_ref, grad0, grad1, grad2, grad3, log_ref, cos_ref, sin_ref, here_ref, away_ref,
    x_ref, mean_ref, inverse_ref, out_ref, part_ref, sums_ref, key_t, key_sum, value_sum, probs,
    grads, grad_ref, total_ref
):
    block = pl.program_id(0)
    _, frames, columns = qkv_ref.shape
    size = grad0.shape[0]
    pairs = columns // 128
    heads = 2 * pairs

    @pl.when(block == 0)
    def _():
        key_sum[...] = jnp.zeros_like(key_sum)
        value_sum[...] = jnp.zeros_like(value_sum)

        def rows(i, carry):
            at = pl.ds(pl.multiple_of(i * BLOCK, BLOCK), BLOCK)
            key_t[:, at] = qkv_ref[1, at, :].T
            return carry

        lax.fori_loop(0, frames // BLOCK, rows, 0)

    here = pl.ds(pl.multiple_of(block * size, 128), size)
    relative = jnp.bitwise_xor(block, info_ref[0])
    for r, piece in enumerate((grad0, grad1, grad2, grad3)):

        @pl.when(relative == r)
        def _():
            grad_ref[...] = piece[...]

    upper_t = lax.broadcasted_iota(jnp.int32, (128, size), 0) < HEAD_DIM
    upper = lax.broadcasted_iota(jnp.int32, (size, 128), 1) < HEAD_DIM
    zero_t, zero = jnp.zeros((128, size), jnp.bfloat16), jnp.zeros((size, 128), jnp.bfloat16)
    query_ts, grad_ts, queries, grad_heads = [], [], [], []
    for p in range(pairs):
        query = qkv_ref[0, here, 128 * p : 128 * p + 128]
        grad = grad_ref[:, 128 * p : 128 * p + 128]
        query_t, grad_t = query.T, grad.T
        query_ts += [jnp.where(upper_t, query_t, zero_t), jnp.where(upper_t, zero_t, query_t)]
        grad_ts += [jnp.where(upper_t, grad_t, zero_t), jnp.where(upper_t, zero_t, grad_t)]
        queries += [jnp.where(upper, query, zero), jnp.where(upper, zero, query)]
        grad_heads += [jnp.where(upper, grad, zero), jnp.where(upper, zero, grad)]
    own = utterance_of(lax.broadcasted_iota(jnp.int32, (1, size), 1) + block * size, info_ref, count)
    begin, end = range_ref[0, block], range_ref[1, block]
    logs = [log_ref[h : h + 1, here] for h in range(heads)]

    def first(i, deltas):
        at = pl.ds(pl.multiple_of(i * BLOCK, BLOCK), BLOCK)
        theirs = utterance_of(lax.broadcasted_iota(jnp.int32, (BLOCK, 1), 0) + i * BLOCK, info_ref, count)
        same = theirs == own
        out = []
        for h in range(heads):
            lanes = slice(128 * (h // 2), 128 * (h // 2) + 128)
            s = jnp.dot(qkv_ref[1, at, lanes], query_ts[h], preferred_element_type=jnp.float32)
            p = jnp.exp(jnp.where(same, s, -1e30) - logs[h])
            g = jnp.dot(qkv_ref[2, at, lanes], grad_ts[h], preferred_element_type=jnp.float32)
            probs[h, at, :] = p
            grads[h, at, :] = g
            out.append(deltas[h] + jnp.sum(p * g, axis=0, keepdims=True))
        return tuple(out)

    none = jnp.zeros((1, size), jnp.float32)
    deltas = lax.fori_loop(begin, end, first, (none,) * heads)

    def second(i, sums):
        at = pl.ds(pl.multiple_of(i * BLOCK, BLOCK), BLOCK)
        out = []
        for p in range(pairs):
            lanes = slice(128 * p, 128 * p + 128)
            key_add, value_add = key_sum[at, lanes], value_sum[at, lanes]
            for h in (2 * p, 2 * p + 1):
                weight = probs[h, at, :]
                ds = (weight * (grads[h, at, :] - deltas[h])).astype(jnp.bfloat16)
                out.append(
                    sums[h]
                    + jnp.dot(key_t[h * HEAD_DIM : (h + 1) * HEAD_DIM, at], ds, preferred_element_type=jnp.float32)
                )
                key_add = key_add + jnp.dot(ds, queries[h], preferred_element_type=jnp.float32)
                value_add = value_add + jnp.dot(
                    weight.astype(jnp.bfloat16), grad_heads[h], preferred_element_type=jnp.float32
                )
            key_sum[at, lanes] = key_add
            value_sum[at, lanes] = value_add
        return tuple(out)

    zero_sum = jnp.zeros((HEAD_DIM, size), jnp.float32)
    sums = lax.fori_loop(begin, end, second, (zero_sum,) * heads)
    grad_query = jnp.concatenate(sums, axis=0).T * 0.125
    for p in range(pairs):
        lanes = slice(128 * p, 128 * p + 128)
        out_ref[0, here, lanes] = turn(grad_query[:, lanes], cos_ref[here, :], -sin_ref[here, :]).astype(jnp.bfloat16)

    @pl.when(block == pl.num_programs(0) - 1)
    def _():
        def rows(i, carry):
            at = pl.ds(pl.multiple_of(i * BLOCK, BLOCK), BLOCK)
            for p in range(pairs):
                lanes = slice(128 * p, 128 * p + 128)
                out_ref[1, at, lanes] = turn(key_sum[at, lanes], cos_ref[at, :], -sin_ref[at, :]).astype(jnp.bfloat16)
            out_ref[2, at, :] = value_sum[at, :].astype(jnp.bfloat16)
            return carry

        lax.fori_loop(0, frames // BLOCK, rows, 0)
        depth = here_ref.shape[1]
        chunk = 64
        sums_ref[...] = jnp.zeros_like(sums_ref)

        def share(i, carry):
            base = i * size
            at = pl.ds(pl.multiple_of(base, 128), size)
            for side, weight in ((info_ref[1], here_ref), (1 - info_ref[1], away_ref)):
                total = dot_rows(out_ref[0, at, :], weight[0])
                for c in (1, 2):
                    total = total + dot_rows(out_ref[c, at, :], weight[c])
                total_ref[:, pl.ds(pl.multiple_of(side * depth, 128), depth)] = total

            def add(own, first):
                start = base + first
                rows = pl.ds(pl.multiple_of(start, chunk), chunk)
                grad_in = total_ref[own, :]
                part_ref[rows, :] = grad_in.astype(part_ref.dtype)
                normed = (x_ref[rows, :].astype(jnp.float32) - mean_ref[rows, 0:1]) * inverse_ref[rows, 0:1]
                index = lax.broadcasted_iota(jnp.int32, (chunk, 1), 0) + start
                for u in range(count):
                    begin = info_ref[BOUNDS + u - 1] if u else 0
                    end = info_ref[BOUNDS + u]

                    @pl.when((begin < start + chunk) & (end > start))
                    def _():
                        chosen = jnp.where((index >= begin) & (index < end), grad_in, 0.0)
                        sums_ref[0, u : u + 1, :] += jnp.sum(chosen, axis=0, keepdims=True)
                        sums_ref[1, u : u + 1, :] += jnp.sum(chosen * normed, axis=0, keepdims=True)

            over_rows(size, chunk, add)
            return carry

        lax.fori_loop(0, frames // size, share, 0)


def key_ranges(ending, frames, size):
    starting = jnp.concatenate([jnp.zeros((1,), jnp.int32), ending[:-1]])
    begins = jnp.arange(frames // size, dtype=jnp.int32) * size
    first_key = jnp.min(jnp.where(ending[None, :] > begins[:, None], starting[None, :], frames), axis=1)
    last_key = jnp.max(jnp.where(starting[None, :] < begins[:, None] + size, ending[None, :], 0), axis=1)
    return jnp.stack([first_key // BLOCK, (last_key + BLOCK - 1) // BLOCK]).astype(jnp.int32)


def attend(info, ranges, qkv, count):
    _, frames, columns = qkv.shape
    heads = columns // HEAD_DIM
    size = frames // 4
    flat = lambda b, *_: (0, 0)
    return pl.pallas_call(
        partial(forward_kernel, count),
        grid_spec=pltpu.PrefetchScalarGridSpec(
            num_scalar_prefetch=2,
            grid=(4,),
            in_specs=[pl.BlockSpec((3, frames, columns), lambda b, *_: (0, 0, 0))],
            out_specs=[pl.BlockSpec((size, columns), flat)] * 4 + [pl.BlockSpec((heads, frames), flat)],
            scratch_shapes=[
                pltpu.VMEM((columns, frames), jnp.bfloat16),
                pltpu.VMEM((heads, frames, size), jnp.float32),
            ],
        ),
        out_shape=[jax.ShapeDtypeStruct((size, columns), jnp.bfloat16)] * 4
        + [jax.ShapeDtypeStruct((heads, frames), jnp.float32)],
        cost_estimate=pl.CostEstimate(
            flops=8 * frames * frames * columns, transcendentals=heads * frames * frames, bytes_accessed=frames * columns * 8
        ),
        name="attend",
    )(info, ranges, qkv)


def attend_back(info, ranges, qkv, grad_pieces, logs, cosine, sine, here, away, features_full, means, inverses, count):
    _, frames, columns = qkv.shape
    model_width = features_full.shape[1]
    heads = columns // HEAD_DIM
    size = frames // 4
    cube = lambda b, *_: (0, 0, 0)
    flat = lambda b, *_: (0, 0)
    return pl.pallas_call(
        partial(backward_kernel, count),
        grid_spec=pltpu.PrefetchScalarGridSpec(
            num_scalar_prefetch=2,
            grid=(4,),
            in_specs=[pl.BlockSpec((3, frames, columns), cube)]
            + [pl.BlockSpec((size, columns), flat)] * 4
            + [pl.BlockSpec((heads, frames), flat), pl.BlockSpec((frames, 128), flat), pl.BlockSpec((frames, 128), flat)]
            + [whole(a) for a in (here, away, features_full, means, inverses)],
            out_specs=[pl.BlockSpec((3, frames, columns), cube)]
            + [pl.BlockSpec((frames, model_width), flat)]
            + [pl.BlockSpec((2, 8, model_width), cube)],
            scratch_shapes=[
                pltpu.VMEM((columns, frames), jnp.bfloat16),
                pltpu.VMEM((frames, columns), jnp.float32),
                pltpu.VMEM((frames, columns), jnp.float32),
                pltpu.VMEM((heads, frames, size), jnp.float32),
                pltpu.VMEM((heads, frames, size), jnp.float32),
                pltpu.VMEM((size, columns), jnp.bfloat16),
                pltpu.VMEM((size, model_width), jnp.float32),
            ],
        ),
        out_shape=[jax.ShapeDtypeStruct((3, frames, columns), jnp.bfloat16)]
        + [jax.ShapeDtypeStruct((frames, model_width), jnp.bfloat16)]
        + [jax.ShapeDtypeStruct((2, 8, model_width), jnp.float32)],
        cost_estimate=pl.CostEstimate(
            flops=16 * frames * frames * columns, transcendentals=heads * frames * frames, bytes_accessed=frames * columns * 20
        ),
        name="attend_back",
    )(info, ranges, qkv, *grad_pieces, logs, cosine, sine, here, away, features_full, means, inverses)


def middle_kernel(
    count, info_ref, x_ref, cot_ref, mixed0, mixed1, mixed2, mixed3, mod_ref, *refs
):
    pieces = refs[:10]
    out_ref, res_ref, g0, g1, g2, g3, sums_ref, ffn_in_ref, hidden_ref, grad_up_ref, grad_attn_ref, grad_ffn_ref = refs[10:22]
    mixed, wide, residual, attn, up, ffn, inverse, sems = refs[22:]
    me, core, group = info_ref[0], info_ref[1], info_ref[2]
    size = x_ref.shape[0]
    width = mixed0.shape[1]
    quarter = pieces[0].shape[2]
    depth = 4 * quarter

    copies = ([], [])
    for side in range(2):
        half = core if side == 0 else 1 - core
        for k, r in [(k, r) for k in range(4) for r in range(4)]:
            if k < 3:
                piece = pieces[5 * side + k].at[r]
            else:
                piece = pieces[5 * side + 3 + r // 2].at[r % 2]
            at = pl.ds(pl.multiple_of(half * depth + jnp.bitwise_xor(group, k) * quarter, 16), quarter)
            lanes = pl.ds(pl.multiple_of(jnp.bitwise_xor(me, r) * width, 128), width)
            for part, cs in enumerate((slice(0, 1), slice(1, 5))):
                copy = pltpu.make_async_copy(
                    piece.at[cs], wide.at[cs, at, lanes], sems.at[part * 32 + side * 16 + k * 4 + r]
                )
                copies[part].append(copy)
    for copy in copies[0] + copies[1]:
        copy.start()
    for r, piece in enumerate((mixed0, mixed1, mixed2, mixed3)):
        mixed[:, r * width : (r + 1) * width] = piece[...]
    chunk = 64

    def table(c, number):
        return by_utterance(number, mod_ref[c, 0:count, :])

    def numbers(first):
        return utterance_of(lax.broadcasted_iota(jnp.int32, (chunk, 1), 0) + me * size + first, info_ref, count)

    for copy in copies[0]:
        copy.wait()
    attn[...] = dot_rows(mixed[...], wide[0])

    def enter(at, first):
        number = numbers(first)
        value = x_ref[at, :].astype(jnp.float32) + table(2, number) * attn[at, :]
        residual[at, :] = value
        normed, scale = spread(value)
        inverse[at, :] = jnp.broadcast_to(scale, (chunk, 128))
        ffn[at, :] = normed
        ffn_in_ref[at, :] = (normed * (1.0 + table(4, number)) + table(3, number)).astype(jnp.bfloat16)
        grad_ffn_ref[at, :] = (cot_ref[at, :].astype(jnp.float32) * table(5, number)).astype(jnp.bfloat16)

    over_rows(size, chunk, enter)
    for copy in copies[1]:
        copy.wait()
    for c in range(2):
        up[c] = dot(ffn_in_ref[...], wide[3 + c])

    root = math.sqrt(2.0 / math.pi)

    def act(at, first):
        for c in range(2):
            value = up[c, at, :]
            square = value * value
            bend = jnp.tanh(root * (value + 0.044715 * (value * square)))
            hidden_ref[c, at, :] = (0.5 * value * (1.0 + bend)).astype(jnp.bfloat16)
            up[c, at, :] = 0.5 * (1.0 + bend) + 0.5 * value * (1.0 - bend * bend) * (root * (1.0 + 0.134145 * square))

    over_rows(size, chunk, act)
    grad_hidden = [dot(grad_ffn_ref[...], wide[1 + c]) for c in range(2)]
    for c in range(2):
        grad_up_ref[c] = (up[c] * grad_hidden[c]).astype(jnp.bfloat16)
    up[0] = dot_rows(hidden_ref[0], wide[1]) + dot_rows(hidden_ref[1], wide[2])
    up[1] = dot_rows(grad_up_ref[0], wide[3]) + dot_rows(grad_up_ref[1], wide[4])
    sums_ref[...] = jnp.zeros_like(sums_ref)

    def leave(at, first):
        number = numbers(first)
        cot = cot_ref[at, :].astype(jnp.float32)
        ffn_out, grad_in, normed = up[0, at, :], up[1, at, :], ffn[at, :]
        out_ref[at, :] = (residual[at, :] + table(5, number) * ffn_out).astype(jnp.bfloat16)
        h = grad_in * (1.0 + table(4, number))
        grad = cot + inverse[at, 0:1] * (
            h - jnp.mean(h, axis=-1, keepdims=True) - normed * jnp.mean(h * normed, axis=-1, keepdims=True)
        )
        res_ref[at, :] = grad
        grad_attn_ref[at, :] = (grad * table(2, number)).astype(jnp.bfloat16)
        for c, rows in enumerate((grad * attn[at, :], grad_in, grad_in * normed, cot * ffn_out)):
            for u in range(count):
                sums_ref[c, u : u + 1, :] += jnp.sum(jnp.where(number == u, rows, 0.0), axis=0, keepdims=True)

    over_rows(size, chunk, leave)
    grad_mixed = dot(grad_attn_ref[...], wide[0]).astype(jnp.bfloat16)
    for r, piece in enumerate((g0, g1, g2, g3)):
        piece[...] = grad_mixed[:, r * width : (r + 1) * width]


def middle(info, features, cotangent, mixed_pieces, modulation, wide_here, wide_away, count):
    size, model_width = features.shape
    width = mixed_pieces[0].shape[1]
    pieces = (*wide_here, *wide_away)
    shapes = [
        ((size, model_width), jnp.bfloat16),
        ((size, model_width), jnp.float32),
        *[((size, width), jnp.bfloat16)] * 4,
        ((4, 8, model_width), jnp.float32),
        ((size, model_width), jnp.bfloat16),
        ((2, size, 4 * width), jnp.bfloat16),
        ((2, size, 4 * width), jnp.bfloat16),
        ((size, model_width), jnp.bfloat16),
        ((size, model_width), jnp.bfloat16),
        ((size, 4 * width), jnp.bfloat16),
    ]
    outs = [jax.ShapeDtypeStruct(shape, kind) for shape, kind in shapes]
    return pl.pallas_call(
        partial(middle_kernel, count),
        grid_spec=pltpu.PrefetchScalarGridSpec(
            num_scalar_prefetch=1,
            grid=(1,),
            in_specs=[whole(a) for a in (features, cotangent, *mixed_pieces, modulation)]
            + [pl.BlockSpec(memory_space=pl.ANY)] * 10,
            out_specs=[whole(a) for a in outs],
            scratch_shapes=[
                pltpu.VMEM((5, model_width, 4 * width), jnp.bfloat16),
                pltpu.VMEM((size, model_width), jnp.float32),
                pltpu.VMEM((size, model_width), jnp.float32),
                pltpu.VMEM((2, size, 4 * width), jnp.float32),
                pltpu.VMEM((size, model_width), jnp.float32),
                pltpu.VMEM((size, 128), jnp.float32),
                pltpu.SemaphoreType.DMA((64,)),
            ],
        ),
        out_shape=outs,
        cost_estimate=pl.CostEstimate(
            flops=20 * size * model_width * 4 * width, transcendentals=size * 8 * width, bytes_accessed=10 * model_width * 4 * width
        ),
        name="middle",
    )(info, features, cotangent, *mixed_pieces, modulation, *pieces)


def wide_grad_kernel(side, summed, info_ref, mixed_ref, hidden_ref, grad_up_ref, *refs):
    grad_refs, other_ref, out_ref, turned = refs[:3], refs[3] if summed else None, refs[-2], refs[-1]
    depth = out_ref.shape[2]
    half = info_ref[1] if side == 0 else 1 - info_ref[1]

    @pl.when(pl.program_id(0) == 0)
    def _():
        at = pl.ds(pl.multiple_of(half * depth, 128), depth)
        for i in range(3):
            turned[i] = grad_refs[i][:, at].T

    def block(c):
        if c == 0:
            return dot(turned[0], mixed_ref[...])
        if c < 3:
            return dot(turned[1], hidden_ref[c - 1])
        return dot(turned[2], grad_up_ref[c - 3])

    for c in range(5):
        value = block(c)
        if summed:
            value = value + other_ref[0, c].astype(jnp.float32)
        out_ref[0, c] = value.astype(jnp.bfloat16)


def wide_grads(info, side, mixed, hidden, grad_up, grad_attn, grad_ffn, ffn_in, other=None):
    size, width = mixed.shape[0], mixed.shape[1] // 4
    depth = grad_attn.shape[1] // 2
    lanes = lambda r, info: (0, 0, r)
    target = pl.BlockSpec((1, 5, depth, width), lambda r, info: (jnp.bitwise_xor(info[0], r), 0, 0, 0))
    return pl.pallas_call(
        partial(wide_grad_kernel, side, other is not None),
        grid_spec=pltpu.PrefetchScalarGridSpec(
            num_scalar_prefetch=1,
            grid=(4,),
            in_specs=[
                pl.BlockSpec((size, width), lambda r, info: (0, r)),
                pl.BlockSpec((2, size, width), lanes),
                pl.BlockSpec((2, size, width), lanes),
                whole(grad_attn),
                whole(grad_ffn),
                whole(ffn_in),
            ]
            + ([target] if other is not None else []),
            out_specs=target,
            scratch_shapes=[pltpu.VMEM((3, depth, size), jnp.bfloat16)],
        ),
        out_shape=jax.ShapeDtypeStruct((4, 5, depth, width), jnp.bfloat16),
        cost_estimate=pl.CostEstimate(
            flops=40 * size * depth * width, transcendentals=0, bytes_accessed=60 * depth * width
        ),
        name="wide_grads",
    )(info, mixed, hidden, grad_up, grad_attn, grad_ffn, ffn_in, *([other] if other is not None else []))


def qkv_grad_kernel(side, summed, info_ref, grad_ref, att_ref, *refs):
    other_ref, out_ref, turned = refs[0] if summed else None, refs[-2], refs[-1]
    depth = out_ref.shape[1]
    half = info_ref[1] if side == 0 else 1 - info_ref[1]

    @pl.when(pl.program_id(0) == 0)
    def _():
        turned[...] = att_ref[:, pl.ds(pl.multiple_of(half * depth, 128), depth)].T

    value = dot(turned[...], grad_ref[0])
    if summed:
        value = value + other_ref[0].astype(jnp.float32)
    out_ref[0] = value.astype(out_ref.dtype)


def qkv_grads(info, side, gradients, att_full, other=None, kind=jnp.bfloat16):
    _, frames, columns = gradients.shape
    depth = att_full.shape[1] // 2
    target = pl.BlockSpec((1, depth, columns), lambda c, *_: (c, 0, 0))
    return pl.pallas_call(
        partial(qkv_grad_kernel, side, other is not None),
        grid_spec=pltpu.PrefetchScalarGridSpec(
            num_scalar_prefetch=1,
            grid=(3,),
            in_specs=[pl.BlockSpec((1, frames, columns), lambda c, *_: (c, 0, 0)), whole(att_full)]
            + ([target] if other is not None else []),
            out_specs=target,
            scratch_shapes=[pltpu.VMEM((depth, frames), jnp.bfloat16)],
        ),
        out_shape=jax.ShapeDtypeStruct((3, depth, columns), kind),
        cost_estimate=pl.CostEstimate(
            flops=6 * frames * depth * columns, transcendentals=0, bytes_accessed=frames * depth * 6
        ),
        name="qkv_grads",
    )(info, gradients, att_full, *([other] if other is not None else []))


def inner_step(grads, first, second, weights, steps_done):
    first_new = beta_first * first + (1.0 - beta_first) * grads
    second_new = beta_second * second + (1.0 - beta_second) * grads * grads
    correct_one = 1.0 - beta_first**steps_done
    correct_two = 1.0 - beta_second**steps_done
    difference = inner_rate * (
        first_new / correct_one / (jnp.sqrt(second_new / correct_two) + adam_epsilon)
        + weight_decay * weights
    )
    return (first_new[None], second_new[None], difference)


def outer_step(average, outer, weights):
    outer_new = outer_beta * outer + average
    return (outer_new, weights - outer_rate * (average + outer_beta * outer_new))


def swapped(values, axis, bits):
    size = lax.axis_size(axis)
    return lax.ppermute(values, axis, [(i, i ^ bits) for i in range(size)])


def exchange(blocks, axis="tensor"):
    return [blocks[0]] + [swapped(blocks[r], axis, r) for r in range(1, 4)]


def after(values, *others):
    return lax.optimization_barrier((values, *others))[0]


def dp_rows(own):
    if lax.axis_size("dp") != 2:
        return lax.all_gather(own, "dp", axis=0, tiled=True)
    other = swapped(own, "dp", 1)
    first = lax.axis_index("dp") == 0
    return jnp.concatenate([jnp.where(first, own, other), jnp.where(first, other, own)], axis=0)


def dp_pair(own):
    if lax.axis_size("dp") == 2:
        return own, swapped(own, "dp", 1)
    return tuple(jnp.split(lax.all_gather(own, "dp", axis=1, tiled=True), 2, axis=1))


def quarter_of(half):
    quarter = half.shape[1] // 4
    return lax.dynamic_slice_in_dim(half, lax.axis_index("group") * quarter, quarter, 1)


def spread_wide(stack):
    one, two = swapped(stack, "group", 1), swapped(stack, "group", 2)
    return [stack, one, two, swapped(one[:2], "group", 2), swapped(two[2:], "group", 1)]


def group_parts(values):
    group = lax.axis_index("group")
    quarter = values.shape[1] // 4
    return exchange([lax.dynamic_slice_in_dim(values, (group ^ r) * quarter, quarter, 1) for r in range(4)], "group")


def add_parts(parts):
    return sum(part.astype(jnp.float32) for part in parts).astype(low)


def group_pieces(total):
    return exchange([total] * 4, "group")


def group_average(pieces):
    group = lax.axis_index("group")
    for bit in (1, 2):
        differs = (group & bit) == bit
        pieces = [jnp.where(differs, pieces[q ^ bit], pieces[q]) for q in range(4)]
    return jnp.concatenate(pieces, axis=1).astype(jnp.float32) / lax.axis_size("group")


def per_device(
    features,
    cotangent,
    frame_counts,
    buckets,
    step_count,
    col_weights,
    mod_weights,
    row_weights,
    col_first,
    col_second,
    mod_first,
    mod_second,
    row_first,
    row_second,
    col_outer,
    mod_outer,
    row_outer,
):
    group_count = lax.axis_size("group")
    packs_here = lax.axis_size("dp")
    own_rows, model_width = features.shape
    frames = own_rows * 4
    me = lax.axis_index("tensor")
    core = lax.axis_index("dp")
    group = lax.axis_index("group")
    count = buckets.shape[1]
    share = mod_weights.shape[0]
    width = col_weights.shape[2]

    def columns_first(values):
        return jnp.swapaxes(values, -3, -2)

    col_major = columns_first(col_weights).astype(low)
    wide_low = jnp.concatenate([row_weights.astype(low), col_major[3:5]], axis=0)
    halves = [wide_low] if packs_here == 2 else list(dp_pair(wide_low))
    stacks = [lax.all_gather(quarter_of(half), "tensor", axis=0) for half in halves]
    features_full = lax.all_gather(after(features, *stacks), "tensor", axis=0, tiled=True)

    buckets_all = dp_rows(buckets[0])
    flow_time = ((group * NBUCK + buckets_all).astype(jnp.float32) + 0.5) / (NBUCK * group_count)
    condition_all = jax.nn.silu(time_embedding(flow_time, model_width)).astype(low)
    condition_here = lax.dynamic_slice_in_dim(condition_all, core * share, share, 1)
    mod_terms = jnp.einsum("ud,dcj->cuj", condition_here, mod_weights.astype(low), preferred_element_type=jnp.float32)
    if packs_here != 2:
        mod_part = lax.psum_scatter(mod_terms, "dp", scatter_dimension=1, tiled=True)
    else:
        mod_away = lax.dynamic_slice_in_dim(mod_terms, (1 - core) * count, count, 1)
        mod_part = lax.dynamic_slice_in_dim(mod_terms, core * count, count, 1) + swapped(mod_away, "dp", 1)
    mod_pieces = exchange([mod_part] * 4)

    ending = jnp.cumsum(frame_counts[0]).astype(jnp.int32)
    half_core = core if packs_here == 2 else jnp.zeros_like(core)
    info = jnp.concatenate([jnp.stack([me, half_core, group]).astype(jnp.int32), ending])
    _, position = utterance_rows(ending, jnp.arange(frames, dtype=jnp.int32))
    cosine, sine = rotary_tables(position)
    ranges = key_ranges(ending, frames, own_rows)
    qkv_here, qkv_away = dp_pair(col_major[0:3])
    wide_sets = [spread_wide(stack) for stack in stacks]
    if packs_here == 2:
        wide_sets.append([swapped(piece, "dp", 1) for piece in wide_sets[0]])

    att_full, qkv, modulation, means, inverses = project(info, features_full, mod_pieces, qkv_here, qkv_away, cosine, sine)
    *mixed_pieces, log_totals = attend(info, ranges, qkv, count)
    mixed_pieces = exchange(mixed_pieces)

    (output, grad_residual, g0, g1, g2, g3, late_sums, ffn_in, hidden, grad_up, grad_attn, grad_ffn, mixed) = middle(
        info, features, cotangent, mixed_pieces, modulation, *wide_sets, count
    )
    def to_owners(sums):
        return sum(exchange([lax.dynamic_slice_in_dim(sums, (me ^ r) * width, width, 2) for r in range(4)]))

    def mod_gradient(sums):
        columns = dp_rows(jnp.swapaxes(sums, 0, 1))
        if packs_here != 2:
            return jnp.einsum("ud,ucj->cdj", condition_here.astype(jnp.float32), columns, precision=highest)
        total = 0.0
        for u in range(columns.shape[0]):
            total = total + condition_here[u].astype(jnp.float32)[None, :, None] * columns[u][:, None, :]
        return total

    def some_diff(grads, first, second, weights, some):
        state = [columns_first(a)[some] for a in (first[0], second[0], weights)]
        return inner_step(grads, *state, steps_done)[2].astype(low)

    steps_done = step_count[0].astype(jnp.float32)
    grad_pieces = exchange([g0, g1, g2, g3])
    late_sums = late_sums[:, :count]
    wide_args = (mixed, hidden, grad_up, grad_attn, grad_ffn, ffn_in)
    if packs_here == 2:
        wide_other = swapped(wide_grads(info, 1, *wide_args), "dp", 1)
        late_sums = to_owners(after(late_sums, wide_other))
        wide_other, *grad_pieces = lax.optimization_barrier((wide_other, *grad_pieces))
        wide_blocks = wide_grads(info, 0, *wide_args, other=wide_other)
    else:
        both = jnp.concatenate([wide_grads(info, side, *wide_args) for side in range(2)], axis=2).astype(jnp.float32)
        wide_blocks = lax.psum_scatter(both, "dp", scatter_dimension=2, tiled=True).astype(low)
        late_sums = to_owners(late_sums)
    wide_grad = lax.psum_scatter(wide_blocks, "tensor", scatter_dimension=0, tiled=False)

    late_mod = mod_gradient(after(late_sums, wide_blocks))
    first_parts = group_parts(some_diff(late_mod, mod_first, mod_second, mod_weights, slice(2, 6)))
    attended = attend_back(
        info, ranges, qkv, grad_pieces, log_totals, cosine, sine, qkv_here, qkv_away, features_full, means, inverses, count
    )
    gradients, att_part, early_sums, *first_parts = lax.optimization_barrier((*attended, *first_parts))
    grad_att_in = lax.psum_scatter(after(att_part, wide_blocks), "tensor", scatter_dimension=0, tiled=True)
    first_pieces = group_pieces(add_parts(first_parts))
    early_mod = mod_gradient(to_owners(early_sums[:, :count]))
    if packs_here == 2:
        qkv_away_grad = swapped(qkv_grads(info, 1, gradients, att_full), "dp", 1)
        qkv_away_grad, *first_pieces = lax.optimization_barrier((qkv_away_grad, *first_pieces))
        qkv_share = qkv_grads(info, 0, gradients, att_full, other=qkv_away_grad, kind=jnp.float32)
    else:
        both = [qkv_grads(info, side, gradients, att_full, kind=jnp.float32) for side in range(2)]
        qkv_share = lax.psum_scatter(jnp.concatenate(both, axis=1), "dp", scatter_dimension=1, tiled=True)
    second_parts = group_parts(
        jnp.concatenate(
            [
                some_diff(qkv_share, col_first, col_second, col_weights, slice(0, 3)),
                some_diff(early_mod, mod_first, mod_second, mod_weights, slice(0, 2)),
            ],
            axis=0,
        )
    )

    row_first_new, row_second_new, row_diff = inner_step(
        wide_grad[0:3].astype(jnp.float32), row_first[0], row_second[0], row_weights, steps_done
    )
    col_first_new, col_second_new, col_diff = inner_step(
        columns_first(jnp.concatenate([qkv_share, wide_grad[3:5].astype(jnp.float32)], axis=0)), col_first[0], col_second[0], col_weights, steps_done
    )
    wide_diff = jnp.concatenate([row_diff.astype(low), columns_first(col_diff)[3:5].astype(low)], axis=0)
    wide_diff, *second_parts = lax.optimization_barrier((wide_diff, *second_parts))
    third_parts = group_parts(wide_diff)
    second_sum = add_parts(second_parts)
    second_pieces = group_pieces(second_sum)
    mod_first_new, mod_second_new, _ = inner_step(
        columns_first(jnp.concatenate(lax.optimization_barrier((early_mod, late_mod, second_pieces[1]))[:2], axis=0)),
        mod_first[0],
        mod_second[0],
        mod_weights,
        steps_done,
    )
    own_bounds, own_means, own_inverses, _ = lax.optimization_barrier((ending, means, inverses, second_pieces[1]))
    number_own, _ = utterance_rows(own_bounds, me * own_rows + jnp.arange(own_rows, dtype=jnp.int32))
    own_mean, inverse_scale = (
        lax.dynamic_slice_in_dim(a, me * own_rows, own_rows, 0)[:, 0] for a in (own_means, own_inverses)
    )
    both = lax.optimization_barrier(
        (*second_pieces, *third_parts, number_own, own_mean, inverse_scale, mod_first_new, mod_second_new)
    )
    second_pieces, third_parts = both[:4], both[4:8]
    number_own, own_mean, inverse_scale, mod_first_new, mod_second_new = both[8:]
    third_sum = add_parts(third_parts)
    third_pieces = group_pieces(third_sum)
    first_pieces = lax.optimization_barrier((*first_pieces, third_sum))[:4]
    first_average, second_average = group_average(first_pieces), group_average(second_pieces)
    mod_average = columns_first(jnp.concatenate([second_average[3:5], first_average], axis=0))
    mod_outer_new, mod_new = outer_step(mod_average, mod_outer, mod_weights)
    grad_att_in = after(grad_att_in, third_sum, mod_new).astype(jnp.float32)
    normed = (features.astype(jnp.float32) - own_mean[:, None]) * inverse_scale[:, None]
    grad_features = grad_residual + normalize_back(
        grad_att_in * (1.0 + by_utterance(number_own[:, None], modulation[1, :count])), normed, inverse_scale[:, None]
    )
    third_pieces = lax.optimization_barrier((*third_pieces, mod_average, mod_outer_new, mod_new, grad_features))[:4]
    third_average = group_average(third_pieces)
    row_average = third_average[0:3]
    col_average = columns_first(jnp.concatenate([second_average[0:3], third_average[3:5]], axis=0))
    col_outer_new, col_new = outer_step(col_average, col_outer, col_weights)
    row_outer_new, row_new = outer_step(row_average, row_outer, row_weights)

    return (
        output,
        grad_features,
        col_first_new,
        col_second_new,
        col_average,
        col_outer_new,
        col_new,
        mod_first_new,
        mod_second_new,
        mod_average,
        mod_outer_new,
        mod_new,
        row_first_new,
        row_second_new,
        row_average,
        row_outer_new,
        row_new,
    )


def solution(mesh):
    placed = (
        P(("group", "dp", "tensor"), None),
        P(("group", "dp", "tensor"), None),
        P(("group", "dp"), None),
        P(("group", "dp"), None),
        P(),
        P("dp", None, "tensor"),
        P("dp", None, "tensor"),
        P(None, "dp", "tensor"),
        P("group", "dp", None, "tensor"),
        P("group", "dp", None, "tensor"),
        P("group", "dp", None, "tensor"),
        P("group", "dp", None, "tensor"),
        P("group", None, "dp", "tensor"),
        P("group", None, "dp", "tensor"),
        P("dp", None, "tensor"),
        P("dp", None, "tensor"),
        P(None, "dp", "tensor"),
    )
    return jax.shard_map(
        per_device,
        mesh=mesh,
        in_specs=placed,
        out_specs=(
            P(("group", "dp", "tensor"), None),
            P(("group", "dp", "tensor"), None),
            P("group", "dp", None, "tensor"),
            P("group", "dp", None, "tensor"),
            P("dp", None, "tensor"),
            P("dp", None, "tensor"),
            P("dp", None, "tensor"),
            P("group", "dp", None, "tensor"),
            P("group", "dp", None, "tensor"),
            P("dp", None, "tensor"),
            P("dp", None, "tensor"),
            P("dp", None, "tensor"),
            P("group", None, "dp", "tensor"),
            P("group", None, "dp", "tensor"),
            P(None, "dp", "tensor"),
            P(None, "dp", "tensor"),
            P(None, "dp", "tensor"),
        ),
        check_vma=False,
    )
```

```python
from functools import partial
import math

import jax
import jax.numpy as jnp
from jax import lax
from jax.experimental import pallas as pl
from jax.experimental.pallas import tpu as pltpu
from jax.sharding import PartitionSpec as P

HEAD_DIM = 64
NBUCK = 8
BLOCK = 256
BOUNDS = 3

highest = lax.Precision.HIGHEST
norm_epsilon = 1e-06
adam_epsilon = 1e-08
beta_first = 0.9
beta_second = 0.999
inner_rate = 0.05
weight_decay = 0.01
outer_rate = 0.7
outer_beta = 0.9
low = jnp.bfloat16


def time_embedding(flow_time, width_all):
    half_width = width_all // 2
    frequency = jnp.exp(
        jnp.arange(half_width, dtype=jnp.float32) * (-math.log(10000.0) / (half_width - 1))
    )
    angles = 1000.0 * flow_time[:, None] * frequency[None, :]
    return jnp.concatenate([jnp.sin(angles), jnp.cos(angles)], axis=1)


def utterance_rows(ending, indices):
    number = jnp.zeros(indices.shape, jnp.int32)
    begin = jnp.zeros(indices.shape, jnp.int32)
    for u in range(ending.shape[0] - 1):
        after = indices >= ending[u]
        number = number + after.astype(jnp.int32)
        begin = jnp.where(after, ending[u], begin)
    return number, indices - begin


def rotary_tables(position):
    half_width = HEAD_DIM // 2
    frequency = jnp.exp(
        jnp.arange(half_width, dtype=jnp.float32) * (-2.0 * math.log(10000.0) / HEAD_DIM)
    )
    angles = position.astype(jnp.float32)[:, None] * frequency[None, :]
    cosine, sine = jnp.cos(angles), jnp.sin(angles)
    return jnp.concatenate([cosine] * 4, axis=1), jnp.concatenate([-sine, sine, -sine, sine], axis=1)


def normalize_back(grads, normed, inverse_scale):
    return inverse_scale * (
        grads
        - jnp.mean(grads, axis=-1, keepdims=True)
        - normed * jnp.mean(grads * normed, axis=-1, keepdims=True)
    )


def turn(values, cosine, signed_sine):
    lanes = lax.broadcasted_iota(jnp.int32, values.shape, 1)
    swapped = jnp.where(lanes % 64 < 32, pltpu.roll(values, 96, 1), pltpu.roll(values, 32, 1))
    return values * cosine + swapped * signed_sine


def utterance_of(indices, info_ref, count):
    number = jnp.zeros(indices.shape, jnp.int32)
    for u in range(count - 1):
        number = number + (indices >= info_ref[BOUNDS + u]).astype(jnp.int32)
    return number


def by_utterance(number, table):
    out = table[0:1, :]
    for u in range(1, table.shape[0]):
        out = jnp.where(number >= u, table[u : u + 1, :], out)
    return out


def dot_rows(a, b):
    return lax.dot_general(a, b, (((1,), (1,)), ((), ())), preferred_element_type=jnp.float32)


def dot(a, b):
    return jnp.dot(a, b, preferred_element_type=jnp.float32)


def spread(values):
    centered = values - jnp.mean(values, axis=-1, keepdims=True)
    inverse = lax.rsqrt(jnp.mean(centered * centered, axis=-1, keepdims=True) + norm_epsilon)
    return centered * inverse, inverse


def over_rows(total, chunk, body):
    def step(i, carry):
        body(pl.ds(pl.multiple_of(i * chunk, chunk), chunk), i * chunk)
        return carry

    lax.fori_loop(0, total // chunk, step, 0)


def whole(a):
    shape = a.shape
    return pl.BlockSpec(shape, lambda *_: (0,) * len(shape))


def project_kernel(
    count, info_ref, x_ref, m0_ref, m1_ref, m2_ref, m3_ref, here_ref, away_ref, cos_ref, sin_ref, att_ref, qkv_ref, mod_ref,
    mean_ref, inverse_ref
):
    step = pl.program_id(0)
    me, core = info_ref[0], info_ref[1]
    size = x_ref.shape[0]
    width = m0_ref.shape[2]

    @pl.when(step == 0)
    def _():
        mod_ref[...] = jnp.zeros_like(mod_ref)
        for r, piece in enumerate((m0_ref, m1_ref, m2_ref, m3_ref)):
            at = pl.ds(pl.multiple_of(jnp.bitwise_xor(me, r) * width, 128), width)
            mod_ref[:, 0:count, at] = piece[...]

    chunk = 64

    def norm(at, first):
        values = x_ref[at, :].astype(jnp.float32)
        mean = jnp.mean(values, axis=-1, keepdims=True)
        centered = values - mean
        inverse = lax.rsqrt(jnp.mean(centered * centered, axis=-1, keepdims=True) + norm_epsilon)
        normed = centered * inverse
        mean_ref[at, :] = jnp.broadcast_to(mean, (chunk, 128))
        inverse_ref[at, :] = jnp.broadcast_to(inverse, (chunk, 128))
        number = utterance_of(
            lax.broadcasted_iota(jnp.int32, (chunk, 1), 0) + step * size + first, info_ref, count
        )
        shift, scale = by_utterance(number, mod_ref[0, 0:count, :]), by_utterance(number, mod_ref[1, 0:count, :])
        att_ref[at, :] = (normed * (1.0 + scale) + shift).astype(jnp.bfloat16)

    over_rows(size, chunk, norm)
    depth = here_ref.shape[1]
    near = att_ref[:, pl.ds(pl.multiple_of(core * depth, 128), depth)]
    far = att_ref[:, pl.ds(pl.multiple_of((1 - core) * depth, 128), depth)]
    for c in range(3):
        values = dot(near, here_ref[c]) + dot(far, away_ref[c])
        if c < 2:
            for p in range(values.shape[1] // 128):
                lanes = slice(128 * p, 128 * p + 128)
                turned = turn(values[:, lanes], cos_ref[...], sin_ref[...])
                qkv_ref[c, :, lanes] = (turned * 0.125 if c == 0 else turned).astype(jnp.bfloat16)
        else:
            qkv_ref[c] = values.astype(jnp.bfloat16)


def project(info, features_full, mod_pieces, here, away, cosine, sine):
    frames, model_width = features_full.shape
    size = frames // 4
    cycles, count, width = mod_pieces[0].shape
    columns = here.shape[2]
    rows = lambda i, *_: (i, 0)
    return pl.pallas_call(
        partial(project_kernel, count),
        grid_spec=pltpu.PrefetchScalarGridSpec(
            num_scalar_prefetch=1,
            grid=(4,),
            in_specs=[pl.BlockSpec((size, model_width), rows)]
            + [whole(a) for a in (*mod_pieces, here, away)]
            + [pl.BlockSpec((size, 128), rows)] * 2,
            out_specs=[
                pl.BlockSpec((size, model_width), rows),
                pl.BlockSpec((3, size, columns), lambda i, *_: (0, i, 0)),
                pl.BlockSpec((cycles, 8, model_width), lambda *_: (0, 0, 0)),
            ]
            + [pl.BlockSpec((size, 128), rows)] * 2,
        ),
        out_shape=[
            jax.ShapeDtypeStruct((frames, model_width), jnp.bfloat16),
            jax.ShapeDtypeStruct((3, frames, columns), jnp.bfloat16),
            jax.ShapeDtypeStruct((cycles, 8, model_width), jnp.float32),
        ]
        + [jax.ShapeDtypeStruct((frames, 128), jnp.float32)] * 2,
        cost_estimate=pl.CostEstimate(
            flops=6 * frames * model_width * columns, transcendentals=0, bytes_accessed=frames * model_width * 6
        ),
        name="project",
    )(info, features_full, *mod_pieces, here, away, cosine, sine)


def forward_kernel(count, info_ref, range_ref, qkv_ref, out0, out1, out2, out3, log_ref, value_t, scores):
    block = pl.program_id(0)
    _, frames, columns = qkv_ref.shape
    size = out0.shape[0]
    pairs = columns // 128
    heads = 2 * pairs

    @pl.when(block == 0)
    def _():
        def rows(i, carry):
            at = pl.ds(pl.multiple_of(i * BLOCK, BLOCK), BLOCK)
            value_t[:, at] = qkv_ref[2, at, :].T
            return carry

        lax.fori_loop(0, frames // BLOCK, rows, 0)

    here = pl.ds(pl.multiple_of(block * size, 128), size)
    query_t = qkv_ref[0, here, :].T
    head_of = lax.broadcasted_iota(jnp.int32, (128, size), 0) < HEAD_DIM
    zero = jnp.zeros((128, size), jnp.bfloat16)
    query_heads = []
    for p in range(pairs):
        part = query_t[128 * p : 128 * p + 128]
        query_heads += [jnp.where(head_of, part, zero), jnp.where(head_of, zero, part)]
    own = utterance_of(lax.broadcasted_iota(jnp.int32, (1, size), 1) + block * size, info_ref, count)
    begin, end = range_ref[0, block], range_ref[1, block]

    def score(i, tops):
        at = pl.ds(pl.multiple_of(i * BLOCK, BLOCK), BLOCK)
        theirs = utterance_of(lax.broadcasted_iota(jnp.int32, (BLOCK, 1), 0) + i * BLOCK, info_ref, count)
        same = theirs == own
        out = []
        for h in range(heads):
            keys = qkv_ref[1, at, 128 * (h // 2) : 128 * (h // 2) + 128]
            s = jnp.dot(keys, query_heads[h], preferred_element_type=jnp.float32)
            s = jnp.where(same, s, -1e30)
            scores[h, at, :] = s
            out.append(jnp.maximum(tops[h], jnp.max(s, axis=0, keepdims=True)))
        return tuple(out)

    lowest = jnp.full((1, size), -1e30, jnp.float32)
    tops = lax.fori_loop(begin, end, score, (lowest,) * heads)

    def weigh(i, carry):
        at = pl.ds(pl.multiple_of(i * BLOCK, BLOCK), BLOCK)
        out = []
        for h in range(heads):
            total, mixed = carry[h]
            p = jnp.exp(scores[h, at, :] - tops[h])
            total = total + jnp.sum(p, axis=0, keepdims=True)
            mixed = mixed + jnp.dot(
                value_t[h * HEAD_DIM : (h + 1) * HEAD_DIM, at], p.astype(jnp.bfloat16), preferred_element_type=jnp.float32
            )
            out.append((total, mixed))
        return tuple(out)

    start = (jnp.zeros((1, size), jnp.float32), jnp.zeros((HEAD_DIM, size), jnp.float32))
    sums = lax.fori_loop(begin, end, weigh, (start,) * heads)
    mixed = jnp.concatenate([sums[h][1] / sums[h][0] for h in range(heads)], axis=0).T.astype(jnp.bfloat16)
    relative = jnp.bitwise_xor(block, info_ref[0])
    for r, out in enumerate((out0, out1, out2, out3)):

        @pl.when(relative == r)
        def _():
            out[...] = mixed

    for h in range(heads):
        log_ref[h : h + 1, here] = tops[h] + jnp.log(sums[h][0])


def backward_kernel(
    count, info_ref, range_ref, qkv_ref, grad0, grad1, grad2, grad3, log_ref, cos_ref, sin_ref, here_ref, away_ref,
    x_ref, mean_ref, inverse_ref, out_ref, part_ref, sums_ref, key_t, key_sum, value_sum, probs,
    grads, grad_ref, total_ref
):
    block = pl.program_id(0)
    _, frames, columns = qkv_ref.shape
    size = grad0.shape[0]
    pairs = columns // 128
    heads = 2 * pairs

    @pl.when(block == 0)
    def _():
        key_sum[...] = jnp.zeros_like(key_sum)
        value_sum[...] = jnp.zeros_like(value_sum)

        def rows(i, carry):
            at = pl.ds(pl.multiple_of(i * BLOCK, BLOCK), BLOCK)
            key_t[:, at] = qkv_ref[1, at, :].T
            return carry

        lax.fori_loop(0, frames // BLOCK, rows, 0)

    here = pl.ds(pl.multiple_of(block * size, 128), size)
    relative = jnp.bitwise_xor(block, info_ref[0])
    for r, piece in enumerate((grad0, grad1, grad2, grad3)):

        @pl.when(relative == r)
        def _():
            grad_ref[...] = piece[...]

    upper_t = lax.broadcasted_iota(jnp.int32, (128, size), 0) < HEAD_DIM
    upper = lax.broadcasted_iota(jnp.int32, (size, 128), 1) < HEAD_DIM
    zero_t, zero = jnp.zeros((128, size), jnp.bfloat16), jnp.zeros((size, 128), jnp.bfloat16)
    query_ts, grad_ts, queries, grad_heads = [], [], [], []
    for p in range(pairs):
        query = qkv_ref[0, here, 128 * p : 128 * p + 128]
        grad = grad_ref[:, 128 * p : 128 * p + 128]
        query_t, grad_t = query.T, grad.T
        query_ts += [jnp.where(upper_t, query_t, zero_t), jnp.where(upper_t, zero_t, query_t)]
        grad_ts += [jnp.where(upper_t, grad_t, zero_t), jnp.where(upper_t, zero_t, grad_t)]
        queries += [jnp.where(upper, query, zero), jnp.where(upper, zero, query)]
        grad_heads += [jnp.where(upper, grad, zero), jnp.where(upper, zero, grad)]
    own = utterance_of(lax.broadcasted_iota(jnp.int32, (1, size), 1) + block * size, info_ref, count)
    begin, end = range_ref[0, block], range_ref[1, block]
    logs = [log_ref[h : h + 1, here] for h in range(heads)]

    def first(i, deltas):
        at = pl.ds(pl.multiple_of(i * BLOCK, BLOCK), BLOCK)
        theirs = utterance_of(lax.broadcasted_iota(jnp.int32, (BLOCK, 1), 0) + i * BLOCK, info_ref, count)
        same = theirs == own
        out = []
        for h in range(heads):
            lanes = slice(128 * (h // 2), 128 * (h // 2) + 128)
            s = jnp.dot(qkv_ref[1, at, lanes], query_ts[h], preferred_element_type=jnp.float32)
            p = jnp.exp(jnp.where(same, s, -1e30) - logs[h])
            g = jnp.dot(qkv_ref[2, at, lanes], grad_ts[h], preferred_element_type=jnp.float32)
            probs[h, at, :] = p
            grads[h, at, :] = g
            out.append(deltas[h] + jnp.sum(p * g, axis=0, keepdims=True))
        return tuple(out)

    none = jnp.zeros((1, size), jnp.float32)
    deltas = lax.fori_loop(begin, end, first, (none,) * heads)

    def second(i, sums):
        at = pl.ds(pl.multiple_of(i * BLOCK, BLOCK), BLOCK)
        out = []
        for p in range(pairs):
            lanes = slice(128 * p, 128 * p + 128)
            key_add, value_add = key_sum[at, lanes], value_sum[at, lanes]
            for h in (2 * p, 2 * p + 1):
                weight = probs[h, at, :]
                ds = (weight * (grads[h, at, :] - deltas[h])).astype(jnp.bfloat16)
                out.append(
                    sums[h]
                    + jnp.dot(key_t[h * HEAD_DIM : (h + 1) * HEAD_DIM, at], ds, preferred_element_type=jnp.float32)
                )
                key_add = key_add + jnp.dot(ds, queries[h], preferred_element_type=jnp.float32)
                value_add = value_add + jnp.dot(
                    weight.astype(jnp.bfloat16), grad_heads[h], preferred_element_type=jnp.float32
                )
            key_sum[at, lanes] = key_add
            value_sum[at, lanes] = value_add
        return tuple(out)

    zero_sum = jnp.zeros((HEAD_DIM, size), jnp.float32)
    sums = lax.fori_loop(begin, end, second, (zero_sum,) * heads)
    grad_query = jnp.concatenate(sums, axis=0).T * 0.125
    for p in range(pairs):
        lanes = slice(128 * p, 128 * p + 128)
        out_ref[0, here, lanes] = turn(grad_query[:, lanes], cos_ref[here, :], -sin_ref[here, :]).astype(jnp.bfloat16)

    @pl.when(block == pl.num_programs(0) - 1)
    def _():
        def rows(i, carry):
            at = pl.ds(pl.multiple_of(i * BLOCK, BLOCK), BLOCK)
            for p in range(pairs):
                lanes = slice(128 * p, 128 * p + 128)
                out_ref[1, at, lanes] = turn(key_sum[at, lanes], cos_ref[at, :], -sin_ref[at, :]).astype(jnp.bfloat16)
            out_ref[2, at, :] = value_sum[at, :].astype(jnp.bfloat16)
            return carry

        lax.fori_loop(0, frames // BLOCK, rows, 0)
        depth = here_ref.shape[1]
        chunk = 64
        sums_ref[...] = jnp.zeros_like(sums_ref)

        def share(i, carry):
            base = i * size
            at = pl.ds(pl.multiple_of(base, 128), size)
            for side, weight in ((info_ref[1], here_ref), (1 - info_ref[1], away_ref)):
                total = dot_rows(out_ref[0, at, :], weight[0])
                for c in (1, 2):
                    total = total + dot_rows(out_ref[c, at, :], weight[c])
                total_ref[:, pl.ds(pl.multiple_of(side * depth, 128), depth)] = total

            def add(own, first):
                start = base + first
                rows = pl.ds(pl.multiple_of(start, chunk), chunk)
                grad_in = total_ref[own, :]
                part_ref[rows, :] = grad_in.astype(part_ref.dtype)
                normed = (x_ref[rows, :].astype(jnp.float32) - mean_ref[rows, 0:1]) * inverse_ref[rows, 0:1]
                index = lax.broadcasted_iota(jnp.int32, (chunk, 1), 0) + start
                for u in range(count):
                    begin = info_ref[BOUNDS + u - 1] if u else 0
                    end = info_ref[BOUNDS + u]

                    @pl.when((begin < start + chunk) & (end > start))
                    def _():
                        chosen = jnp.where((index >= begin) & (index < end), grad_in, 0.0)
                        sums_ref[0, u : u + 1, :] += jnp.sum(chosen, axis=0, keepdims=True)
                        sums_ref[1, u : u + 1, :] += jnp.sum(chosen * normed, axis=0, keepdims=True)

            over_rows(size, chunk, add)
            return carry

        lax.fori_loop(0, frames // size, share, 0)


def key_ranges(ending, frames, size):
    starting = jnp.concatenate([jnp.zeros((1,), jnp.int32), ending[:-1]])
    begins = jnp.arange(frames // size, dtype=jnp.int32) * size
    first_key = jnp.min(jnp.where(ending[None, :] > begins[:, None], starting[None, :], frames), axis=1)
    last_key = jnp.max(jnp.where(starting[None, :] < begins[:, None] + size, ending[None, :], 0), axis=1)
    return jnp.stack([first_key // BLOCK, (last_key + BLOCK - 1) // BLOCK]).astype(jnp.int32)


def attend(info, ranges, qkv, count):
    _, frames, columns = qkv.shape
    heads = columns // HEAD_DIM
    size = frames // 4
    flat = lambda b, *_: (0, 0)
    return pl.pallas_call(
        partial(forward_kernel, count),
        grid_spec=pltpu.PrefetchScalarGridSpec(
            num_scalar_prefetch=2,
            grid=(4,),
            in_specs=[pl.BlockSpec((3, frames, columns), lambda b, *_: (0, 0, 0))],
            out_specs=[pl.BlockSpec((size, columns), flat)] * 4 + [pl.BlockSpec((heads, frames), flat)],
            scratch_shapes=[
                pltpu.VMEM((columns, frames), jnp.bfloat16),
                pltpu.VMEM((heads, frames, size), jnp.float32),
            ],
        ),
        out_shape=[jax.ShapeDtypeStruct((size, columns), jnp.bfloat16)] * 4
        + [jax.ShapeDtypeStruct((heads, frames), jnp.float32)],
        cost_estimate=pl.CostEstimate(
            flops=8 * frames * frames * columns, transcendentals=heads * frames * frames, bytes_accessed=frames * columns * 8
        ),
        name="attend",
    )(info, ranges, qkv)


def attend_back(info, ranges, qkv, grad_pieces, logs, cosine, sine, here, away, features_full, means, inverses, count):
    _, frames, columns = qkv.shape
    model_width = features_full.shape[1]
    heads = columns // HEAD_DIM
    size = frames // 4
    cube = lambda b, *_: (0, 0, 0)
    flat = lambda b, *_: (0, 0)
    return pl.pallas_call(
        partial(backward_kernel, count),
        grid_spec=pltpu.PrefetchScalarGridSpec(
            num_scalar_prefetch=2,
            grid=(4,),
            in_specs=[pl.BlockSpec((3, frames, columns), cube)]
            + [pl.BlockSpec((size, columns), flat)] * 4
            + [pl.BlockSpec((heads, frames), flat), pl.BlockSpec((frames, 128), flat), pl.BlockSpec((frames, 128), flat)]
            + [whole(a) for a in (here, away, features_full, means, inverses)],
            out_specs=[pl.BlockSpec((3, frames, columns), cube)]
            + [pl.BlockSpec((frames, model_width), flat)]
            + [pl.BlockSpec((2, 8, model_width), cube)],
            scratch_shapes=[
                pltpu.VMEM((columns, frames), jnp.bfloat16),
                pltpu.VMEM((frames, columns), jnp.float32),
                pltpu.VMEM((frames, columns), jnp.float32),
                pltpu.VMEM((heads, frames, size), jnp.float32),
                pltpu.VMEM((heads, frames, size), jnp.float32),
                pltpu.VMEM((size, columns), jnp.bfloat16),
                pltpu.VMEM((size, model_width), jnp.float32),
            ],
        ),
        out_shape=[jax.ShapeDtypeStruct((3, frames, columns), jnp.bfloat16)]
        + [jax.ShapeDtypeStruct((frames, model_width), jnp.bfloat16)]
        + [jax.ShapeDtypeStruct((2, 8, model_width), jnp.float32)],
        cost_estimate=pl.CostEstimate(
            flops=16 * frames * frames * columns, transcendentals=heads * frames * frames, bytes_accessed=frames * columns * 20
        ),
        name="attend_back",
    )(info, ranges, qkv, *grad_pieces, logs, cosine, sine, here, away, features_full, means, inverses)


def middle_kernel(
    count, info_ref, x_ref, cot_ref, mixed0, mixed1, mixed2, mixed3, mod_ref, *refs
):
    pieces = refs[:10]
    out_ref, res_ref, g0, g1, g2, g3, sums_ref, ffn_in_ref, hidden_ref, grad_up_ref, grad_attn_ref, grad_ffn_ref = refs[10:22]
    mixed, wide, residual, attn, up, ffn, inverse, sems = refs[22:]
    me, core, group = info_ref[0], info_ref[1], info_ref[2]
    size = x_ref.shape[0]
    width = mixed0.shape[1]
    quarter = pieces[0].shape[2]
    depth = 4 * quarter

    copies = ([], [])
    for side in range(2):
        half = core if side == 0 else 1 - core
        for k, r in [(k, r) for k in range(4) for r in range(4)]:
            if k < 3:
                piece = pieces[5 * side + k].at[r]
            else:
                piece = pieces[5 * side + 3 + r // 2].at[r % 2]
            at = pl.ds(pl.multiple_of(half * depth + jnp.bitwise_xor(group, k) * quarter, 16), quarter)
            lanes = pl.ds(pl.multiple_of(jnp.bitwise_xor(me, r) * width, 128), width)
            for part, cs in enumerate((slice(0, 1), slice(1, 5))):
                copy = pltpu.make_async_copy(
                    piece.at[cs], wide.at[cs, at, lanes], sems.at[part * 32 + side * 16 + k * 4 + r]
                )
                copies[part].append(copy)
    for copy in copies[0] + copies[1]:
        copy.start()
    for r, piece in enumerate((mixed0, mixed1, mixed2, mixed3)):
        mixed[:, r * width : (r + 1) * width] = piece[...]
    chunk = 64

    def table(c, number):
        return by_utterance(number, mod_ref[c, 0:count, :])

    def numbers(first):
        return utterance_of(lax.broadcasted_iota(jnp.int32, (chunk, 1), 0) + me * size + first, info_ref, count)

    for copy in copies[0]:
        copy.wait()
    attn[...] = dot_rows(mixed[...], wide[0])

    def enter(at, first):
        number = numbers(first)
        value = x_ref[at, :].astype(jnp.float32) + table(2, number) * attn[at, :]
        residual[at, :] = value
        normed, scale = spread(value)
        inverse[at, :] = jnp.broadcast_to(scale, (chunk, 128))
        ffn[at, :] = normed
        ffn_in_ref[at, :] = (normed * (1.0 + table(4, number)) + table(3, number)).astype(jnp.bfloat16)
        grad_ffn_ref[at, :] = (cot_ref[at, :].astype(jnp.float32) * table(5, number)).astype(jnp.bfloat16)

    over_rows(size, chunk, enter)
    for copy in copies[1]:
        copy.wait()
    for c in range(2):
        up[c] = dot(ffn_in_ref[...], wide[3 + c])

    root = math.sqrt(2.0 / math.pi)

    def act(at, first):
        for c in range(2):
            value = up[c, at, :]
            square = value * value
            bend = jnp.tanh(root * (value + 0.044715 * (value * square)))
            hidden_ref[c, at, :] = (0.5 * value * (1.0 + bend)).astype(jnp.bfloat16)
            up[c, at, :] = 0.5 * (1.0 + bend) + 0.5 * value * (1.0 - bend * bend) * (root * (1.0 + 0.134145 * square))

    over_rows(size, chunk, act)
    grad_hidden = [dot(grad_ffn_ref[...], wide[1 + c]) for c in range(2)]
    for c in range(2):
        grad_up_ref[c] = (up[c] * grad_hidden[c]).astype(jnp.bfloat16)
    up[0] = dot_rows(hidden_ref[0], wide[1]) + dot_rows(hidden_ref[1], wide[2])
    up[1] = dot_rows(grad_up_ref[0], wide[3]) + dot_rows(grad_up_ref[1], wide[4])
    sums_ref[...] = jnp.zeros_like(sums_ref)

    def leave(at, first):
        number = numbers(first)
        cot = cot_ref[at, :].astype(jnp.float32)
        ffn_out, grad_in, normed = up[0, at, :], up[1, at, :], ffn[at, :]
        out_ref[at, :] = (residual[at, :] + table(5, number) * ffn_out).astype(jnp.bfloat16)
        h = grad_in * (1.0 + table(4, number))
        grad = cot + inverse[at, 0:1] * (
            h - jnp.mean(h, axis=-1, keepdims=True) - normed * jnp.mean(h * normed, axis=-1, keepdims=True)
        )
        res_ref[at, :] = grad
        grad_attn_ref[at, :] = (grad * table(2, number)).astype(jnp.bfloat16)
        for c, rows in enumerate((grad * attn[at, :], grad_in, grad_in * normed, cot * ffn_out)):
            for u in range(count):
                sums_ref[c, u : u + 1, :] += jnp.sum(jnp.where(number == u, rows, 0.0), axis=0, keepdims=True)

    over_rows(size, chunk, leave)
    grad_mixed = dot(grad_attn_ref[...], wide[0]).astype(jnp.bfloat16)
    for r, piece in enumerate((g0, g1, g2, g3)):
        piece[...] = grad_mixed[:, r * width : (r + 1) * width]


def middle(info, features, cotangent, mixed_pieces, modulation, wide_here, wide_away, count):
    size, model_width = features.shape
    width = mixed_pieces[0].shape[1]
    pieces = (*wide_here, *wide_away)
    shapes = [
        ((size, model_width), jnp.bfloat16),
        ((size, model_width), jnp.float32),
        *[((size, width), jnp.bfloat16)] * 4,
        ((4, 8, model_width), jnp.float32),
        ((size, model_width), jnp.bfloat16),
        ((2, size, 4 * width), jnp.bfloat16),
        ((2, size, 4 * width), jnp.bfloat16),
        ((size, model_width), jnp.bfloat16),
        ((size, model_width), jnp.bfloat16),
        ((size, 4 * width), jnp.bfloat16),
    ]
    outs = [jax.ShapeDtypeStruct(shape, kind) for shape, kind in shapes]
    return pl.pallas_call(
        partial(middle_kernel, count),
        grid_spec=pltpu.PrefetchScalarGridSpec(
            num_scalar_prefetch=1,
            grid=(1,),
            in_specs=[whole(a) for a in (features, cotangent, *mixed_pieces, modulation)]
            + [pl.BlockSpec(memory_space=pl.ANY)] * 10,
            out_specs=[whole(a) for a in outs],
            scratch_shapes=[
                pltpu.VMEM((5, model_width, 4 * width), jnp.bfloat16),
                pltpu.VMEM((size, model_width), jnp.float32),
                pltpu.VMEM((size, model_width), jnp.float32),
                pltpu.VMEM((2, size, 4 * width), jnp.float32),
                pltpu.VMEM((size, model_width), jnp.float32),
                pltpu.VMEM((size, 128), jnp.float32),
                pltpu.SemaphoreType.DMA((64,)),
            ],
        ),
        out_shape=outs,
        cost_estimate=pl.CostEstimate(
            flops=20 * size * model_width * 4 * width, transcendentals=size * 8 * width, bytes_accessed=10 * model_width * 4 * width
        ),
        name="middle",
    )(info, features, cotangent, *mixed_pieces, modulation, *pieces)


def wide_grad_kernel(side, summed, info_ref, mixed_ref, hidden_ref, grad_up_ref, *refs):
    grad_refs, other_ref, out_ref, turned = refs[:3], refs[3] if summed else None, refs[-2], refs[-1]
    depth = out_ref.shape[2]
    half = info_ref[1] if side == 0 else 1 - info_ref[1]

    @pl.when(pl.program_id(0) == 0)
    def _():
        at = pl.ds(pl.multiple_of(half * depth, 128), depth)
        for i in range(3):
            turned[i] = grad_refs[i][:, at].T

    def block(c):
        if c == 0:
            return dot(turned[0], mixed_ref[...])
        if c < 3:
            return dot(turned[1], hidden_ref[c - 1])
        return dot(turned[2], grad_up_ref[c - 3])

    for c in range(5):
        value = block(c)
        if summed:
            value = value + other_ref[0, c].astype(jnp.float32)
        out_ref[0, c] = value.astype(jnp.bfloat16)


def wide_grads(info, side, mixed, hidden, grad_up, grad_attn, grad_ffn, ffn_in, other=None):
    size, width = mixed.shape[0], mixed.shape[1] // 4
    depth = grad_attn.shape[1] // 2
    lanes = lambda r, info: (0, 0, r)
    target = pl.BlockSpec((1, 5, depth, width), lambda r, info: (jnp.bitwise_xor(info[0], r), 0, 0, 0))
    return pl.pallas_call(
        partial(wide_grad_kernel, side, other is not None),
        grid_spec=pltpu.PrefetchScalarGridSpec(
            num_scalar_prefetch=1,
            grid=(4,),
            in_specs=[
                pl.BlockSpec((size, width), lambda r, info: (0, r)),
                pl.BlockSpec((2, size, width), lanes),
                pl.BlockSpec((2, size, width), lanes),
                whole(grad_attn),
                whole(grad_ffn),
                whole(ffn_in),
            ]
            + ([target] if other is not None else []),
            out_specs=target,
            scratch_shapes=[pltpu.VMEM((3, depth, size), jnp.bfloat16)],
        ),
        out_shape=jax.ShapeDtypeStruct((4, 5, depth, width), jnp.bfloat16),
        cost_estimate=pl.CostEstimate(
            flops=40 * size * depth * width, transcendentals=0, bytes_accessed=60 * depth * width
        ),
        name="wide_grads",
    )(info, mixed, hidden, grad_up, grad_attn, grad_ffn, ffn_in, *([other] if other is not None else []))


def qkv_grad_kernel(side, summed, info_ref, grad_ref, att_ref, *refs):
    other_ref, out_ref, turned = refs[0] if summed else None, refs[-2], refs[-1]
    depth = out_ref.shape[1]
    half = info_ref[1] if side == 0 else 1 - info_ref[1]

    @pl.when(pl.program_id(0) == 0)
    def _():
        turned[...] = att_ref[:, pl.ds(pl.multiple_of(half * depth, 128), depth)].T

    value = dot(turned[...], grad_ref[0])
    if summed:
        value = value + other_ref[0].astype(jnp.float32)
    out_ref[0] = value.astype(out_ref.dtype)


def qkv_grads(info, side, gradients, att_full, other=None, kind=jnp.bfloat16):
    _, frames, columns = gradients.shape
    depth = att_full.shape[1] // 2
    target = pl.BlockSpec((1, depth, columns), lambda c, *_: (c, 0, 0))
    return pl.pallas_call(
        partial(qkv_grad_kernel, side, other is not None),
        grid_spec=pltpu.PrefetchScalarGridSpec(
            num_scalar_prefetch=1,
            grid=(3,),
            in_specs=[pl.BlockSpec((1, frames, columns), lambda c, *_: (c, 0, 0)), whole(att_full)]
            + ([target] if other is not None else []),
            out_specs=target,
            scratch_shapes=[pltpu.VMEM((depth, frames), jnp.bfloat16)],
        ),
        out_shape=jax.ShapeDtypeStruct((3, depth, columns), kind),
        cost_estimate=pl.CostEstimate(
            flops=6 * frames * depth * columns, transcendentals=0, bytes_accessed=frames * depth * 6
        ),
        name="qkv_grads",
    )(info, gradients, att_full, *([other] if other is not None else []))


def inner_step(grads, first, second, weights, steps_done):
    first_new = beta_first * first + (1.0 - beta_first) * grads
    second_new = beta_second * second + (1.0 - beta_second) * grads * grads
    correct_one = 1.0 - beta_first**steps_done
    correct_two = 1.0 - beta_second**steps_done
    difference = inner_rate * (
        first_new / correct_one / (jnp.sqrt(second_new / correct_two) + adam_epsilon)
        + weight_decay * weights
    )
    return (first_new[None], second_new[None], difference)


def outer_step(average, outer, weights):
    outer_new = outer_beta * outer + average
    return (outer_new, weights - outer_rate * (average + outer_beta * outer_new))


def swapped(values, axis, bits):
    size = lax.axis_size(axis)
    return lax.ppermute(values, axis, [(i, i ^ bits) for i in range(size)])


def exchange(blocks, axis="tensor"):
    return [blocks[0]] + [swapped(blocks[r], axis, r) for r in range(1, 4)]


def after(values, *others):
    return lax.optimization_barrier((values, *others))[0]


def dp_rows(own):
    if lax.axis_size("dp") != 2:
        return lax.all_gather(own, "dp", axis=0, tiled=True)
    other = swapped(own, "dp", 1)
    first = lax.axis_index("dp") == 0
    return jnp.concatenate([jnp.where(first, own, other), jnp.where(first, other, own)], axis=0)


def dp_pair(own):
    if lax.axis_size("dp") == 2:
        return own, swapped(own, "dp", 1)
    return tuple(jnp.split(lax.all_gather(own, "dp", axis=1, tiled=True), 2, axis=1))


def quarter_of(half):
    quarter = half.shape[1] // 4
    return lax.dynamic_slice_in_dim(half, lax.axis_index("group") * quarter, quarter, 1)


def spread_wide(stack):
    one, two = swapped(stack, "group", 1), swapped(stack, "group", 2)
    return [stack, one, two, swapped(one[:2], "group", 2), swapped(two[2:], "group", 1)]


def group_parts(values):
    group = lax.axis_index("group")
    quarter = values.shape[1] // 4
    return exchange([lax.dynamic_slice_in_dim(values, (group ^ r) * quarter, quarter, 1) for r in range(4)], "group")


def add_parts(parts):
    return sum(part.astype(jnp.float32) for part in parts).astype(low)


def group_pieces(total):
    return exchange([total] * 4, "group")


def group_average(pieces):
    group = lax.axis_index("group")
    for bit in (1, 2):
        differs = (group & bit) == bit
        pieces = [jnp.where(differs, pieces[q ^ bit], pieces[q]) for q in range(4)]
    return jnp.concatenate(pieces, axis=1).astype(jnp.float32) / lax.axis_size("group")


def per_device(
    features,
    cotangent,
    frame_counts,
    buckets,
    step_count,
    col_weights,
    mod_weights,
    row_weights,
    col_first,
    col_second,
    mod_first,
    mod_second,
    row_first,
    row_second,
    col_outer,
    mod_outer,
    row_outer,
):
    group_count = lax.axis_size("group")
    packs_here = lax.axis_size("dp")
    own_rows, model_width = features.shape
    frames = own_rows * 4
    me = lax.axis_index("tensor")
    core = lax.axis_index("dp")
    group = lax.axis_index("group")
    count = buckets.shape[1]
    share = mod_weights.shape[0]
    width = col_weights.shape[2]

    def columns_first(values):
        return jnp.swapaxes(values, -3, -2)

    if packs_here == 2:
        col_quarter = quarter_of(columns_first(col_weights))[3:5]
        quarters = [jnp.concatenate([quarter_of(row_weights).astype(low), col_quarter.astype(low)], axis=0)]
    else:
        wide_low = jnp.concatenate([row_weights, columns_first(col_weights)[3:5]], axis=0).astype(low)
        quarters = [quarter_of(half) for half in dp_pair(wide_low)]
    stacks = [lax.all_gather(quarter, "tensor", axis=0) for quarter in quarters]
    features_full = lax.all_gather(after(features, *stacks), "tensor", axis=0, tiled=True)

    buckets_all = dp_rows(buckets[0])
    flow_time = ((group * NBUCK + buckets_all).astype(jnp.float32) + 0.5) / (NBUCK * group_count)
    condition_all = jax.nn.silu(time_embedding(flow_time, model_width)).astype(low)
    condition_here = lax.dynamic_slice_in_dim(condition_all, core * share, share, 1)
    mod_terms = jnp.einsum("ud,dcj->cuj", condition_here, mod_weights.astype(low), preferred_element_type=jnp.float32)
    if packs_here != 2:
        mod_part = lax.psum_scatter(mod_terms, "dp", scatter_dimension=1, tiled=True)
    else:
        mod_away = lax.dynamic_slice_in_dim(mod_terms, (1 - core) * count, count, 1)
        mod_part = lax.dynamic_slice_in_dim(mod_terms, core * count, count, 1) + swapped(mod_away, "dp", 1)
    mod_pieces = exchange([mod_part] * 4)

    ending = jnp.cumsum(frame_counts[0]).astype(jnp.int32)
    half_core = core if packs_here == 2 else jnp.zeros_like(core)
    info = jnp.concatenate([jnp.stack([me, half_core, group]).astype(jnp.int32), ending])
    _, position = utterance_rows(ending, jnp.arange(frames, dtype=jnp.int32))
    cosine, sine = rotary_tables(position)
    ranges = key_ranges(ending, frames, own_rows)
    qkv_here, qkv_away = dp_pair(columns_first(col_weights)[0:3].astype(low))
    wide_sets = [spread_wide(stack) for stack in stacks]
    if packs_here == 2:
        wide_sets.append([swapped(piece, "dp", 1) for piece in wide_sets[0]])

    att_full, qkv, modulation, means, inverses = project(info, features_full, mod_pieces, qkv_here, qkv_away, cosine, sine)
    *mixed_pieces, log_totals = attend(info, ranges, qkv, count)
    mixed_pieces = exchange(mixed_pieces)

    (output, grad_residual, g0, g1, g2, g3, late_sums, ffn_in, hidden, grad_up, grad_attn, grad_ffn, mixed) = middle(
        info, features, cotangent, mixed_pieces, modulation, *wide_sets, count
    )
    def to_owners(sums):
        return sum(exchange([lax.dynamic_slice_in_dim(sums, (me ^ r) * width, width, 2) for r in range(4)]))

    def mod_gradient(sums):
        columns = dp_rows(jnp.swapaxes(sums, 0, 1))
        if packs_here != 2:
            return jnp.einsum("ud,ucj->cdj", condition_here.astype(jnp.float32), columns, precision=highest)
        total = 0.0
        for u in range(columns.shape[0]):
            total = total + condition_here[u].astype(jnp.float32)[None, :, None] * columns[u][:, None, :]
        return total

    def some_diff(grads, first, second, weights, some):
        state = [columns_first(a)[some] for a in (first[0], second[0], weights)]
        return inner_step(grads, *state, steps_done)[2].astype(low)

    steps_done = step_count[0].astype(jnp.float32)
    grad_pieces = exchange([g0, g1, g2, g3])
    late_sums = late_sums[:, :count]
    wide_args = (mixed, hidden, grad_up, grad_attn, grad_ffn, ffn_in)
    if packs_here == 2:
        wide_other = swapped(wide_grads(info, 1, *wide_args), "dp", 1)
        late_sums = to_owners(after(late_sums, wide_other))
        wide_other, *grad_pieces = lax.optimization_barrier((wide_other, *grad_pieces))
        wide_blocks = wide_grads(info, 0, *wide_args, other=wide_other)
    else:
        both = jnp.concatenate([wide_grads(info, side, *wide_args) for side in range(2)], axis=2).astype(jnp.float32)
        wide_blocks = lax.psum_scatter(both, "dp", scatter_dimension=2, tiled=True).astype(low)
        late_sums = to_owners(late_sums)
    wide_grad = lax.psum_scatter(wide_blocks, "tensor", scatter_dimension=0, tiled=False)

    late_mod = mod_gradient(after(late_sums, wide_blocks))
    first_parts = group_parts(some_diff(late_mod, mod_first, mod_second, mod_weights, slice(2, 6)))
    attended = attend_back(
        info, ranges, qkv, grad_pieces, log_totals, cosine, sine, qkv_here, qkv_away, features_full, means, inverses, count
    )
    gradients, att_part, early_sums, *first_parts = lax.optimization_barrier((*attended, *first_parts))
    grad_att_in = lax.psum_scatter(after(att_part, wide_blocks), "tensor", scatter_dimension=0, tiled=True)
    first_pieces = group_pieces(add_parts(first_parts))
    early_mod = mod_gradient(to_owners(early_sums[:, :count]))
    if packs_here == 2:
        qkv_away_grad = swapped(qkv_grads(info, 1, gradients, att_full), "dp", 1)
        qkv_away_grad, *first_pieces = lax.optimization_barrier((qkv_away_grad, *first_pieces))
        qkv_share = qkv_grads(info, 0, gradients, att_full, other=qkv_away_grad, kind=jnp.float32)
    else:
        both = [qkv_grads(info, side, gradients, att_full, kind=jnp.float32) for side in range(2)]
        qkv_share = lax.psum_scatter(jnp.concatenate(both, axis=1), "dp", scatter_dimension=1, tiled=True)
    second_parts = group_parts(
        jnp.concatenate(
            [
                some_diff(qkv_share, col_first, col_second, col_weights, slice(0, 3)),
                some_diff(early_mod, mod_first, mod_second, mod_weights, slice(0, 2)),
            ],
            axis=0,
        )
    )

    row_first_new, row_second_new, row_diff = inner_step(
        wide_grad[0:3].astype(jnp.float32), row_first[0], row_second[0], row_weights, steps_done
    )
    col_first_new, col_second_new, col_diff = inner_step(
        columns_first(jnp.concatenate([qkv_share, wide_grad[3:5].astype(jnp.float32)], axis=0)), col_first[0], col_second[0], col_weights, steps_done
    )
    wide_diff = jnp.concatenate([row_diff.astype(low), columns_first(col_diff)[3:5].astype(low)], axis=0)
    wide_diff, *second_parts = lax.optimization_barrier((wide_diff, *second_parts))
    third_parts = group_parts(wide_diff)
    second_sum = add_parts(second_parts)
    second_pieces = group_pieces(second_sum)
    mod_first_new, mod_second_new, _ = inner_step(
        columns_first(jnp.concatenate(lax.optimization_barrier((early_mod, late_mod, second_pieces[1]))[:2], axis=0)),
        mod_first[0],
        mod_second[0],
        mod_weights,
        steps_done,
    )
    own_bounds, own_means, own_inverses, _ = lax.optimization_barrier((ending, means, inverses, second_pieces[1]))
    number_own, _ = utterance_rows(own_bounds, me * own_rows + jnp.arange(own_rows, dtype=jnp.int32))
    own_mean, inverse_scale = (
        lax.dynamic_slice_in_dim(a, me * own_rows, own_rows, 0)[:, 0] for a in (own_means, own_inverses)
    )
    both = lax.optimization_barrier(
        (*second_pieces, *third_parts, number_own, own_mean, inverse_scale, mod_first_new, mod_second_new)
    )
    second_pieces, third_parts = both[:4], both[4:8]
    number_own, own_mean, inverse_scale, mod_first_new, mod_second_new = both[8:]
    third_sum = add_parts(third_parts)
    third_pieces = group_pieces(third_sum)
    first_pieces = lax.optimization_barrier((*first_pieces, third_sum))[:4]
    first_average, second_average = group_average(first_pieces), group_average(second_pieces)
    mod_average = columns_first(jnp.concatenate([second_average[3:5], first_average], axis=0))
    mod_outer_new, mod_new = outer_step(mod_average, mod_outer, mod_weights)
    grad_att_in = after(grad_att_in, third_sum, mod_new).astype(jnp.float32)
    normed = (features.astype(jnp.float32) - own_mean[:, None]) * inverse_scale[:, None]
    grad_features = grad_residual + normalize_back(
        grad_att_in * (1.0 + by_utterance(number_own[:, None], modulation[1, :count])), normed, inverse_scale[:, None]
    )
    third_pieces = lax.optimization_barrier((*third_pieces, mod_average, mod_outer_new, mod_new, grad_features))[:4]
    third_average = group_average(third_pieces)
    row_average = third_average[0:3]
    col_average = columns_first(jnp.concatenate([second_average[0:3], third_average[3:5]], axis=0))
    col_outer_new, col_new = outer_step(col_average, col_outer, col_weights)
    row_outer_new, row_new = outer_step(row_average, row_outer, row_weights)

    return (
        output,
        grad_features,
        col_first_new,
        col_second_new,
        col_average,
        col_outer_new,
        col_new,
        mod_first_new,
        mod_second_new,
        mod_average,
        mod_outer_new,
        mod_new,
        row_first_new,
        row_second_new,
        row_average,
        row_outer_new,
        row_new,
    )


def solution(mesh):
    placed = (
        P(("group", "dp", "tensor"), None),
        P(("group", "dp", "tensor"), None),
        P(("group", "dp"), None),
        P(("group", "dp"), None),
        P(),
        P("dp", None, "tensor"),
        P("dp", None, "tensor"),
        P(None, "dp", "tensor"),
        P("group", "dp", None, "tensor"),
        P("group", "dp", None, "tensor"),
        P("group", "dp", None, "tensor"),
        P("group", "dp", None, "tensor"),
        P("group", None, "dp", "tensor"),
        P("group", None, "dp", "tensor"),
        P("dp", None, "tensor"),
        P("dp", None, "tensor"),
        P(None, "dp", "tensor"),
    )
    return jax.shard_map(
        per_device,
        mesh=mesh,
        in_specs=placed,
        out_specs=(
            P(("group", "dp", "tensor"), None),
            P(("group", "dp", "tensor"), None),
            P("group", "dp", None, "tensor"),
            P("group", "dp", None, "tensor"),
            P("dp", None, "tensor"),
            P("dp", None, "tensor"),
            P("dp", None, "tensor"),
            P("group", "dp", None, "tensor"),
            P("group", "dp", None, "tensor"),
            P("dp", None, "tensor"),
            P("dp", None, "tensor"),
            P("dp", None, "tensor"),
            P("group", None, "dp", "tensor"),
            P("group", None, "dp", "tensor"),
            P(None, "dp", "tensor"),
            P(None, "dp", "tensor"),
            P(None, "dp", "tensor"),
        ),
        check_vma=False,
    )
```
